128 devices in a mesh: face: 8 (over x, z_hi), tile: 16 (over z_lo, y, core).
Axes of the slice: x: 4, y: 4, z: 4 (z_hi: 2, z_lo: 2; z = z_hi * 2 + z_lo), core: 2. Of those that a mesh axis runs over, the one named last changes fastest.
Arguments:
- state_field: bfloat16 [4, 512, 1024, 256], P(None, 'face', 'tile'), may hold values from -6 to 6
- cotangent: bfloat16 [4, 512, 1024, 256], P(None, 'face', 'tile'), may hold values from -6 to 6
- depth_weight: float32 [9, 256], replicated, may hold values from -2 to 2
- depth_bias: float32 [256], replicated, may hold values from -3 to 3
- point_weight: bfloat16 [256, 256], replicated, may hold values from -0.375 to 0.375
- tile_links: int32 [128, 4], P(('face', 'tile')), may hold values from 0 to 127, as said below
- link_sides: int32 [128, 4], P(('face', 'tile')), may hold values from 0 to 3
- link_flips: int32 [128, 4], P(('face', 'tile')), may hold values from 0 to 1
- corner_masks: int32 [128, 4], P(('face', 'tile')), may hold values 0 or 1
Outputs:
- field_grad: bfloat16 [4, 512, 1024, 256], P(None, 'face', 'tile')
- depth_grad: float32 [9, 256], replicated
- bias_grad: float32 [256], replicated
- point_grad: float32 [256, 256], replicated
The draws below stay inside these ranges and needn't reach their ends.
Inputs may be any that keep to these rules, and one draw needn't show every extreme that they name: Tile ids number the grid row by row, the row being the index along face. The four neighbours of a tile are the four tiles one step away along face or along tile with wrap-around, each exactly once. Links are mutual: if tile_links[a, s] = b and link_sides[a, s] = o then tile_links[b, o] = a, link_sides[b, o] = s and link_flips[b, o] = link_flips[a, s].
All inputs are finite; a program needn't handle non-finite values. No bound on the sum of `corner_masks` on one device may be relied on, other than what follows from the above.
Results may differ from the reference program's by a relative error of at most 0.0049.
Values may be sent and summed in bfloat16 or wider, within the bound.
No kernel may reach another device: no remote copies, remote signals or barrier semaphores. Data moves between devices by JAX's collectives and lax.ppermute only.
A program may use at most 192 MiB of HBM per device.

```python
import jax
import jax.numpy as jnp
from jax import lax

CH = 256
BATCH = 4
SIDE = 64
TILES = 128
PIXELS = 2097152
N_FACE = 8
N_TILE = 16


def tile_graph(key):
    rotation = jax.random.randint(jax.random.fold_in(key, 11), (N_FACE, N_TILE), 0, 4)
    flip_south = jax.random.randint(jax.random.fold_in(key, 12), (N_FACE, N_TILE), 0, 2)
    flip_east = jax.random.randint(jax.random.fold_in(key, 13), (N_FACE, N_TILE), 0, 2)
    face_rows = jnp.arange(N_FACE, dtype=jnp.int32)[:, None, None]
    tile_cols = jnp.arange(N_TILE, dtype=jnp.int32)[None, :, None]
    side_ids = jnp.arange(4, dtype=jnp.int32)[None, None, :]
    heading = (side_ids + rotation[:, :, None]) % 4
    step_face = jnp.where(heading == 0, -1, jnp.where(heading == 2, 1, 0))
    step_tile = jnp.where(heading == 1, 1, jnp.where(heading == 3, -1, 0))
    other_face = (face_rows + step_face) % N_FACE
    other_tile = (tile_cols + step_tile) % N_TILE
    linked = other_face * N_TILE + other_tile
    facing = (heading + 2 - rotation[other_face, other_tile]) % 4
    own_south = jnp.broadcast_to(flip_south[:, :, None], heading.shape)
    own_east = jnp.broadcast_to(flip_east[:, :, None], heading.shape)
    far_south = flip_south[other_face, other_tile]
    far_east = flip_east[other_face, other_tile]
    flipping = jnp.where(heading == 2, own_south, jnp.where(heading == 1, own_east, jnp.where(heading == 0, far_south, far_east)))
    return (linked.reshape(TILES, 4).astype(jnp.int32), facing.reshape(TILES, 4).astype(jnp.int32), flipping.reshape(TILES, 4).astype(jnp.int32))


def draw_tile_links(key, part):
    return tile_graph(key)[0]


def draw_link_sides(key, part):
    return tile_graph(key)[1]


def draw_link_flips(key, part):
    return tile_graph(key)[2]


def with_ends(drawn, own_key, least, high):
    shape = drawn.shape
    place = [jax.random.randint(jax.random.fold_in(own_key, axis), (), 0, shape[axis]) for axis in range(len(shape))]
    drawn = drawn.at[tuple(place)].set(least)
    longest = shape.index(max(shape))
    place[longest] = (place[longest] + 1) % shape[longest]
    return drawn.at[tuple(place)].set(high)


def steps_of(rng, extent, cuts, smallest, top_value):
    loudness, own = 1.0, jax.random.fold_in(rng, 6)
    for axis_at, shards_of in cuts:
        steps = jnp.exp(jax.random.uniform(jax.random.fold_in(own, axis_at), (shards_of,), jnp.float32, smallest / len(cuts), top_value / len(cuts)))
        loudness = loudness * jnp.repeat(steps, extent[axis_at] // shards_of).reshape([-1 if axis == axis_at else 1 for axis in range(len(extent))])
    return loudness


def bell_draw(stream_key, dims, scale, bound, shards=(), held_as=jnp.bfloat16):
    gain = steps_of(stream_key, dims, shards, -0.22, 0.18) if shards else 1.0
    drawn = jax.random.normal(stream_key, dims, jnp.float32) * scale * gain
    return jnp.minimum(jnp.maximum(drawn, -bound), bound).astype(held_as)


def setup_inputs(seed: int = 0) -> dict:
    splits = jax.random.split(jax.random.key(seed), 10)
    state_field = bell_draw(splits[0], (BATCH, N_FACE * SIDE, N_TILE * SIDE, CH), 1.0, 6.0, ((1, 8), (2, 16)))
    cotangent = bell_draw(splits[1], (BATCH, N_FACE * SIDE, N_TILE * SIDE, CH), 1.0, 6.0, ((1, 8), (2, 16)))
    depth_weight = bell_draw(splits[2], (9, CH), 9 ** -0.5, 2.0, (), jnp.float32)
    depth_bias = bell_draw(splits[3], (CH,), 0.5, 3.0, (), jnp.float32)
    point_weight = bell_draw(splits[4], (CH, CH), CH ** -0.5, 0.375)
    tile_links = draw_tile_links(jax.random.fold_in(splits[9], 71), 0)
    link_sides = draw_link_sides(jax.random.fold_in(splits[9], 71), 0)
    link_flips = draw_link_flips(jax.random.fold_in(splits[9], 71), 0)
    corner_masks = with_ends((jax.random.randint(splits[8], (TILES, 4), 0, 4) < 3).astype(jnp.int32), jax.random.fold_in(splits[8], 1), 0, 1)
    return {"state_field": state_field, "cotangent": cotangent, "depth_weight": depth_weight, "depth_bias": depth_bias, "point_weight": point_weight, "tile_links": tile_links, "link_sides": link_sides, "link_flips": link_flips, "corner_masks": corner_masks}


root_two_pi = 0.7978845608028654
cubic_coef = 0.044715


def gelu_pair(hidden):
    inside = root_two_pi * (hidden + cubic_coef * hidden * hidden * hidden)
    tanh_val = jnp.tanh(inside)
    output = 0.5 * hidden * (1.0 + tanh_val)
    slope = 0.5 * (1.0 + tanh_val) + 0.5 * hidden * (1.0 - tanh_val * tanh_val) * root_two_pi * (1.0 + 3.0 * cubic_coef * hidden * hidden)
    return output, slope


def edge_rows(block):
    return jnp.stack([block[:, 0], block[:, :, -1], block[:, -1], block[:, :, 0]], axis=0)


def padded_tile(block, rim_rows, corner_row):
    cmask = corner_row.astype(jnp.float32)
    rim32 = rim_rows.astype(jnp.float32)
    north_west = (cmask[0] * 0.5 * (rim32[0][:, 0] + rim32[3][:, 0])).astype(jnp.bfloat16)
    north_east = (cmask[1] * 0.5 * (rim32[0][:, -1] + rim32[1][:, 0])).astype(jnp.bfloat16)
    south_east = (cmask[2] * 0.5 * (rim32[1][:, -1] + rim32[2][:, -1])).astype(jnp.bfloat16)
    south_west = (cmask[3] * 0.5 * (rim32[2][:, 0] + rim32[3][:, -1])).astype(jnp.bfloat16)
    top_row = jnp.concatenate([north_west[:, None], rim_rows[0], north_east[:, None]], axis=1)
    low_row = jnp.concatenate([south_west[:, None], rim_rows[2], south_east[:, None]], axis=1)
    middle = jnp.concatenate([rim_rows[3][:, :, None], block, rim_rows[1][:, :, None]], axis=2)
    return jnp.concatenate([top_row[:, None], middle, low_row[:, None]], axis=1)


def tile_pass(block, cotan, rim_rows, corner_row, depth_weight, depth_bias, point_weight):
    tile_side = block.shape[1]
    channels = block.shape[3]
    padded = padded_tile(block, rim_rows, corner_row)
    tap_table = depth_weight.reshape(3, 3, channels)
    hidden = jnp.zeros(block.shape, jnp.float32) + depth_bias
    for row_off in range(3):
        for col_off in range(3):
            hidden = hidden + tap_table[row_off, col_off] * padded[:, row_off:row_off + tile_side, col_off:col_off + tile_side].astype(jnp.float32)
    output, slope = gelu_pair(hidden)
    act = output.astype(jnp.bfloat16)
    row_count = block.shape[0] * tile_side * tile_side
    cot_rows = cotan.reshape(row_count, channels)
    grad_act = jnp.dot(cot_rows, point_weight.T, preferred_element_type=jnp.float32)
    grad_hidden = (grad_act.reshape(hidden.shape) * slope).astype(jnp.bfloat16)
    point_part = jnp.dot(act.reshape(row_count, channels).T, cot_rows, preferred_element_type=jnp.float32)
    grad32 = grad_hidden.astype(jnp.float32)
    depth_list = []
    grad_pad = jnp.zeros(padded.shape, jnp.float32)
    for row_off in range(3):
        for col_off in range(3):
            window = padded[:, row_off:row_off + tile_side, col_off:col_off + tile_side].astype(jnp.float32)
            depth_list.append(jnp.sum(grad32 * window, axis=(0, 1, 2)))
            grad_pad = grad_pad.at[:, row_off:row_off + tile_side, col_off:col_off + tile_side].add(tap_table[row_off, col_off] * grad32)
    depth_part = jnp.stack(depth_list, axis=0)
    bias_part = jnp.sum(grad32, axis=(0, 1, 2))
    inner_grad = grad_pad[:, 1:-1, 1:-1]
    cmask = corner_row.astype(jnp.float32)
    north_west = 0.5 * cmask[0] * grad_pad[:, 0, 0]
    north_east = 0.5 * cmask[1] * grad_pad[:, 0, -1]
    south_east = 0.5 * cmask[2] * grad_pad[:, -1, -1]
    south_west = 0.5 * cmask[3] * grad_pad[:, -1, 0]
    north = grad_pad[:, 0, 1:-1].at[:, 0].add(north_west).at[:, -1].add(north_east)
    east = grad_pad[:, 1:-1, -1].at[:, 0].add(north_east).at[:, -1].add(south_east)
    south = grad_pad[:, -1, 1:-1].at[:, 0].add(south_west).at[:, -1].add(south_east)
    west = grad_pad[:, 1:-1, 0].at[:, 0].add(north_west).at[:, -1].add(south_west)
    rim_grad = jnp.stack([north, east, south, west], axis=0)
    return rim_grad, point_part, depth_part, bias_part, inner_grad


def reference(state_field, cotangent, depth_weight, depth_bias, point_weight, tile_links, link_sides, link_flips, corner_masks):
    def to_tiles(whole):
        return whole.reshape(BATCH, N_FACE, SIDE, N_TILE, SIDE, CH).transpose(1, 3, 0, 2, 4, 5).reshape(TILES, BATCH, SIDE, SIDE, CH)

    tiles = to_tiles(state_field)
    cot_tiles = to_tiles(cotangent)
    edges = jax.vmap(edge_rows)(tiles)
    sources = edges[tile_links, link_sides]
    flipped = (link_flips == 1)[:, :, None, None, None]
    rim_all = jnp.where(flipped, sources[:, :, :, ::-1], sources)

    def first_pass(items):
        outcome = tile_pass(items[0], items[1], items[2], items[3], depth_weight, depth_bias, point_weight)
        return outcome[0], outcome[1], outcome[2], outcome[3]

    rim_grads, point_parts, depth_parts, bias_parts = lax.map(first_pass, (tiles, cot_tiles, rim_all, corner_masks))
    incoming = rim_grads[tile_links, link_sides]
    incoming = jnp.where(flipped, incoming[:, :, :, ::-1], incoming)

    def second_pass(items):
        inner_grad = tile_pass(items[0], items[1], items[2], items[3], depth_weight, depth_bias, point_weight)[4]
        extra = items[4]
        inner_grad = inner_grad.at[:, 0].add(extra[0]).at[:, :, -1].add(extra[1]).at[:, -1].add(extra[2]).at[:, :, 0].add(extra[3])
        return inner_grad.astype(jnp.bfloat16)

    grad_tiles = lax.map(second_pass, (tiles, cot_tiles, rim_all, corner_masks, incoming))
    field_grad = grad_tiles.reshape(N_FACE, N_TILE, BATCH, SIDE, SIDE, CH).transpose(2, 0, 3, 1, 4, 5).reshape(BATCH, N_FACE * SIDE, N_TILE * SIDE, CH)
    norm_scale = float(PIXELS) ** -0.5
    depth_grad = jnp.sum(depth_parts, axis=0) * norm_scale
    bias_grad = jnp.sum(bias_parts, axis=0) * norm_scale
    point_grad = jnp.sum(point_parts, axis=0) * norm_scale
    return field_grad, depth_grad, bias_grad, point_grad
```

```python
import functools

import jax
import jax.numpy as jnp
from jax import lax
from jax.experimental import pallas as pl
from jax.experimental.pallas import tpu as pltpu
from jax.sharding import PartitionSpec as P

ROOT = 0.7978845608028654
CUBIC = 0.044715
F32 = jnp.float32
BF16 = jnp.bfloat16
LANES = 128
SUB = 8
PAD = 8


def gelu_pair(h):
    h2 = h * h
    s = 0.5 * jnp.tanh(h * ((CUBIC * ROOT) * h2 + ROOT)) + 0.5
    act = h * s
    slope = s + act * (1.0 - s) * ((6.0 * CUBIC * ROOT) * h2 + 2.0 * ROOT)
    return act, slope


def inner_body(rows_at_once, x_ref, cot_ref, w_ref, tap_ref, bias_ref, gh_ref, pg_ref, dg_ref, xf, ga, act, acc):
    step = pl.program_id(0)
    side = x_ref.shape[1]
    cols = x_ref.shape[2]

    @pl.when(step == 0)
    def _():
        edge = jnp.zeros((side, PAD, LANES), F32)
        for hf in range(2):
            xf[hf, :, 0:PAD, :] = edge
            xf[hf, :, PAD + cols : 2 * PAD + cols, :] = edge
        act[0] = jnp.zeros(act.shape[1:], BF16)
        act[side - 1] = jnp.zeros(act.shape[1:], BF16)
        acc[...] = jnp.zeros_like(acc)
        pg_ref[...] = jnp.zeros_like(pg_ref)

    gh_ref[0, 0] = jnp.zeros(gh_ref.shape[2:], BF16)
    gh_ref[0, side - 1] = jnp.zeros(gh_ref.shape[2:], BF16)

    def widen(i, _):
        v = x_ref[0, i].astype(F32)
        xf[0, i, PAD : PAD + cols, :] = v[:, :LANES]
        xf[1, i, PAD : PAD + cols, :] = v[:, LANES:]
        return 0

    lax.fori_loop(0, side, widen, 0, unroll=4)
    w = w_ref[...]

    def back_rows(k, _):
        c = cot_ref[0, pl.ds(k * 8, 8)].reshape(8 * cols, 2 * LANES)
        g = lax.dot_general(c, w, (((1,), (1,)), ((), ())), preferred_element_type=F32)
        g = g.reshape(8, cols, 2 * LANES)
        ga[0, pl.ds(k * 8, 8)] = g[:, :, :LANES]
        ga[1, pl.ds(k * 8, 8)] = g[:, :, LANES:]
        return 0

    lax.fori_loop(0, side // 8, back_rows, 0)
    row = lax.broadcasted_iota(jnp.int32, (SUB, LANES), 0)
    inner = side - 2
    for hf in range(2):
        lanes = slice(hf * LANES, hf * LANES + LANES)
        for jb in range(cols // 16):

            def body(it, carry, count, base):
                i = base + it * count
                accs = list(carry)
                win = {}
                for q in range(count):
                    pair = []
                    for part in range(2):
                        j = PAD + jb * 16 + part * SUB
                        for r in range(3):
                            for c in range(3):
                                if (q + r, c, part) not in win:
                                    win[q + r, c, part] = xf[hf, i - 1 + q + r, j - 1 + c : j - 1 + c + SUB, :]
                        h = bias_ref[hf]
                        for r in range(3):
                            for c in range(3):
                                h = h + tap_ref[hf, 3 * r + c] * win[q + r, c, part]
                        a, slope = gelu_pair(h)
                        g = ga[hf, i + q, jb * 16 + part * SUB : jb * 16 + part * SUB + SUB, :] * slope
                        if jb == 0 and part == 0:
                            g = jnp.where(row > 0, g, 0.0)
                            a = jnp.where(row > 0, a, 0.0)
                        if jb == cols // 16 - 1 and part == 1:
                            g = jnp.where(row < SUB - 1, g, 0.0)
                            a = jnp.where(row < SUB - 1, a, 0.0)
                        pair.append((a, g))
                        for r in range(3):
                            for c in range(3):
                                accs[3 * r + c] = accs[3 * r + c] + g * win[q + r, c, part]
                        accs[9] = accs[9] + g
                    act[i + q, jb * 16 : jb * 16 + 16, lanes] = jnp.concatenate(
                        [pair[0][0], pair[1][0]], axis=0
                    ).astype(BF16)
                    gh_ref[0, i + q, jb * 16 : jb * 16 + 16, lanes] = jnp.concatenate(
                        [pair[0][1], pair[1][1]], axis=0
                    ).astype(BF16)
                return tuple(accs)

            out = tuple(acc[hf, k] for k in range(10))
            trips = inner // rows_at_once
            out = lax.fori_loop(0, trips, functools.partial(body, count=rows_at_once, base=1), out)
            if inner % rows_at_once:
                out = body(0, out, inner % rows_at_once, 1 + trips * rows_at_once)
            for k in range(10):
                acc[hf, k] = out[k]

    def outer_rows(k, _):
        a = act[pl.ds(k * 16, 16)].reshape(16 * cols, 2 * LANES)
        c = cot_ref[0, pl.ds(k * 16, 16)].reshape(16 * cols, 2 * LANES)
        pg_ref[...] += lax.dot_general(a, c, (((0,), (0,)), ((), ())), preferred_element_type=F32)
        return 0

    lax.fori_loop(0, side // 16, outer_rows, 0)

    @pl.when(step == pl.num_programs(0) - 1)
    def _():
        dg_ref[...] = acc[...]


def inner_call(state, cotangent, weight, taps, bias):
    batch, side, cols, channels = state.shape
    tile = pl.BlockSpec((1, side, cols, channels), lambda b: (b, 0, 0, 0))
    return pl.pallas_call(
        functools.partial(inner_body, 4),
        grid=(batch,),
        in_specs=[
            tile,
            tile,
            pl.BlockSpec((channels, channels), lambda b: (0, 0)),
            pl.BlockSpec((2, 9, SUB, LANES), lambda b: (0, 0, 0, 0)),
            pl.BlockSpec((2, SUB, LANES), lambda b: (0, 0, 0)),
        ],
        out_specs=[
            tile,
            pl.BlockSpec((channels, channels), lambda b: (0, 0)),
            pl.BlockSpec((2, 10, SUB, LANES), lambda b: (0, 0, 0, 0)),
        ],
        out_shape=[
            jax.ShapeDtypeStruct(state.shape, BF16),
            jax.ShapeDtypeStruct((channels, channels), F32),
            jax.ShapeDtypeStruct((2, 10, SUB, LANES), F32),
        ],
        scratch_shapes=[
            pltpu.VMEM((2, side, cols + 2 * PAD, LANES), F32),
            pltpu.VMEM((2, side, cols, LANES), F32),
            pltpu.VMEM((side, cols, channels), BF16),
            pltpu.VMEM((2, 10, SUB, LANES), F32),
        ],
        compiler_params=pltpu.CompilerParams(vmem_limit_bytes=56 << 20),
        cost_estimate=pl.CostEstimate(
            flops=40_000_000_000, bytes_accessed=26 << 20, transcendentals=state.size
        ),
        name="inner",
    )(state, cotangent, weight, taps, bias)


LOW = (0, 1, 3, 0)
HIGH = (1, 2, 2, 3)


def ring_body(
    mask_ref, top_ref, low_ref, left_ref, right_ref, ctop_ref, clow_ref, cleft_ref, cright_ref,
    rim_ref, w_ref, tap_ref, bias_ref, gr_ref, rg_ref, pg_ref, dg_ref, strip, ext, acts, acc,
):
    step = pl.program_id(0)
    side = rim_ref.shape[2]

    @pl.when(step == 0)
    def _():
        acc[...] = jnp.zeros_like(acc)
        pg_ref[...] = jnp.zeros_like(pg_ref)
        ext[...] = jnp.zeros_like(ext)

    rims = [rim_ref[s, 0].astype(F32) for s in range(4)]
    top = top_ref[0].astype(F32)
    low = low_ref[0].astype(F32)
    left = left_ref[0].astype(F32)
    right = right_ref[0].astype(F32)
    last = left.shape[1] - 1
    end = side - 1

    def corner(k, first, second):
        return (mask_ref[k] * 0.5 * (first + second)).astype(BF16).astype(F32)

    def at(s, i):
        return rims[s][i : i + 1]

    nw = corner(0, at(0, 0), at(3, 0))
    ne = corner(1, at(0, end), at(1, 0))
    se = corner(2, at(1, end), at(2, end))
    sw = corner(3, at(2, 0), at(3, end))
    lines = (
        ((rims[0], nw, ne), (top[0], at(3, 0), at(1, 0)), (top[1], at(3, 1), at(1, 1))),
        (
            (right[:, last - 1], at(0, end - 1), at(2, end - 1)),
            (right[:, last], at(0, end), at(2, end)),
            (rims[1], ne, se),
        ),
        (
            (low[0], at(3, end - 1), at(1, end - 1)),
            (low[1], at(3, end), at(1, end)),
            (rims[2], sw, se),
        ),
        ((rims[3], nw, sw), (left[:, 0], at(0, 0), at(2, 0)), (left[:, 1], at(0, 1), at(2, 1))),
    )
    for s in range(4):
        for a in range(3):
            line, before, after = lines[s][a]
            for hf in range(2):
                lanes = slice(hf * LANES, hf * LANES + LANES)
                strip[s, hf, a, PAD : PAD + side, :] = line[:, lanes]
                strip[s, hf, a, PAD - 1 : PAD, :] = before[:, lanes]
                strip[s, hf, a, PAD + side : PAD + side + 1, :] = after[:, lanes]
    cots = jnp.concatenate(
        [
            ctop_ref[0, 0].astype(F32),
            cright_ref[0].astype(F32)[:, last],
            clow_ref[0, 0].astype(F32),
            cleft_ref[0].astype(F32)[:, 0],
        ],
        axis=0,
    ).astype(BF16)
    ga = lax.dot_general(cots, w_ref[...], (((1,), (1,)), ((), ())), preferred_element_type=F32)
    row = lax.broadcasted_iota(jnp.int32, (side, LANES), 0)
    middle = jnp.logical_and(row > 0, row < end)
    for s in range(4):
        upright = s % 2 == 0
        rim_line = 0 if s in (0, 3) else 2
        for hf in range(2):
            lanes = slice(hf * LANES, hf * LANES + LANES)

            def tap(a, b):
                k = 3 * a + b if upright else 3 * b + a
                return k, tap_ref[hf, k, 0:1, :]

            h = jnp.zeros((side, LANES), F32) + bias_ref[hf, 0:1, :]
            for a in range(3):
                for b in range(3):
                    h = h + tap(a, b)[1] * strip[s, hf, a, PAD - 1 + b : PAD - 1 + b + side, :]
            act, slope = gelu_pair(h)
            g = (ga[s * side : s * side + side, lanes] * slope).astype(BF16)
            gr_ref[s, 0, :, lanes] = g
            g = g.astype(F32)
            counted = g
            if not upright:
                counted = jnp.where(middle, g, 0.0)
                act = jnp.where(middle, act, 0.0)
            acts[s * side : s * side + side, lanes] = act.astype(BF16)
            for a in range(3):
                for b in range(3):
                    k = tap(a, b)[0]
                    term = counted * strip[s, hf, a, PAD - 1 + b : PAD - 1 + b + side, :]
                    acc[hf, k] += jnp.sum(term.reshape(side // SUB, SUB, LANES), axis=0)
            acc[hf, 9] += jnp.sum(counted.reshape(side // SUB, SUB, LANES), axis=0)
            ext[PAD : PAD + side, :] = g
            first, mid, final = (tap(rim_line, b)[1] for b in range(3))
            back = (
                first * ext[PAD + 1 : PAD + 1 + side, :]
                + mid * g
                + final * ext[PAD - 1 : PAD - 1 + side, :]
            )
            back = back + jnp.where(row == 0, (0.5 * mask_ref[LOW[s]]) * first * g, 0.0)
            back = back + jnp.where(row == end, (0.5 * mask_ref[HIGH[s]]) * final * g, 0.0)
            rg_ref[s, 0, :, lanes] = back.astype(BF16)
    pg_ref[...] += lax.dot_general(acts[...], cots, (((0,), (0,)), ((), ())), preferred_element_type=F32)

    @pl.when(step == pl.num_programs(0) - 1)
    def _():
        dg_ref[...] = acc[...]


def ring_call(mask, state, cotangent, rims, weight, taps, bias):
    batch, side, cols, channels = state.shape
    wide = 16
    two = lambda at: pl.BlockSpec((1, 2, cols, channels), lambda b: (b, at, 0, 0))
    one = lambda at: pl.BlockSpec((1, 1, cols, channels), lambda b: (b, at, 0, 0))
    column = lambda at: pl.BlockSpec((1, side, wide, channels), lambda b: (b, 0, at, 0))
    strips = pl.BlockSpec((4, 1, side, channels), lambda b: (0, b, 0, 0))
    far = cols // wide - 1
    return pl.pallas_call(
        ring_body,
        grid=(batch,),
        in_specs=[
            pl.BlockSpec(memory_space=pltpu.SMEM),
            two(0),
            two(side // 2 - 1),
            column(0),
            column(far),
            one(0),
            one(side - 1),
            column(0),
            column(far),
            strips,
            pl.BlockSpec((channels, channels), lambda b: (0, 0)),
            pl.BlockSpec((2, 9, SUB, LANES), lambda b: (0, 0, 0, 0)),
            pl.BlockSpec((2, SUB, LANES), lambda b: (0, 0, 0)),
        ],
        out_specs=[
            strips,
            strips,
            pl.BlockSpec((channels, channels), lambda b: (0, 0)),
            pl.BlockSpec((2, 10, SUB, LANES), lambda b: (0, 0, 0, 0)),
        ],
        out_shape=[
            jax.ShapeDtypeStruct((4, batch, side, channels), BF16),
            jax.ShapeDtypeStruct((4, batch, side, channels), BF16),
            jax.ShapeDtypeStruct((channels, channels), F32),
            jax.ShapeDtypeStruct((2, 10, SUB, LANES), F32),
        ],
        scratch_shapes=[
            pltpu.VMEM((4, 2, 3, cols + 2 * PAD, LANES), F32),
            pltpu.VMEM((cols + 2 * PAD, LANES), F32),
            pltpu.VMEM((4 * side, channels), BF16),
            pltpu.VMEM((2, 10, SUB, LANES), F32),
        ],
        compiler_params=pltpu.CompilerParams(vmem_limit_bytes=40 << 20),
        cost_estimate=pl.CostEstimate(
            flops=3_000_000_000, bytes_accessed=12 << 20, transcendentals=state.size // 16
        ),
        name="ring",
    )(mask, state, state, state, state, cotangent, cotangent, cotangent, cotangent, rims, weight, taps, bias)


def spread_body(rows_at_once, gh_ref, gr_ref, in_ref, tap_ref, out_ref, gf, near, far):
    side = gh_ref.shape[1]
    cols = gh_ref.shape[2]
    for hf in range(2):
        gf[hf, 0] = jnp.zeros(gf.shape[2:], F32)
        gf[hf, side + 1] = jnp.zeros(gf.shape[2:], F32)
        gf[hf, :, 0:PAD, :] = jnp.zeros((side + 2, PAD, LANES), F32)
        gf[hf, :, PAD + cols : 2 * PAD + cols, :] = jnp.zeros((side + 2, PAD, LANES), F32)
    near[...] = jnp.zeros_like(near)
    far[...] = jnp.zeros_like(far)

    def widen(i, _):
        v = gh_ref[0, i].astype(F32)
        gf[0, i + 1, PAD : PAD + cols, :] = v[:, :LANES]
        gf[1, i + 1, PAD : PAD + cols, :] = v[:, LANES:]
        return 0

    lax.fori_loop(1, side - 1, widen, 0)
    ring = [gr_ref[s, 0].astype(F32) for s in range(4)]
    back = [in_ref[s, 0].astype(F32) for s in (1, 3)]
    for hf in range(2):
        lanes = slice(hf * LANES, hf * LANES + LANES)
        gf[hf, 1 : side + 1, PAD : PAD + 1, :] = ring[3][:, lanes].reshape(side, 1, LANES)
        gf[hf, 1 : side + 1, PAD + cols - 1 : PAD + cols, :] = ring[1][:, lanes].reshape(side, 1, LANES)
        gf[hf, 1, PAD : PAD + cols, :] = ring[0][:, lanes]
        gf[hf, side, PAD : PAD + cols, :] = ring[2][:, lanes]
        near[hf, :, 0:1, :] = back[1][:, lanes].reshape(side, 1, LANES)
        far[hf, :, SUB - 1 : SUB, :] = back[0][:, lanes].reshape(side, 1, LANES)
    for hf in range(2):
        lanes = slice(hf * LANES, hf * LANES + LANES)
        for jb in range(cols // 16):

            def body(it, carry):
                i = it * rows_at_once
                win = {}
                for q in range(rows_at_once):
                    pair = []
                    for part in range(2):
                        j = PAD + jb * 16 + part * SUB
                        total = None
                        for r in range(3):
                            for c in range(3):
                                at = (q + 2 - r, 2 - c, part)
                                if at not in win:
                                    win[at] = gf[hf, i + at[0], j - 1 + at[1] : j - 1 + at[1] + SUB, :]
                                term = tap_ref[hf, 3 * r + c] * win[at]
                                total = term if total is None else total + term
                        if jb == 0 and part == 0:
                            total = total + near[hf, i + q]
                        if jb == cols // 16 - 1 and part == 1:
                            total = total + far[hf, i + q]
                        pair.append(total)
                    out_ref[0, i + q, jb * 16 : jb * 16 + 16, lanes] = jnp.concatenate(pair, axis=0).astype(BF16)
                return carry

            lax.fori_loop(0, side // rows_at_once, body, 0)
    for at, s in ((0, 0), (side - 1, 2)):
        out_ref[0, at] = (out_ref[0, at].astype(F32) + in_ref[s, 0].astype(F32)).astype(BF16)


def spread_call(grad, ring, incoming, taps):
    batch, side, cols, channels = grad.shape
    tile = pl.BlockSpec((1, side, cols, channels), lambda b: (b, 0, 0, 0))
    strips = pl.BlockSpec((4, 1, side, channels), lambda b: (0, b, 0, 0))
    return pl.pallas_call(
        functools.partial(spread_body, 4),
        grid=(batch,),
        in_specs=[tile, strips, strips, pl.BlockSpec((2, 9, SUB, LANES), lambda b: (0, 0, 0, 0))],
        out_specs=tile,
        out_shape=jax.ShapeDtypeStruct(grad.shape, BF16),
        scratch_shapes=[
            pltpu.VMEM((2, side + 2, cols + 2 * PAD, LANES), F32),
            pltpu.VMEM((2, side, SUB, LANES), F32),
            pltpu.VMEM((2, side, SUB, LANES), F32),
        ],
        compiler_params=pltpu.CompilerParams(vmem_limit_bytes=40 << 20),
        cost_estimate=pl.CostEstimate(flops=15_000_000_000, bytes_accessed=17 << 20, transcendentals=0),
        name="spread",
    )(grad, ring, incoming, taps)


def exchange(by_side, side_of_dir, dir_of_side, flips):
    facing = jnp.take(by_side, side_of_dir, axis=0)
    turned = jnp.take(flips, side_of_dir, axis=0)[:, None, None, None] == 1
    facing = jnp.where(turned, facing[:, :, ::-1], facing)
    got = [None] * 4
    for axis, low, high in (("face", 0, 2), ("tile", 3, 1)):
        count = lax.axis_size(axis)
        up = [(i, (i + 1) % count) for i in range(count)]
        down = [(target, source) for source, target in up]
        got[low] = lax.ppermute(facing[high], axis, up)
        got[high] = lax.ppermute(facing[low], axis, down)
    return jnp.take(jnp.stack(got, axis=0), dir_of_side, axis=0)


def all_sum(part):
    for axis in ("tile", "face"):
        count = lax.axis_size(axis)
        bit = 1
        while bit < count:
            part = part + lax.ppermute(part, axis, [(i, i ^ bit) for i in range(count)])
            bit *= 2
    return part


def shards(
    state, cotangent, depth_weight, depth_bias, point_weight, tile_links, link_sides, link_flips, corner_masks
):
    batch, side, cols, channels = state.shape
    face_count = lax.axis_size("face")
    tile_count = lax.axis_size("tile")
    face_pos = lax.axis_index("face")
    tile_pos = lax.axis_index("tile")
    toward = jnp.stack(
        [
            (face_pos - 1) % face_count * tile_count + tile_pos,
            face_pos * tile_count + (tile_pos + 1) % tile_count,
            (face_pos + 1) % face_count * tile_count + tile_pos,
            face_pos * tile_count + (tile_pos - 1) % tile_count,
        ]
    )
    matched = tile_links[0][:, None] == toward[None, :]
    counter = jnp.arange(4, dtype=jnp.int32)
    dir_of_side = jnp.sum(jnp.where(matched, counter[None, :], 0), axis=1)
    side_of_dir = jnp.sum(jnp.where(matched, counter[:, None], 0), axis=0)
    flips = link_flips[0]
    mask = corner_masks[0].astype(F32)

    taps = jnp.broadcast_to(
        depth_weight.reshape(9, 2, 1, LANES).transpose(1, 0, 2, 3), (2, 9, SUB, LANES)
    )
    bias = jnp.broadcast_to(depth_bias.reshape(2, 1, LANES), (2, SUB, LANES))

    edges = jnp.stack([state[:, 0], state[:, :, -1], state[:, -1], state[:, :, 0]], axis=0)
    rims = exchange(edges, side_of_dir, dir_of_side, flips)
    grad, point_inner, depth_inner = inner_call(state, cotangent, point_weight, taps, bias)
    ring, rim_grads, point_ring, depth_ring = ring_call(
        mask, state, cotangent, rims, point_weight, taps, bias
    )
    incoming = exchange(rim_grads, side_of_dir, dir_of_side, flips)
    field_grad = spread_call(grad, ring, incoming, taps)

    depth_part = jnp.sum(depth_inner + depth_ring, axis=2).transpose(1, 0, 2).reshape(10, channels)
    part = jnp.concatenate(
        [point_inner + point_ring, depth_part, jnp.zeros((6, channels), F32)], axis=0
    )
    total = all_sum(part) * float(batch * side * cols * face_count * tile_count) ** -0.5
    return field_grad, total[channels : channels + 9], total[channels + 9], total[:channels]


def solution(mesh):
    tiles = P(None, "face", "tile", None)
    table = P(("face", "tile"), None)
    return jax.shard_map(
        shards,
        mesh=mesh,
        in_specs=(tiles, tiles, P(), P(), P(), table, table, table, table),
        out_specs=(tiles, P(), P(), P()),
        check_vma=False,
    )
```

```python
import functools

import jax
import jax.numpy as jnp
from jax import lax
from jax.experimental import pallas as pl
from jax.experimental.pallas import tpu as pltpu
from jax.sharding import PartitionSpec as P

ROOT = 0.7978845608028654
CUBIC = 0.044715
F32 = jnp.float32
BF16 = jnp.bfloat16
LANES = 128
SUB = 8
PAD = 8


def gelu_pair(h):
    h2 = h * h
    s = 0.5 * jnp.tanh(h * ((CUBIC * ROOT) * h2 + ROOT)) + 0.5
    act = h * s
    slope = s + act * (1.0 - s) * ((6.0 * CUBIC * ROOT) * h2 + 2.0 * ROOT)
    return act, slope


def inner_body(rows_at_once, x_ref, cot_ref, w_ref, tap_ref, bias_ref, gh_ref, pg_ref, dg_ref, xf, ga, act, acc):
    step = pl.program_id(0)
    side = x_ref.shape[1]
    cols = x_ref.shape[2]

    @pl.when(step == 0)
    def _():
        edge = jnp.zeros((side, PAD, LANES), F32)
        for hf in range(2):
            xf[hf, :, 0:PAD, :] = edge
            xf[hf, :, PAD + cols : 2 * PAD + cols, :] = edge
        act[0] = jnp.zeros(act.shape[1:], BF16)
        act[side - 1] = jnp.zeros(act.shape[1:], BF16)
        acc[...] = jnp.zeros_like(acc)
        pg_ref[...] = jnp.zeros_like(pg_ref)

    gh_ref[0, 0] = jnp.zeros(gh_ref.shape[2:], BF16)
    gh_ref[0, side - 1] = jnp.zeros(gh_ref.shape[2:], BF16)

    def widen(i, _):
        v = x_ref[0, i].astype(F32)
        xf[0, i, PAD : PAD + cols, :] = v[:, :LANES]
        xf[1, i, PAD : PAD + cols, :] = v[:, LANES:]
        return 0

    lax.fori_loop(0, side, widen, 0, unroll=4)
    w = w_ref[...]

    def back_rows(k, _):
        c = cot_ref[0, pl.ds(k * 8, 8)].reshape(8 * cols, 2 * LANES)
        g = lax.dot_general(c, w, (((1,), (1,)), ((), ())), preferred_element_type=F32)
        g = g.reshape(8, cols, 2 * LANES)
        ga[0, pl.ds(k * 8, 8)] = g[:, :, :LANES]
        ga[1, pl.ds(k * 8, 8)] = g[:, :, LANES:]
        return 0

    lax.fori_loop(0, side // 8, back_rows, 0)
    row = lax.broadcasted_iota(jnp.int32, (SUB, LANES), 0)
    inner = side - 2
    for hf in range(2):
        lanes = slice(hf * LANES, hf * LANES + LANES)
        for jb in range(cols // 16):

            def body(it, carry, count, base):
                i = base + it * count
                accs = list(carry)
                win = {}
                for q in range(count):
                    pair = []
                    for part in range(2):
                        j = PAD + jb * 16 + part * SUB
                        for r in range(3):
                            for c in range(3):
                                if (q + r, c, part) not in win:
                                    win[q + r, c, part] = xf[hf, i - 1 + q + r, j - 1 + c : j - 1 + c + SUB, :]
                        h = bias_ref[hf]
                        for r in range(3):
                            for c in range(3):
                                h = h + tap_ref[hf, 3 * r + c] * win[q + r, c, part]
                        a, slope = gelu_pair(h)
                        g = ga[hf, i + q, jb * 16 + part * SUB : jb * 16 + part * SUB + SUB, :] * slope
                        if jb == 0 and part == 0:
                            g = jnp.where(row > 0, g, 0.0)
                            a = jnp.where(row > 0, a, 0.0)
                        if jb == cols // 16 - 1 and part == 1:
                            g = jnp.where(row < SUB - 1, g, 0.0)
                            a = jnp.where(row < SUB - 1, a, 0.0)
                        pair.append((a, g))
                        for r in range(3):
                            for c in range(3):
                                accs[3 * r + c] = accs[3 * r + c] + g * win[q + r, c, part]
                        accs[9] = accs[9] + g
                    act[i + q, jb * 16 : jb * 16 + 16, lanes] = jnp.concatenate(
                        [pair[0][0], pair[1][0]], axis=0
                    ).astype(BF16)
                    gh_ref[0, i + q, jb * 16 : jb * 16 + 16, lanes] = jnp.concatenate(
                        [pair[0][1], pair[1][1]], axis=0
                    ).astype(BF16)
                return tuple(accs)

            out = tuple(acc[hf, k] for k in range(10))
            trips = inner // rows_at_once
            out = lax.fori_loop(0, trips, functools.partial(body, count=rows_at_once, base=1), out)
            if inner % rows_at_once:
                out = body(0, out, inner % rows_at_once, 1 + trips * rows_at_once)
            for k in range(10):
                acc[hf, k] = out[k]

    def outer_rows(k, _):
        a = act[pl.ds(k * 16, 16)].reshape(16 * cols, 2 * LANES)
        c = cot_ref[0, pl.ds(k * 16, 16)].reshape(16 * cols, 2 * LANES)
        pg_ref[...] += lax.dot_general(a, c, (((0,), (0,)), ((), ())), preferred_element_type=F32)
        return 0

    lax.fori_loop(0, side // 16, outer_rows, 0)

    @pl.when(step == pl.num_programs(0) - 1)
    def _():
        dg_ref[...] = acc[...]


def inner_call(state, cotangent, weight, taps, bias):
    batch, side, cols, channels = state.shape
    tile = pl.BlockSpec((1, side, cols, channels), lambda b: (b, 0, 0, 0))
    return pl.pallas_call(
        functools.partial(inner_body, 4),
        grid=(batch,),
        in_specs=[
            tile,
            tile,
            pl.BlockSpec((channels, channels), lambda b: (0, 0)),
            pl.BlockSpec((2, 9, SUB, LANES), lambda b: (0, 0, 0, 0)),
            pl.BlockSpec((2, SUB, LANES), lambda b: (0, 0, 0)),
        ],
        out_specs=[
            tile,
            pl.BlockSpec((channels, channels), lambda b: (0, 0)),
            pl.BlockSpec((2, 10, SUB, LANES), lambda b: (0, 0, 0, 0)),
        ],
        out_shape=[
            jax.ShapeDtypeStruct(state.shape, BF16),
            jax.ShapeDtypeStruct((channels, channels), F32),
            jax.ShapeDtypeStruct((2, 10, SUB, LANES), F32),
        ],
        scratch_shapes=[
            pltpu.VMEM((2, side, cols + 2 * PAD, LANES), F32),
            pltpu.VMEM((2, side, cols, LANES), F32),
            pltpu.VMEM((side, cols, channels), BF16),
            pltpu.VMEM((2, 10, SUB, LANES), F32),
        ],
        compiler_params=pltpu.CompilerParams(vmem_limit_bytes=60 << 20),
        cost_estimate=pl.CostEstimate(
            flops=40_000_000_000, bytes_accessed=26 << 20, transcendentals=state.size
        ),
        name="inner",
    )(state, cotangent, weight, taps, bias)


LOW = (0, 1, 3, 0)
HIGH = (1, 2, 2, 3)


def ring_body(
    mask_ref, top_ref, low_ref, left_ref, right_ref, ctop_ref, clow_ref, cleft_ref, cright_ref,
    rim_ref, w_ref, tap_ref, bias_ref, pg_ref, dg_ref, gr_ref, rg_ref, part_ref, strip, ext, acts, acc,
):
    step = pl.program_id(0)
    side = rim_ref.shape[2]

    @pl.when(step == 0)
    def _():
        acc[...] = dg_ref[...]
        part_ref[0 : 2 * LANES, :] = pg_ref[...]
        ext[...] = jnp.zeros_like(ext)

    rims = [rim_ref[s, 0].astype(F32) for s in range(4)]
    top = top_ref[0].astype(F32)
    low = low_ref[0].astype(F32)
    left = left_ref[0].astype(F32)
    right = right_ref[0].astype(F32)
    last = left.shape[1] - 1
    end = side - 1

    def corner(k, first, second):
        return (mask_ref[k] * 0.5 * (first + second)).astype(BF16).astype(F32)

    def at(s, i):
        return rims[s][i : i + 1]

    nw = corner(0, at(0, 0), at(3, 0))
    ne = corner(1, at(0, end), at(1, 0))
    se = corner(2, at(1, end), at(2, end))
    sw = corner(3, at(2, 0), at(3, end))
    lines = (
        ((rims[0], nw, ne), (top[0], at(3, 0), at(1, 0)), (top[1], at(3, 1), at(1, 1))),
        (
            (right[:, last - 1], at(0, end - 1), at(2, end - 1)),
            (right[:, last], at(0, end), at(2, end)),
            (rims[1], ne, se),
        ),
        (
            (low[0], at(3, end - 1), at(1, end - 1)),
            (low[1], at(3, end), at(1, end)),
            (rims[2], sw, se),
        ),
        ((rims[3], nw, sw), (left[:, 0], at(0, 0), at(2, 0)), (left[:, 1], at(0, 1), at(2, 1))),
    )
    for s in range(4):
        for a in range(3):
            line, before, after = lines[s][a]
            for hf in range(2):
                lanes = slice(hf * LANES, hf * LANES + LANES)
                strip[s, hf, a, PAD : PAD + side, :] = line[:, lanes]
                strip[s, hf, a, PAD - 1 : PAD, :] = before[:, lanes]
                strip[s, hf, a, PAD + side : PAD + side + 1, :] = after[:, lanes]
    cots = jnp.concatenate(
        [
            ctop_ref[0, 0].astype(F32),
            cright_ref[0].astype(F32)[:, last],
            clow_ref[0, 0].astype(F32),
            cleft_ref[0].astype(F32)[:, 0],
        ],
        axis=0,
    ).astype(BF16)
    ga = lax.dot_general(cots, w_ref[...], (((1,), (1,)), ((), ())), preferred_element_type=F32)
    row = lax.broadcasted_iota(jnp.int32, (side, LANES), 0)
    middle = jnp.logical_and(row > 0, row < end)
    for s in range(4):
        upright = s % 2 == 0
        rim_line = 0 if s in (0, 3) else 2
        for hf in range(2):
            lanes = slice(hf * LANES, hf * LANES + LANES)

            def tap(a, b):
                k = 3 * a + b if upright else 3 * b + a
                return k, tap_ref[hf, k, 0:1, :]

            h = jnp.zeros((side, LANES), F32) + bias_ref[hf, 0:1, :]
            for a in range(3):
                for b in range(3):
                    h = h + tap(a, b)[1] * strip[s, hf, a, PAD - 1 + b : PAD - 1 + b + side, :]
            act, slope = gelu_pair(h)
            g = (ga[s * side : s * side + side, lanes] * slope).astype(BF16)
            gr_ref[s, 0, :, lanes] = g
            g = g.astype(F32)
            counted = g
            if not upright:
                counted = jnp.where(middle, g, 0.0)
                act = jnp.where(middle, act, 0.0)
            acts[s * side : s * side + side, lanes] = act.astype(BF16)
            for a in range(3):
                for b in range(3):
                    k = tap(a, b)[0]
                    term = counted * strip[s, hf, a, PAD - 1 + b : PAD - 1 + b + side, :]
                    acc[hf, k] += jnp.sum(term.reshape(side // SUB, SUB, LANES), axis=0)
            acc[hf, 9] += jnp.sum(counted.reshape(side // SUB, SUB, LANES), axis=0)
            ext[PAD : PAD + side, :] = g
            first, mid, final = (tap(rim_line, b)[1] for b in range(3))
            back = (
                first * ext[PAD + 1 : PAD + 1 + side, :]
                + mid * g
                + final * ext[PAD - 1 : PAD - 1 + side, :]
            )
            back = back + jnp.where(row == 0, (0.5 * mask_ref[LOW[s]]) * first * g, 0.0)
            back = back + jnp.where(row == end, (0.5 * mask_ref[HIGH[s]]) * final * g, 0.0)
            rg_ref[s, 0, :, lanes] = back.astype(BF16)
    part_ref[0 : 2 * LANES, :] += lax.dot_general(
        acts[...], cots, (((0,), (0,)), ((), ())), preferred_element_type=F32
    )

    @pl.when(step == pl.num_programs(0) - 1)
    def _():
        part_ref[2 * LANES :, :] = jnp.zeros((16, 2 * LANES), F32)
        for hf in range(2):
            for k in range(10):
                line = jnp.sum(acc[hf, k], axis=0, keepdims=True)
                part_ref[2 * LANES + k : 2 * LANES + k + 1, hf * LANES : hf * LANES + LANES] = line


def ring_call(mask, state, cotangent, rims, weight, taps, bias, point_inner, depth_inner):
    batch, side, cols, channels = state.shape
    wide = 16
    two = lambda at: pl.BlockSpec((1, 2, cols, channels), lambda b: (b, at, 0, 0))
    one = lambda at: pl.BlockSpec((1, 1, cols, channels), lambda b: (b, at, 0, 0))
    column = lambda at: pl.BlockSpec((1, side, wide, channels), lambda b: (b, 0, at, 0))
    strips = pl.BlockSpec((4, 1, side, channels), lambda b: (0, b, 0, 0))
    far = cols // wide - 1
    return pl.pallas_call(
        ring_body,
        grid=(batch,),
        in_specs=[
            pl.BlockSpec(memory_space=pltpu.SMEM),
            two(0),
            two(side // 2 - 1),
            column(0),
            column(far),
            one(0),
            one(side - 1),
            column(0),
            column(far),
            strips,
            pl.BlockSpec((channels, channels), lambda b: (0, 0)),
            pl.BlockSpec((2, 9, SUB, LANES), lambda b: (0, 0, 0, 0)),
            pl.BlockSpec((2, SUB, LANES), lambda b: (0, 0, 0)),
            pl.BlockSpec((channels, channels), lambda b: (0, 0)),
            pl.BlockSpec((2, 10, SUB, LANES), lambda b: (0, 0, 0, 0)),
        ],
        out_specs=[strips, strips, pl.BlockSpec((channels + 16, channels), lambda b: (0, 0))],
        out_shape=[
            jax.ShapeDtypeStruct((4, batch, side, channels), BF16),
            jax.ShapeDtypeStruct((4, batch, side, channels), BF16),
            jax.ShapeDtypeStruct((channels + 16, channels), F32),
        ],
        scratch_shapes=[
            pltpu.VMEM((4, 2, 3, cols + 2 * PAD, LANES), F32),
            pltpu.VMEM((cols + 2 * PAD, LANES), F32),
            pltpu.VMEM((4 * side, channels), BF16),
            pltpu.VMEM((2, 10, SUB, LANES), F32),
        ],
        compiler_params=pltpu.CompilerParams(vmem_limit_bytes=60 << 20),
        cost_estimate=pl.CostEstimate(
            flops=3_000_000_000, bytes_accessed=12 << 20, transcendentals=state.size // 16
        ),
        name="ring",
    )(mask, state, state, state, state, cotangent, cotangent, cotangent, cotangent, rims, weight, taps, bias,
      point_inner, depth_inner)


def spread_body(rows, gh_ref, above_ref, below_ref, gr_ref, in_ref, tap_ref, *rest):
    out_ref, token_ref, gf, near, far, ring = rest[-6:]
    step = pl.program_id(0) + rest[-7]
    side = gr_ref.shape[2]
    cols = gh_ref.shape[2]
    count = gh_ref.shape[1]
    chunks = side // count
    token_ref[...] = jnp.zeros_like(token_ref)
    start = step * count

    @pl.when(pl.program_id(0) == 0)
    def _():
        for hf in range(2):
            lanes = slice(hf * LANES, hf * LANES + LANES)
            gf[hf, :, 0:PAD, :] = jnp.zeros((count + 2, PAD, LANES), F32)
            gf[hf, :, PAD + cols : 2 * PAD + cols, :] = jnp.zeros((count + 2, PAD, LANES), F32)
            for k, s in enumerate((1, 3)):
                ring[k, hf, 0:PAD, :] = jnp.zeros((PAD, LANES), F32)
                ring[k, hf, PAD + side :, :] = jnp.zeros((PAD, LANES), F32)
                ring[k, hf, PAD : PAD + side, :] = gr_ref[s, 0, :, lanes].astype(F32)
        near[...] = jnp.zeros_like(near)
        far[...] = jnp.zeros_like(far)

    def put(i, v):
        v = v.astype(F32)
        gf[0, i, PAD : PAD + cols, :] = v[:, :LANES]
        gf[1, i, PAD : PAD + cols, :] = v[:, LANES:]

    put(0, jnp.where(step > 0, above_ref[0, 0], jnp.zeros_like(above_ref[0, 0])))
    put(count + 1, jnp.where(step < chunks - 1, below_ref[0, 0], jnp.zeros_like(below_ref[0, 0])))
    for i in range(count):
        put(i + 1, gh_ref[0, i])
    back = [in_ref[s, 0, pl.ds(pl.multiple_of(start, count), count), :].astype(F32) for s in (1, 3)]
    for hf in range(2):
        lanes = slice(hf * LANES, hf * LANES + LANES)
        for k, j in ((0, PAD + cols - 1), (1, PAD)):
            own = ring[k, hf, pl.ds(pl.multiple_of(PAD + start, SUB), count), :]
            gf[hf, 1 : count + 1, j : j + 1, :] = own.reshape(count, 1, LANES)
            gf[hf, 0, j : j + 1, :] = ring[k, hf, pl.ds(PAD + start - 1, 1), :]
            gf[hf, count + 1, j : j + 1, :] = ring[k, hf, pl.ds(PAD + start + count, 1), :]
        near[hf, :, 0:1, :] = back[1][:, lanes].reshape(count, 1, LANES)
        far[hf, :, SUB - 1 : SUB, :] = back[0][:, lanes].reshape(count, 1, LANES)

    def line(i, s):
        v = gr_ref[s, 0].astype(F32)
        for hf in range(2):
            gf[hf, i, PAD : PAD + cols, :] = v[:, hf * LANES : hf * LANES + LANES]

    @pl.when(step == 0)
    def _():
        line(1, 0)

    @pl.when(step == chunks - 1)
    def _():
        line(count, 2)

    for hf in range(2):
        lanes = slice(hf * LANES, hf * LANES + LANES)

        for jb in range(cols // 16):

            def body(it, carry):
                i = it * rows
                win = {}
                for q in range(rows):
                    pair = []
                    for half in range(2):
                        j = PAD + jb * 16 + half * SUB
                        total = None
                        for r in range(3):
                            for c in range(3):
                                at = (q + 2 - r, 2 - c, half)
                                if at not in win:
                                    win[at] = gf[hf, i + at[0], j - 1 + at[1] : j - 1 + at[1] + SUB, :]
                                term = tap_ref[hf, 3 * r + c] * win[at]
                                total = term if total is None else total + term
                        if jb == 0 and half == 0:
                            total = total + near[hf, i + q]
                        if jb == cols // 16 - 1 and half == 1:
                            total = total + far[hf, i + q]
                        pair.append(total)
                    out_ref[0, i + q, jb * 16 : jb * 16 + 16, lanes] = jnp.concatenate(pair, axis=0).astype(BF16)
                return carry

            lax.fori_loop(0, count // rows, body, 0)

    def add(i, s):
        out_ref[0, i] = (out_ref[0, i].astype(F32) + in_ref[s, 0].astype(F32)).astype(BF16)

    @pl.when(step == 0)
    def _():
        add(0, 0)

    @pl.when(step == chunks - 1)
    def _():
        add(count - 1, 2)


CHUNK = 16
STEPS = 2


def spread_call(part, grad, ring, incoming, taps, into):
    batch, side, cols, channels = grad.shape
    parts = side // (CHUNK * STEPS)
    b, first = part // parts, part % parts * STEPS
    low, high = first * CHUNK, side - 1
    strips = pl.BlockSpec((4, 1, side, channels), lambda i: (0, b, 0, 0))
    in_specs = [
        pl.BlockSpec((1, CHUNK, cols, channels), lambda i: (b, i + first, 0, 0)),
        pl.BlockSpec((1, 1, cols, channels), lambda i: (b, jnp.maximum((i + first) * CHUNK - 1, 0), 0, 0)),
        pl.BlockSpec((1, 1, cols, channels), lambda i: (b, jnp.minimum((i + first + 1) * CHUNK, high), 0, 0)),
        strips,
        strips,
        pl.BlockSpec((2, 9, SUB, LANES), lambda i: (0, 0, 0, 0)),
    ]
    operands = [grad, grad, grad, ring, incoming, taps]
    aliases = {}
    if into is not None:
        in_specs.append(pl.BlockSpec(memory_space=pl.ANY))
        operands.append(into)
        aliases = {6: 0}

    def body(*refs):
        n = len(operands)
        spread_body(4, *refs[:6], first, *refs[n:])

    return pl.pallas_call(
        body,
        grid=(STEPS,),
        in_specs=in_specs,
        out_specs=[
            pl.BlockSpec((1, CHUNK, cols, channels), lambda i: (b, i + first, 0, 0)),
            pl.BlockSpec((SUB, LANES), lambda i: (0, 0)),
        ],
        out_shape=[jax.ShapeDtypeStruct(grad.shape, BF16), jax.ShapeDtypeStruct((SUB, LANES), F32)],
        scratch_shapes=[
            pltpu.VMEM((2, CHUNK + 2, cols + 2 * PAD, LANES), F32),
            pltpu.VMEM((2, CHUNK, SUB, LANES), F32),
            pltpu.VMEM((2, CHUNK, SUB, LANES), F32),
            pltpu.VMEM((2, 2, side + 2 * PAD, LANES), F32),
        ],
        input_output_aliases=aliases,
        compiler_params=pltpu.CompilerParams(vmem_limit_bytes=60 << 20),
        cost_estimate=pl.CostEstimate(
            flops=1_500_000_000, bytes_accessed=grad.size * 4 // (batch * parts), transcendentals=0
        ),
        name="spread",
    )(*operands)


def finish_body(scale, bit_ref, mine_ref, other_ref, dg_ref, bg_ref, pg_ref):
    rows = mine_ref.shape[0]
    channels = pg_ref.shape[0]
    own = mine_ref[...] * scale
    far = other_ref[...] * scale
    first = bit_ref[0] == 0
    low = jnp.where(first, own, far)
    high = jnp.where(first, far, own)
    pg_ref[0:rows, :] = low
    pg_ref[rows:channels, :] = high[: channels - rows]
    tail = high[channels - rows :]
    dg_ref[...] = tail[0:9]
    bg_ref[...] = tail[9:10]


def finish_call(scale, bit, mine, other):
    channels = mine.shape[1]
    vmem = pl.BlockSpec(memory_space=pltpu.VMEM)
    return pl.pallas_call(
        functools.partial(finish_body, scale),
        in_specs=[pl.BlockSpec(memory_space=pltpu.SMEM), vmem, vmem],
        out_specs=[vmem, vmem, vmem],
        out_shape=[
            jax.ShapeDtypeStruct((9, channels), F32),
            jax.ShapeDtypeStruct((1, channels), F32),
            jax.ShapeDtypeStruct((channels, channels), F32),
        ],
        name="finish",
    )(bit, mine, other)


def exchange(by_side, side_of_dir, dir_of_side, flips):
    facing = jnp.take(by_side, side_of_dir, axis=0)
    turned = jnp.take(flips, side_of_dir, axis=0)[:, None, None, None] == 1
    facing = jnp.where(turned, facing[:, :, ::-1], facing)
    got = [None] * 4
    for axis, low, high in (("face", 0, 2), ("tile", 3, 1)):
        count = lax.axis_size(axis)
        up = [(i, (i + 1) % count) for i in range(count)]
        down = [(target, source) for source, target in up]
        got[low] = lax.ppermute(facing[high], axis, up)
        got[high] = lax.ppermute(facing[low], axis, down)
    return jnp.take(jnp.stack(got, axis=0), dir_of_side, axis=0)


def swap(value, mask):
    devices = lax.axis_size("face") * lax.axis_size("tile")
    return lax.ppermute(value, ("face", "tile"), [(i, i ^ mask) for i in range(devices)])


def after(value, *others):
    return lax.optimization_barrier((value, *others))[0]


def shards(
    state, cotangent, depth_weight, depth_bias, point_weight, tile_links, link_sides, link_flips, corner_masks
):
    batch, side, cols, channels = state.shape
    face_count = lax.axis_size("face")
    tile_count = lax.axis_size("tile")
    face_pos = lax.axis_index("face")
    tile_pos = lax.axis_index("tile")
    toward = jnp.stack(
        [
            (face_pos - 1) % face_count * tile_count + tile_pos,
            face_pos * tile_count + (tile_pos + 1) % tile_count,
            (face_pos + 1) % face_count * tile_count + tile_pos,
            face_pos * tile_count + (tile_pos - 1) % tile_count,
        ]
    )
    matched = tile_links[0][:, None] == toward[None, :]
    counter = jnp.arange(4, dtype=jnp.int32)
    dir_of_side = jnp.sum(jnp.where(matched, counter[None, :], 0), axis=1)
    side_of_dir = jnp.sum(jnp.where(matched, counter[:, None], 0), axis=0)
    flips = link_flips[0]
    mask = corner_masks[0].astype(F32)

    taps = jnp.broadcast_to(
        depth_weight.reshape(9, 2, 1, LANES).transpose(1, 0, 2, 3), (2, 9, SUB, LANES)
    )
    bias = jnp.broadcast_to(depth_bias.reshape(2, 1, LANES), (2, SUB, LANES))

    edges = jnp.stack([state[:, 0], state[:, :, -1], state[:, -1], state[:, :, 0]], axis=0)
    rims = exchange(edges, side_of_dir, dir_of_side, flips)
    grad, point_inner, depth_inner = inner_call(state, cotangent, point_weight, taps, bias)
    ring, rim_grads, part = ring_call(
        mask, state, cotangent, rims, point_weight, taps, bias, point_inner, depth_inner
    )
    incoming = exchange(rim_grads, side_of_dir, dir_of_side, flips)

    core = tile_pos % 2
    half = part.shape[0] // 2
    low, high = part[:half], part[half:]
    mine = jnp.where(core == 0, low, high)
    sent = jnp.where(core == 0, high, low)
    pieces = batch * side // (CHUNK * STEPS)
    field_grad = None
    for stage, mask_bits in enumerate((1, 2, 6, 8, 24, 32, 96, 1)):
        got = swap(sent if stage == 0 else mine, mask_bits)
        if stage < pieces:
            held = after(taps, mine if stage else sent)
            field_grad, token = spread_call(stage, grad, ring, incoming, held, field_grad)
            got = after(got, token)
        if stage < 7:
            mine = mine + got
    scale = float(batch * side * cols * face_count * tile_count) ** -0.5
    depth_grad, bias_grad, point_grad = finish_call(scale, core.reshape(1), mine, got)
    return field_grad, depth_grad, bias_grad.reshape(channels), point_grad


def solution(mesh):
    tiles = P(None, "face", "tile", None)
    table = P(("face", "tile"), None)
    return jax.shard_map(
        shards,
        mesh=mesh,
        in_specs=(tiles, tiles, P(), P(), P(), table, table, table, table),
        out_specs=(tiles, P(), P(), P()),
        check_vma=False,
    )
```

```python
import functools

import jax
import jax.numpy as jnp
from jax import lax
from jax.experimental import pallas as pl
from jax.experimental.pallas import tpu as pltpu
from jax.sharding import PartitionSpec as P

ROOT = 0.7978845608028654
CUBIC = 0.044715
F32 = jnp.float32
BF16 = jnp.bfloat16
LANES = 128
SUB = 8
PAD = 8


def gelu_pair(h):
    h2 = h * h
    s = 0.5 * jnp.tanh(h * ((CUBIC * ROOT) * h2 + ROOT)) + 0.5
    act = h * s
    slope = s + act * (1.0 - s) * ((6.0 * CUBIC * ROOT) * h2 + 2.0 * ROOT)
    return act, slope


ALPHA = (CUBIC * ROOT) ** (1.0 / 3.0)
KAPPA = ROOT / ALPHA


def gelu_scaled(h):
    h2 = h * h
    t = jnp.tanh(h * (h2 + KAPPA))
    up = 1.0 + t
    act = h * up
    return act, up + act * (1.0 - t) * (3.0 * h2 + KAPPA)


def tap_at(ref, hf, k):
    return jnp.broadcast_to(ref[k : k + 1, hf * LANES : hf * LANES + LANES], (SUB, LANES))


def inner_body(pairs, x_ref, cot_ref, w_ref, tap_ref, bias_ref, gh_ref, pg_ref, dg_ref, u, hide, acc, half_w, *bufs):
    step = pl.program_id(0)
    side = x_ref.shape[1]
    cols = x_ref.shape[2]
    sets = (bufs[0:4], bufs[4:8])

    @pl.when(step == 0)
    def _():
        for hf in range(2):
            for c in range(3):
                w0, w1, w2 = (tap_at(tap_ref, hf, 3 * r + c) * ALPHA for r in range(3))
                u[hf, c] = w0
                u[hf, 3 + c] = (w0 + w1 + w2) * 0.5
                u[hf, 6 + c] = (w0 - w1 + w2) * 0.5
                u[hf, 9 + c] = w2
            u[hf, 12] = tap_at(bias_ref, hf, 0) * ALPHA
        half_w[...] = w_ref[...] * jnp.asarray(0.5, BF16)
        for qt, _, _, _ in sets:
            edge = jnp.zeros((2, pairs, 4, PAD, LANES), F32)
            qt[:, :, :, 0:PAD, :] = edge
            qt[:, :, :, PAD + cols :, :] = edge
        col = lax.broadcasted_iota(jnp.int32, (cols, 2 * LANES), 0)
        keep = jnp.logical_and(col > 0, col < cols - 1)
        hide[0] = jnp.where(keep, 1.0, 0.0).astype(BF16)
        hide[1] = jnp.zeros((cols, 2 * LANES), BF16)
        acc[...] = jnp.zeros_like(acc)
        pg_ref[...] = jnp.zeros_like(pg_ref)

    rows = 2 * pairs

    def outer(buf):
        _, _, act, cot = buf
        pg_ref[...] += lax.dot_general(
            act[...], cot[...], (((0,), (0,)), ((), ())), preferred_element_type=F32
        )

    def chunk(t, buf):
        qt, ga, act, cot = buf
        base = t * rows
        for q in range(rows):
            i = base + q
            kind = jnp.where(jnp.logical_or(i == 0, i == side - 1), 1, 0)
            cot[q * cols : q * cols + cols, :] = cot_ref[0, i] * hide[kind]
        g = lax.dot_general(cot[...], half_w[...], (((1,), (1,)), ((), ())), preferred_element_type=F32)
        ga[0] = g[:, :LANES]
        ga[1] = g[:, LANES:]
        for hf in range(2):
            lanes = slice(hf * LANES, hf * LANES + LANES)
            line = [x_ref[0, jnp.maximum(base - 1, 0), :, lanes].astype(F32)]
            for q in range(rows):
                line.append(x_ref[0, base + q, :, lanes].astype(F32))
            line.append(x_ref[0, jnp.minimum(base + rows, side - 1), :, lanes].astype(F32))
            for p in range(pairs):
                q0, q1, q2, q3 = line[2 * p : 2 * p + 4]
                for k, v in enumerate((q0 - q2, q1 + q2, q2 - q1, q1 - q3)):
                    qt[hf, p, k, PAD : PAD + cols, :] = v
        for hf in range(2):
            lanes = slice(hf * LANES, hf * LANES + LANES)
            sums = [acc[hf, k] for k in range(13)]
            for p in range(pairs):
                for jb in range(cols // 16):
                    halves = []
                    for half in range(2):
                        j = jb * 16 + half * SUB
                        win = [
                            [qt[hf, p, k, PAD - 1 + j + c : PAD - 1 + j + c + SUB, :] for c in range(3)]
                            for k in range(4)
                        ]
                        m = []
                        for k in range(4):
                            v = u[hf, 3 * k] * win[k][0]
                            v = v + u[hf, 3 * k + 1] * win[k][1]
                            m.append(v + u[hf, 3 * k + 2] * win[k][2])
                        both = m[1] + u[hf, 12]
                        found = []
                        for q, h in enumerate((both + m[0] + m[2], both - m[2] - m[3])):
                            a, slope = gelu_scaled(h)
                            at = (2 * p + q) * cols + j
                            found.append((a, ga[hf, at : at + SUB, :] * slope))
                        g0, g1 = found[0][1], found[1][1]
                        plus, minus = g0 + g1, g0 - g1
                        for k, v in enumerate((g0, plus, minus, g1)):
                            for c in range(3):
                                sums[3 * k + c] = sums[3 * k + c] + v * win[k][c]
                        sums[12] = sums[12] + plus
                        halves.append(found)
                    for q in range(2):
                        at = (2 * p + q) * cols + jb * 16
                        act[at : at + 16, lanes] = jnp.concatenate(
                            [halves[0][q][0], halves[1][q][0]], axis=0
                        ).astype(BF16)
                        gh_ref[0, base + 2 * p + q, jb * 16 : jb * 16 + 16, lanes] = jnp.concatenate(
                            [halves[0][q][1], halves[1][q][1]], axis=0
                        ).astype(BF16)
            for k in range(13):
                acc[hf, k] = sums[k]

    def body(t, carry):
        chunk(2 * t, sets[0])
        outer(sets[1])
        chunk(2 * t + 1, sets[1])
        outer(sets[0])
        return carry

    sets[1][2][...] = jnp.zeros_like(sets[1][2])
    sets[1][3][...] = jnp.zeros_like(sets[1][3])
    lax.fori_loop(0, side // (2 * rows), body, 0)
    outer(sets[1])

    @pl.when(step == pl.num_programs(0) - 1)
    def _():
        for hf in range(2):
            for c in range(3):
                d1, d2, d3, d4 = (acc[hf, 3 * k + c] for k in range(4))
                even = 0.5 * (d2 + d3)
                dg_ref[hf, c] = d1 + even
                dg_ref[hf, 3 + c] = 0.5 * (d2 - d3)
                dg_ref[hf, 6 + c] = even - d4
            dg_ref[hf, 9] = acc[hf, 12]
        pg_ref[...] = pg_ref[...] * (0.5 / ALPHA)


PAIRS = 4


def inner_call(state, cotangent, weight, taps, bias):
    batch, side, cols, channels = state.shape
    tile = pl.BlockSpec((1, side, cols, channels), lambda b: (b, 0, 0, 0))
    buf = [
        pltpu.VMEM((2, PAIRS, 4, cols + 2 * PAD, LANES), F32),
        pltpu.VMEM((2, 2 * PAIRS * cols, LANES), F32),
        pltpu.VMEM((2 * PAIRS * cols, channels), BF16),
        pltpu.VMEM((2 * PAIRS * cols, channels), BF16),
    ]
    return pl.pallas_call(
        functools.partial(inner_body, PAIRS),
        grid=(batch,),
        in_specs=[
            tile,
            tile,
            pl.BlockSpec((channels, channels), lambda b: (0, 0)),
            pl.BlockSpec((9, channels), lambda b: (0, 0)),
            pl.BlockSpec((1, channels), lambda b: (0, 0)),
        ],
        out_specs=[
            tile,
            pl.BlockSpec((channels, channels), lambda b: (0, 0)),
            pl.BlockSpec((2, 10, SUB, LANES), lambda b: (0, 0, 0, 0)),
        ],
        out_shape=[
            jax.ShapeDtypeStruct(state.shape, BF16),
            jax.ShapeDtypeStruct((channels, channels), F32),
            jax.ShapeDtypeStruct((2, 10, SUB, LANES), F32),
        ],
        scratch_shapes=[
            pltpu.VMEM((2, 13, SUB, LANES), F32),
            pltpu.VMEM((2, cols, channels), BF16),
            pltpu.VMEM((2, 13, SUB, LANES), F32),
            pltpu.VMEM((channels, channels), BF16),
            *buf,
            *buf,
        ],
        compiler_params=pltpu.CompilerParams(vmem_limit_bytes=57 << 20),
        cost_estimate=pl.CostEstimate(
            flops=40_000_000_000, bytes_accessed=26 << 20, transcendentals=state.size
        ),
        name="inner",
    )(state, cotangent, weight, taps, bias)


DIR_OF_SIDE, SIDE_OF_DIR, FLIPS, MASKS = 0, 4, 8, 12


def from_dir(table, got, s):
    d = table[DIR_OF_SIDE + s]
    rows = got[3][0]
    for k in range(3):
        rows = jnp.where(d == k, got[k][0], rows)
    return rows


def turn(table, s, rows):
    count = rows.shape[0]
    i = lax.broadcasted_iota(jnp.int32, (count, count), 0)
    j = lax.broadcasted_iota(jnp.int32, (count, count), 1)
    source = jnp.where(table[FLIPS + s] == 1, count - 1 - i, i)
    pick = jnp.where(j == source, 1.0, 0.0).astype(BF16)
    return jnp.dot(pick, rows, preferred_element_type=F32).astype(BF16)


def edges_body(table, top_ref, low_ref, left_ref, right_ref, to0, to1, to2, to3, turned):
    last = right_ref.shape[2] - 1
    turned[0] = turn(table, 0, top_ref[0, 0])
    turned[1] = turn(table, 1, right_ref[0].astype(F32)[:, last].astype(BF16))
    turned[2] = turn(table, 2, low_ref[0, 0])
    turned[3] = turn(table, 3, left_ref[0].astype(F32)[:, 0].astype(BF16))
    for d, to in enumerate((to0, to1, to2, to3)):
        to[0] = turned[table[SIDE_OF_DIR + d]]


def edges_call(table, state):
    batch, side, cols, channels = state.shape
    wide = 16
    one = lambda at: pl.BlockSpec((1, 1, cols, channels), lambda b: (b, at, 0, 0))
    column = lambda at: pl.BlockSpec((1, side, wide, channels), lambda b: (b, 0, at, 0))
    facing = pl.BlockSpec((1, side, channels), lambda b: (b, 0, 0))
    return pl.pallas_call(
        edges_body,
        grid=(batch,),
        in_specs=[
            pl.BlockSpec(memory_space=pltpu.SMEM),
            one(0),
            one(side - 1),
            column(0),
            column(cols // wide - 1),
        ],
        out_specs=[facing] * 4,
        out_shape=[jax.ShapeDtypeStruct((batch, side, channels), BF16)] * 4,
        scratch_shapes=[pltpu.VMEM((4, side, channels), BF16)],
        compiler_params=pltpu.CompilerParams(vmem_limit_bytes=57 << 20),
        name="edges",
    )(table, state, state, state, state)


LOW = (0, 1, 3, 0)
HIGH = (1, 2, 2, 3)


def ring_body(
    table, top_ref, low_ref, left_ref, right_ref, ctop_ref, clow_ref, cleft_ref, cright_ref,
    got0, got1, got2, got3, w_ref, tap_ref, bias_ref, pg_ref, dg_ref,
    gr_ref, to0, to1, to2, to3, part_ref, strip, ext, acts, acc, turned,
):
    step = pl.program_id(0)
    side = got0.shape[1]
    got = (got0, got1, got2, got3)
    masks = [table[MASKS + k].astype(F32) for k in range(4)]

    @pl.when(step == 0)
    def _():
        acc[...] = dg_ref[...]
        part_ref[0 : 2 * LANES, :] = pg_ref[...]
        ext[...] = jnp.zeros_like(ext)

    rims = [from_dir(table, got, s).astype(F32) for s in range(4)]
    top = top_ref[0].astype(F32)
    low = low_ref[0].astype(F32)
    left = left_ref[0].astype(F32)
    right = right_ref[0].astype(F32)
    last = left.shape[1] - 1
    end = side - 1

    def corner(k, first, second):
        return (masks[k] * 0.5 * (first + second)).astype(BF16).astype(F32)

    def at(s, i):
        return rims[s][i : i + 1]

    nw = corner(0, at(0, 0), at(3, 0))
    ne = corner(1, at(0, end), at(1, 0))
    se = corner(2, at(1, end), at(2, end))
    sw = corner(3, at(2, 0), at(3, end))
    lines = (
        ((rims[0], nw, ne), (top[0], at(3, 0), at(1, 0)), (top[1], at(3, 1), at(1, 1))),
        (
            (right[:, last - 1], at(0, end - 1), at(2, end - 1)),
            (right[:, last], at(0, end), at(2, end)),
            (rims[1], ne, se),
        ),
        (
            (low[0], at(3, end - 1), at(1, end - 1)),
            (low[1], at(3, end), at(1, end)),
            (rims[2], sw, se),
        ),
        ((rims[3], nw, sw), (left[:, 0], at(0, 0), at(2, 0)), (left[:, 1], at(0, 1), at(2, 1))),
    )
    for s in range(4):
        for a in range(3):
            line, before, after = lines[s][a]
            for hf in range(2):
                lanes = slice(hf * LANES, hf * LANES + LANES)
                strip[s, hf, a, PAD : PAD + side, :] = line[:, lanes]
                strip[s, hf, a, PAD - 1 : PAD, :] = before[:, lanes]
                strip[s, hf, a, PAD + side : PAD + side + 1, :] = after[:, lanes]
    cots = jnp.concatenate(
        [
            ctop_ref[0, 0].astype(F32),
            cright_ref[0].astype(F32)[:, last],
            clow_ref[0, 0].astype(F32),
            cleft_ref[0].astype(F32)[:, 0],
        ],
        axis=0,
    ).astype(BF16)
    ga = lax.dot_general(cots, w_ref[...], (((1,), (1,)), ((), ())), preferred_element_type=F32)
    row = lax.broadcasted_iota(jnp.int32, (side, LANES), 0)
    middle = jnp.logical_and(row > 0, row < end)
    for s in range(4):
        upright = s % 2 == 0
        rim_line = 0 if s in (0, 3) else 2
        for hf in range(2):
            lanes = slice(hf * LANES, hf * LANES + LANES)

            def tap(a, b):
                k = 3 * a + b if upright else 3 * b + a
                return k, tap_ref[k : k + 1, lanes]

            h = jnp.zeros((side, LANES), F32) + bias_ref[0:1, lanes]
            for a in range(3):
                for b in range(3):
                    h = h + tap(a, b)[1] * strip[s, hf, a, PAD - 1 + b : PAD - 1 + b + side, :]
            act, slope = gelu_pair(h)
            g = (ga[s * side : s * side + side, lanes] * slope).astype(BF16)
            gr_ref[s, 0, :, lanes] = g
            g = g.astype(F32)
            counted = g
            if not upright:
                counted = jnp.where(middle, g, 0.0)
                act = jnp.where(middle, act, 0.0)
            acts[s * side : s * side + side, lanes] = act.astype(BF16)
            for a in range(3):
                for b in range(3):
                    k = tap(a, b)[0]
                    term = counted * strip[s, hf, a, PAD - 1 + b : PAD - 1 + b + side, :]
                    acc[hf, k] += jnp.sum(term.reshape(side // SUB, SUB, LANES), axis=0)
            acc[hf, 9] += jnp.sum(counted.reshape(side // SUB, SUB, LANES), axis=0)
            ext[PAD : PAD + side, :] = g
            first, mid, final = (tap(rim_line, b)[1] for b in range(3))
            back = (
                first * ext[PAD + 1 : PAD + 1 + side, :]
                + mid * g
                + final * ext[PAD - 1 : PAD - 1 + side, :]
            )
            back = back + jnp.where(row == 0, (0.5 * masks[LOW[s]]) * first * g, 0.0)
            back = back + jnp.where(row == end, (0.5 * masks[HIGH[s]]) * final * g, 0.0)
            turned[s, :, lanes] = turn(table, s, back.astype(BF16))
    for d, to in enumerate((to0, to1, to2, to3)):
        to[0] = turned[table[SIDE_OF_DIR + d]]
    part_ref[0 : 2 * LANES, :] += lax.dot_general(
        acts[...], cots, (((0,), (0,)), ((), ())), preferred_element_type=F32
    )

    @pl.when(step == pl.num_programs(0) - 1)
    def _():
        part_ref[2 * LANES :, :] = jnp.zeros((16, 2 * LANES), F32)
        for hf in range(2):
            for k in range(10):
                line = jnp.sum(acc[hf, k], axis=0, keepdims=True)
                part_ref[2 * LANES + k : 2 * LANES + k + 1, hf * LANES : hf * LANES + LANES] = line


def ring_call(table, state, cotangent, got, weight, taps, bias, point_inner, depth_inner):
    batch, side, cols, channels = state.shape
    wide = 16
    two = lambda at: pl.BlockSpec((1, 2, cols, channels), lambda b: (b, at, 0, 0))
    one = lambda at: pl.BlockSpec((1, 1, cols, channels), lambda b: (b, at, 0, 0))
    column = lambda at: pl.BlockSpec((1, side, wide, channels), lambda b: (b, 0, at, 0))
    strips = pl.BlockSpec((4, 1, side, channels), lambda b: (0, b, 0, 0))
    facing = pl.BlockSpec((1, side, channels), lambda b: (b, 0, 0))
    far = cols // wide - 1
    return pl.pallas_call(
        ring_body,
        grid=(batch,),
        in_specs=[
            pl.BlockSpec(memory_space=pltpu.SMEM),
            two(0),
            two(side // 2 - 1),
            column(0),
            column(far),
            one(0),
            one(side - 1),
            column(0),
            column(far),
            *[facing] * 4,
            pl.BlockSpec((channels, channels), lambda b: (0, 0)),
            pl.BlockSpec((9, channels), lambda b: (0, 0)),
            pl.BlockSpec((1, channels), lambda b: (0, 0)),
            pl.BlockSpec((channels, channels), lambda b: (0, 0)),
            pl.BlockSpec((2, 10, SUB, LANES), lambda b: (0, 0, 0, 0)),
        ],
        out_specs=[strips, *[facing] * 4, pl.BlockSpec((channels + 16, channels), lambda b: (0, 0))],
        out_shape=[
            jax.ShapeDtypeStruct((4, batch, side, channels), BF16),
            *[jax.ShapeDtypeStruct((batch, side, channels), BF16)] * 4,
            jax.ShapeDtypeStruct((channels + 16, channels), F32),
        ],
        scratch_shapes=[
            pltpu.VMEM((4, 2, 3, cols + 2 * PAD, LANES), F32),
            pltpu.VMEM((cols + 2 * PAD, LANES), F32),
            pltpu.VMEM((4 * side, channels), BF16),
            pltpu.VMEM((2, 10, SUB, LANES), F32),
            pltpu.VMEM((4, side, channels), BF16),
        ],
        compiler_params=pltpu.CompilerParams(vmem_limit_bytes=57 << 20),
        cost_estimate=pl.CostEstimate(
            flops=3_000_000_000, bytes_accessed=12 << 20, transcendentals=state.size // 16
        ),
        name="ring",
    )(table, state, state, state, state, cotangent, cotangent, cotangent, cotangent, *got, weight, taps, bias,
      point_inner, depth_inner)


def spread_body(rows, first, table, gh_ref, above_ref, below_ref, gr_ref, got0, got1, got2, got3, tap_ref, out_ref, token_ref, gf, near, far, ring, back):
    got = (got0, got1, got2, got3)
    side = gr_ref.shape[2]
    cols = gh_ref.shape[2]
    count = gh_ref.shape[1]
    chunks = side // count
    step = (pl.program_id(0) + first) % chunks
    token_ref[...] = jnp.zeros_like(token_ref)
    start = step * count

    @pl.when(jnp.logical_or(pl.program_id(0) == 0, step == 0))
    def _():
        for k, s in enumerate((1, 3)):
            back[k] = from_dir(table, got, s)
        for hf in range(2):
            lanes = slice(hf * LANES, hf * LANES + LANES)
            gf[hf, :, 0:PAD, :] = jnp.zeros((count + 2, PAD, LANES), F32)
            gf[hf, :, PAD + cols : 2 * PAD + cols, :] = jnp.zeros((count + 2, PAD, LANES), F32)
            for k, s in enumerate((1, 3)):
                ring[k, hf, 0:PAD, :] = jnp.zeros((PAD, LANES), F32)
                ring[k, hf, PAD + side :, :] = jnp.zeros((PAD, LANES), F32)
                ring[k, hf, PAD : PAD + side, :] = gr_ref[s, 0, :, lanes].astype(F32)
        near[...] = jnp.zeros_like(near)
        far[...] = jnp.zeros_like(far)

    def put(i, v):
        v = v.astype(F32)
        gf[0, i, PAD : PAD + cols, :] = v[:, :LANES]
        gf[1, i, PAD : PAD + cols, :] = v[:, LANES:]

    put(0, jnp.where(step > 0, above_ref[0, 0], jnp.zeros_like(above_ref[0, 0])))
    put(count + 1, jnp.where(step < chunks - 1, below_ref[0, 0], jnp.zeros_like(below_ref[0, 0])))
    for i in range(count):
        put(i + 1, gh_ref[0, i])
    cut = [back[k, pl.ds(pl.multiple_of(start, count), count), :].astype(F32) for k in range(2)]
    for hf in range(2):
        lanes = slice(hf * LANES, hf * LANES + LANES)
        for k, j in ((0, PAD + cols - 1), (1, PAD)):
            own = ring[k, hf, pl.ds(pl.multiple_of(PAD + start, SUB), count), :]
            gf[hf, 1 : count + 1, j : j + 1, :] = own.reshape(count, 1, LANES)
            gf[hf, 0, j : j + 1, :] = ring[k, hf, pl.ds(PAD + start - 1, 1), :]
            gf[hf, count + 1, j : j + 1, :] = ring[k, hf, pl.ds(PAD + start + count, 1), :]
        near[hf, :, 0:1, :] = cut[1][:, lanes].reshape(count, 1, LANES)
        far[hf, :, SUB - 1 : SUB, :] = cut[0][:, lanes].reshape(count, 1, LANES)

    def line(i, s):
        v = gr_ref[s, 0].astype(F32)
        for hf in range(2):
            gf[hf, i, PAD : PAD + cols, :] = v[:, hf * LANES : hf * LANES + LANES]

    @pl.when(step == 0)
    def _():
        line(1, 0)

    @pl.when(step == chunks - 1)
    def _():
        line(count, 2)

    for hf in range(2):
        lanes = slice(hf * LANES, hf * LANES + LANES)
        taps = [tap_at(tap_ref, hf, k) for k in range(9)]
        for jb in range(cols // 16):

            def body(it, carry):
                i = it * rows
                win = {}
                for q in range(rows):
                    pair = []
                    for half in range(2):
                        j = PAD + jb * 16 + half * SUB
                        total = None
                        for r in range(3):
                            for c in range(3):
                                at = (q + 2 - r, 2 - c, half)
                                if at not in win:
                                    win[at] = gf[hf, i + at[0], j - 1 + at[1] : j - 1 + at[1] + SUB, :]
                                term = taps[3 * r + c] * win[at]
                                total = term if total is None else total + term
                        if jb == 0 and half == 0:
                            total = total + near[hf, i + q]
                        if jb == cols // 16 - 1 and half == 1:
                            total = total + far[hf, i + q]
                        pair.append(total)
                    out_ref[0, i + q, jb * 16 : jb * 16 + 16, lanes] = jnp.concatenate(pair, axis=0).astype(BF16)
                return carry

            lax.fori_loop(0, count // rows, body, 0)

    def add(i, s):
        out_ref[0, i] = (out_ref[0, i].astype(F32) + from_dir(table, got, s).astype(F32)).astype(BF16)

    @pl.when(step == 0)
    def _():
        add(0, 0)

    @pl.when(step == chunks - 1)
    def _():
        add(count - 1, 2)


CHUNK = 16


def spread_call(first, steps, table, grad, ring, got, taps, into):
    batch, side, cols, channels = grad.shape
    chunks = side // CHUNK
    high = side - 1
    at = lambda i: ((i + first) // chunks, (i + first) % chunks)
    strips = pl.BlockSpec((4, 1, side, channels), lambda i: (0, at(i)[0], 0, 0))
    facing = pl.BlockSpec((1, side, channels), lambda i: (at(i)[0], 0, 0))
    rows = pl.BlockSpec((1, CHUNK, cols, channels), lambda i: (*at(i), 0, 0))
    in_specs = [
        pl.BlockSpec(memory_space=pltpu.SMEM),
        rows,
        pl.BlockSpec((1, 1, cols, channels), lambda i: (at(i)[0], jnp.maximum(at(i)[1] * CHUNK - 1, 0), 0, 0)),
        pl.BlockSpec((1, 1, cols, channels), lambda i: (at(i)[0], jnp.minimum(at(i)[1] * CHUNK + CHUNK, high), 0, 0)),
        strips,
        *[facing] * 4,
        pl.BlockSpec((9, channels), lambda i: (0, 0)),
    ]
    operands = [table, grad, grad, grad, ring, *got, taps]
    aliases = {}
    if into is not None:
        aliases = {len(operands): 0}
        in_specs.append(pl.BlockSpec(memory_space=pl.ANY))
        operands.append(into)

    def body(*refs):
        spread_body(4, first, *refs[:10], *refs[len(operands) :])

    return pl.pallas_call(
        body,
        grid=(steps,),
        in_specs=in_specs,
        out_specs=[rows, pl.BlockSpec((SUB, LANES), lambda i: (0, 0))],
        out_shape=[jax.ShapeDtypeStruct(grad.shape, BF16), jax.ShapeDtypeStruct((SUB, LANES), F32)],
        scratch_shapes=[
            pltpu.VMEM((2, CHUNK + 2, cols + 2 * PAD, LANES), F32),
            pltpu.VMEM((2, CHUNK, SUB, LANES), F32),
            pltpu.VMEM((2, CHUNK, SUB, LANES), F32),
            pltpu.VMEM((2, 2, side + 2 * PAD, LANES), F32),
            pltpu.VMEM((2, side, channels), BF16),
        ],
        input_output_aliases=aliases,
        compiler_params=pltpu.CompilerParams(vmem_limit_bytes=57 << 20),
        cost_estimate=pl.CostEstimate(
            flops=750_000_000 * steps, bytes_accessed=grad.size * 4 * steps // (batch * chunks), transcendentals=0
        ),
        name="spread",
    )(*operands)


def finish_body(scale, bit_ref, mine_ref, other_ref, dg_ref, bg_ref, pg_ref):
    rows = mine_ref.shape[0]
    channels = pg_ref.shape[0]
    own = mine_ref[...] * scale
    far = other_ref[...] * scale
    first = bit_ref[0] == 0
    low = jnp.where(first, own, far)
    high = jnp.where(first, far, own)
    pg_ref[0:rows, :] = low
    pg_ref[rows:channels, :] = high[: channels - rows]
    tail = high[channels - rows :]
    dg_ref[...] = tail[0:9]
    bg_ref[...] = tail[9:10]


def finish_call(scale, bit, mine, other):
    channels = mine.shape[1]
    vmem = pl.BlockSpec(memory_space=pltpu.VMEM)
    return pl.pallas_call(
        functools.partial(finish_body, scale),
        in_specs=[pl.BlockSpec(memory_space=pltpu.SMEM), vmem, vmem],
        out_specs=[vmem, vmem, vmem],
        out_shape=[
            jax.ShapeDtypeStruct((9, channels), F32),
            jax.ShapeDtypeStruct((1, channels), F32),
            jax.ShapeDtypeStruct((channels, channels), F32),
        ],
        name="finish",
    )(bit, mine, other)


def exchange(facing):
    got = [None] * 4
    for axis, low, high in (("face", 0, 2), ("tile", 3, 1)):
        count = lax.axis_size(axis)
        up = [(i, (i + 1) % count) for i in range(count)]
        down = [(target, source) for source, target in up]
        got[low] = lax.ppermute(facing[high], axis, up)
        got[high] = lax.ppermute(facing[low], axis, down)
    return got


def swap(value, mask):
    devices = lax.axis_size("face") * lax.axis_size("tile")
    return lax.ppermute(value, ("face", "tile"), [(i, i ^ mask) for i in range(devices)])


def after(value, *others):
    return lax.optimization_barrier((value, *others))[0]


def shards(
    state, cotangent, depth_weight, depth_bias, point_weight, tile_links, link_sides, link_flips, corner_masks
):
    batch, side, cols, channels = state.shape
    face_count = lax.axis_size("face")
    tile_count = lax.axis_size("tile")
    face_pos = lax.axis_index("face")
    tile_pos = lax.axis_index("tile")
    toward = jnp.stack(
        [
            (face_pos - 1) % face_count * tile_count + tile_pos,
            face_pos * tile_count + (tile_pos + 1) % tile_count,
            (face_pos + 1) % face_count * tile_count + tile_pos,
            face_pos * tile_count + (tile_pos - 1) % tile_count,
        ]
    )
    matched = tile_links[0][:, None] == toward[None, :]
    counter = jnp.arange(4, dtype=jnp.int32)
    dir_of_side = jnp.sum(jnp.where(matched, counter[None, :], 0), axis=1)
    side_of_dir = jnp.sum(jnp.where(matched, counter[:, None], 0), axis=0)
    table = jnp.concatenate([dir_of_side, side_of_dir, link_flips[0], corner_masks[0]])
    bias = depth_bias.reshape(1, channels)
    got = exchange(edges_call(table, state))
    grad, point_inner, depth_inner = inner_call(state, cotangent, point_weight, depth_weight, bias)
    ring, *facing, part = ring_call(
        table, state, cotangent, got, point_weight, depth_weight, bias, point_inner, depth_inner
    )
    incoming = exchange(facing)

    core = tile_pos % 2
    half = part.shape[0] // 2
    low, high = part[:half], part[half:]
    mine = jnp.where(core == 0, low, high)
    sent = jnp.where(core == 0, high, low)
    first, field_grad = 0, None
    for stage, (mask_bits, steps) in enumerate(
        ((1, 0), (2, 2), (6, 3), (8, 2), (24, 3), (32, 2), (96, 2), (1, 2))
    ):
        got = swap(sent if stage == 0 else mine, mask_bits)
        if steps:
            held = after(depth_weight, mine)
            field_grad, token = spread_call(first, steps, table, grad, ring, incoming, held, field_grad)
            got = after(got, token)
            first += steps
        if stage < 7:
            mine = mine + got
    scale = float(batch * side * cols * face_count * tile_count) ** -0.5
    depth_grad, bias_grad, point_grad = finish_call(scale, core.reshape(1), mine, got)
    return field_grad, depth_grad, bias_grad.reshape(channels), point_grad


def solution(mesh):
    tiles = P(None, "face", "tile", None)
    table = P(("face", "tile"), None)
    return jax.shard_map(
        shards,
        mesh=mesh,
        in_specs=(tiles, tiles, P(), P(), P(), table, table, table, table),
        out_specs=(tiles, P(), P(), P()),
        check_vma=False,
    )
```

```python
import functools

import jax
import jax.numpy as jnp
from jax import lax
from jax.experimental import pallas as pl
from jax.experimental.pallas import tpu as pltpu
from jax.sharding import PartitionSpec as P

ROOT = 0.7978845608028654
CUBIC = 0.044715
F32 = jnp.float32
BF16 = jnp.bfloat16
LANES = 128
SUB = 8
PAD = 8


def gelu_pair(h):
    h2 = h * h
    s = 0.5 * jnp.tanh(h * ((CUBIC * ROOT) * h2 + ROOT)) + 0.5
    act = h * s
    slope = s + act * (1.0 - s) * ((6.0 * CUBIC * ROOT) * h2 + 2.0 * ROOT)
    return act, slope


ALPHA = (CUBIC * ROOT) ** (1.0 / 3.0)
KAPPA = ROOT / ALPHA


def gelu_scaled(h):
    h2 = h * h
    t = jnp.tanh(h * (h2 + KAPPA))
    up = 1.0 + t
    act = h * up
    return act, up + act * (1.0 - t) * (3.0 * h2 + KAPPA)


def tap_at(ref, hf, k):
    return jnp.broadcast_to(ref[k : k + 1, hf * LANES : hf * LANES + LANES], (SUB, LANES))


def inner_body(pairs, carried, x_ref, cot_ref, w_ref, tap_ref, bias_ref, gh_ref, outs, u, hide, acc, half_w, pg_ref, *bufs):
    step = pl.program_id(0)
    side = x_ref.shape[1]
    cols = x_ref.shape[2]
    sets = (bufs[0:4], bufs[4:8])

    @pl.when(step == 0)
    def _():
        for hf in range(2):
            for c in range(3):
                w0, w1, w2 = (tap_at(tap_ref, hf, 3 * r + c) * ALPHA for r in range(3))
                u[hf, c] = w0
                u[hf, 3 + c] = (w0 + w1 + w2) * 0.5
                u[hf, 6 + c] = (w0 - w1 + w2) * 0.5
                u[hf, 9 + c] = w2
            u[hf, 12] = tap_at(bias_ref, hf, 0) * ALPHA
        half_w[...] = w_ref[...] * jnp.asarray(0.5, BF16)
        for qt, _, _, _ in sets:
            edge = jnp.zeros((2, pairs, 4, PAD, LANES), F32)
            qt[:, :, :, 0:PAD, :] = edge
            qt[:, :, :, PAD + cols :, :] = edge
        col = lax.broadcasted_iota(jnp.int32, (cols, 2 * LANES), 0)
        keep = jnp.logical_and(col > 0, col < cols - 1)
        hide[0] = jnp.where(keep, 1.0, 0.0).astype(BF16)
        hide[1] = jnp.zeros((cols, 2 * LANES), BF16)
        acc[...] = jnp.zeros_like(acc)
        pg_ref[...] = jnp.zeros_like(pg_ref)

    rows = 2 * pairs

    def outer(buf):
        _, _, act, cot = buf
        pg_ref[...] += lax.dot_general(
            act[...], cot[...], (((0,), (0,)), ((), ())), preferred_element_type=F32
        )

    def chunk(t, buf):
        qt, ga, act, cot = buf
        base = t * rows
        for q in range(rows):
            i = base + q
            kind = jnp.where(jnp.logical_or(i == 0, i == side - 1), 1, 0)
            cot[q * cols : q * cols + cols, :] = cot_ref[0, i] * hide[kind]
        g = lax.dot_general(cot[...], half_w[...], (((1,), (1,)), ((), ())), preferred_element_type=F32)
        ga[0] = g[:, :LANES]
        ga[1] = g[:, LANES:]
        for hf in range(2):
            lanes = slice(hf * LANES, hf * LANES + LANES)
            line = [x_ref[0, jnp.maximum(base - 1, 0), :, lanes].astype(F32)]
            for q in range(rows):
                line.append(x_ref[0, base + q, :, lanes].astype(F32))
            line.append(x_ref[0, jnp.minimum(base + rows, side - 1), :, lanes].astype(F32))
            for p in range(pairs):
                q0, q1, q2, q3 = line[2 * p : 2 * p + 4]
                for k, v in enumerate((q0 - q2, q1 + q2, q2 - q1, q1 - q3)):
                    qt[hf, p, k, PAD : PAD + cols, :] = v
        for hf in range(2):
            lanes = slice(hf * LANES, hf * LANES + LANES)
            sums = [acc[hf, k] for k in range(13)]
            for p in range(pairs):
                for jb in range(cols // 16):
                    halves = []
                    for half in range(2):
                        j = jb * 16 + half * SUB
                        win = [
                            [qt[hf, p, k, PAD - 1 + j + c : PAD - 1 + j + c + SUB, :] for c in range(3)]
                            for k in range(4)
                        ]
                        m = []
                        for k in range(4):
                            v = u[hf, 3 * k] * win[k][0]
                            v = v + u[hf, 3 * k + 1] * win[k][1]
                            m.append(v + u[hf, 3 * k + 2] * win[k][2])
                        both = m[1] + u[hf, 12]
                        found = []
                        for q, h in enumerate((both + m[0] + m[2], both - m[2] - m[3])):
                            a, slope = gelu_scaled(h)
                            at = (2 * p + q) * cols + j
                            found.append((a, ga[hf, at : at + SUB, :] * slope))
                        g0, g1 = found[0][1], found[1][1]
                        plus, minus = g0 + g1, g0 - g1
                        for k, v in enumerate((g0, plus, minus, g1)):
                            for c in range(3):
                                sums[3 * k + c] = sums[3 * k + c] + v * win[k][c]
                        sums[12] = sums[12] + plus
                        halves.append(found)
                    for q in range(2):
                        at = (2 * p + q) * cols + jb * 16
                        act[at : at + 16, lanes] = jnp.concatenate(
                            [halves[0][q][0], halves[1][q][0]], axis=0
                        ).astype(BF16)
                        gh_ref[0, base + 2 * p + q, jb * 16 : jb * 16 + 16, lanes] = jnp.concatenate(
                            [halves[0][q][1], halves[1][q][1]], axis=0
                        ).astype(BF16)
            for k in range(13):
                acc[hf, k] = sums[k]

    def body(t, carry):
        chunk(2 * t, sets[0])
        outer(sets[1])
        chunk(2 * t + 1, sets[1])
        outer(sets[0])
        return carry

    sets[1][2][...] = jnp.zeros_like(sets[1][2])
    sets[1][3][...] = jnp.zeros_like(sets[1][3])
    lax.fori_loop(0, side // (2 * rows), body, 0)
    outer(sets[1])

    def tap_sums(hf):
        lines = [None] * 10
        for c in range(3):
            d1, d2, d3, d4 = (acc[hf, 3 * k + c] for k in range(4))
            even = 0.5 * (d2 + d3)
            lines[c] = d1 + even
            lines[3 + c] = 0.5 * (d2 - d3)
            lines[6 + c] = even - d4
        lines[9] = acc[hf, 12]
        return lines

    @pl.when(step == pl.num_programs(0) - 1)
    def _():
        point = pg_ref[...] * (0.5 / ALPHA)
        if carried is None:
            pg_out, dg_out = outs
            pg_out[...] = point
            for hf in range(2):
                for k, line in enumerate(tap_sums(hf)):
                    dg_out[hf, k] = line
            return
        table, _, pg_in, dg_in = carried
        mine, sent = outs
        rows = mine.shape[0]
        lines = []
        for hf in range(2):
            own = [jnp.sum(v + dg_in[hf, k], axis=0, keepdims=True) for k, v in enumerate(tap_sums(hf))]
            lines.append(jnp.concatenate(own + [jnp.zeros((6, LANES), F32)], axis=0))
        point = point + pg_in[...]
        low = point[:rows]
        high = jnp.concatenate([point[rows:], jnp.concatenate(lines, axis=1)], axis=0)
        first = table[CORE] == 0
        mine[...] = jnp.where(first, low, high)
        sent[...] = jnp.where(first, high, low)


PAIRS = 4


def inner_call(first, count, state, cotangent, weight, taps, bias, carried=None):
    batch, side, cols, channels = state.shape
    tile = pl.BlockSpec((1, side, cols, channels), lambda b: (b + first, 0, 0, 0))
    whole = lambda *shape: pl.BlockSpec(shape, lambda b: (0,) * len(shape))
    buf = [
        pltpu.VMEM((2, PAIRS, 4, cols + 2 * PAD, LANES), F32),
        pltpu.VMEM((2, 2 * PAIRS * cols, LANES), F32),
        pltpu.VMEM((2 * PAIRS * cols, channels), BF16),
        pltpu.VMEM((2 * PAIRS * cols, channels), BF16),
    ]
    square, lines, half = (channels, channels), (2, 10, SUB, LANES), ((channels + 16) // 2, channels)
    in_specs = [tile, tile, whole(*square), whole(9, channels), whole(1, channels)]
    operands = [state, cotangent, weight, taps, bias]
    shapes, aliases = (square, lines), {}
    if carried is not None:
        in_specs += [pl.BlockSpec(memory_space=pltpu.SMEM), pl.BlockSpec(memory_space=pl.ANY), whole(*square), whole(*lines)]
        operands += carried
        shapes, aliases = (half, half), {6: 0}
    given = len(operands)

    def body(*refs):
        extra = None if carried is None else refs[5:given]
        inner_body(PAIRS, extra, *refs[:5], refs[given], refs[given + 1 : given + 3], *refs[given + 3 :])

    return pl.pallas_call(
        body,
        grid=(count,),
        in_specs=in_specs,
        out_specs=[tile, *(whole(*shape) for shape in shapes)],
        out_shape=[
            jax.ShapeDtypeStruct(state.shape, BF16),
            *(jax.ShapeDtypeStruct(shape, F32) for shape in shapes),
        ],
        scratch_shapes=[
            pltpu.VMEM((2, 13, SUB, LANES), F32),
            pltpu.VMEM((2, cols, channels), BF16),
            pltpu.VMEM((2, 13, SUB, LANES), F32),
            pltpu.VMEM(square, BF16),
            pltpu.VMEM(square, F32),
            *buf,
            *buf,
        ],
        input_output_aliases=aliases,
        compiler_params=pltpu.CompilerParams(vmem_limit_bytes=57 << 20),
        cost_estimate=pl.CostEstimate(
            flops=10_000_000_000 * count, bytes_accessed=state.size * 6 * count // batch, transcendentals=state.size
        ),
        name="inner",
    )(*operands)


DIR_OF_SIDE, SIDE_OF_DIR, FLIPS, MASKS, CORE = 0, 4, 8, 12, 16


def from_dir(table, got, s):
    d = table[DIR_OF_SIDE + s]
    rows = got[3][0]
    for k in range(3):
        rows = jnp.where(d == k, got[k][0], rows)
    return rows


def turn(table, s, rows):
    count = rows.shape[0]
    i = lax.broadcasted_iota(jnp.int32, (count, count), 0)
    j = lax.broadcasted_iota(jnp.int32, (count, count), 1)
    source = jnp.where(table[FLIPS + s] == 1, count - 1 - i, i)
    pick = jnp.where(j == source, 1.0, 0.0).astype(BF16)
    return jnp.dot(pick, rows, preferred_element_type=F32).astype(BF16)


def edges_body(sizes, where, links, flips, masks, top_ref, low_ref, left_ref, right_ref, to0, to1, to2, to3, table, turned):
    faces, tiles = sizes

    @pl.when(pl.program_id(0) == 0)
    def _():
        face, tile = where[0], where[1]
        towards = (
            lax.rem(face + faces - 1, faces) * tiles + tile,
            face * tiles + lax.rem(tile + 1, tiles),
            lax.rem(face + 1, faces) * tiles + tile,
            face * tiles + lax.rem(tile + tiles - 1, tiles),
        )
        met = [[jnp.where(links[0, s] == to, 1, 0) for to in towards] for s in range(4)]
        for k in range(4):
            table[DIR_OF_SIDE + k] = met[k][1] + 2 * met[k][2] + 3 * met[k][3]
            table[SIDE_OF_DIR + k] = met[1][k] + 2 * met[2][k] + 3 * met[3][k]
            table[FLIPS + k] = flips[0, k]
            table[MASKS + k] = masks[0, k]
        table[CORE] = lax.rem(tile, 2)

    last = right_ref.shape[2] - 1
    turned[0] = turn(table, 0, top_ref[0, 0])
    turned[1] = turn(table, 1, right_ref[0].astype(F32)[:, last].astype(BF16))
    turned[2] = turn(table, 2, low_ref[0, 0])
    turned[3] = turn(table, 3, left_ref[0].astype(F32)[:, 0].astype(BF16))
    for d, to in enumerate((to0, to1, to2, to3)):
        to[0] = turned[table[SIDE_OF_DIR + d]]


def edges_call(where, links, flips, masks, state):
    batch, side, cols, channels = state.shape
    wide = 8
    one = lambda at: pl.BlockSpec((1, 1, cols, channels), lambda b: (b, at, 0, 0))
    column = lambda at: pl.BlockSpec((1, side, wide, channels), lambda b: (b, 0, at, 0))
    facing = pl.BlockSpec((1, side, channels), lambda b: (b, 0, 0))
    return pl.pallas_call(
        functools.partial(edges_body, (lax.axis_size("face"), lax.axis_size("tile"))),
        grid=(batch,),
        in_specs=[
            *[pl.BlockSpec(memory_space=pltpu.SMEM)] * 4,
            one(0),
            one(side - 1),
            column(0),
            column(cols // wide - 1),
        ],
        out_specs=[*[facing] * 4, pl.BlockSpec(memory_space=pltpu.SMEM)],
        out_shape=[
            *[jax.ShapeDtypeStruct((batch, side, channels), BF16)] * 4,
            jax.ShapeDtypeStruct((CORE + 1,), jnp.int32),
        ],
        scratch_shapes=[pltpu.VMEM((4, side, channels), BF16)],
        compiler_params=pltpu.CompilerParams(vmem_limit_bytes=57 << 20),
        name="edges",
    )(where, links, flips, masks, state, state, state, state)


LOW = (0, 1, 3, 0)
HIGH = (1, 2, 2, 3)


def ring_body(
    table, top_ref, low_ref, left_ref, right_ref, ctop_ref, clow_ref, cleft_ref, cright_ref,
    got0, got1, got2, got3, w_ref, tap_ref, bias_ref, pg_ref, dg_ref,
    gr_ref, to0, to1, to2, to3, point_ref, line_ref, strip, ext, acts, acc, turned,
):
    step = pl.program_id(0)
    side = got0.shape[1]
    got = (got0, got1, got2, got3)
    masks = [table[MASKS + k].astype(F32) for k in range(4)]

    @pl.when(step == 0)
    def _():
        acc[...] = dg_ref[...]
        point_ref[...] = pg_ref[...]
        ext[...] = jnp.zeros_like(ext)

    rims = [from_dir(table, got, s).astype(F32) for s in range(4)]
    top = top_ref[0].astype(F32)
    low = low_ref[0].astype(F32)
    left = left_ref[0].astype(F32)
    right = right_ref[0].astype(F32)
    last = left.shape[1] - 1
    end = side - 1

    def corner(k, first, second):
        return (masks[k] * 0.5 * (first + second)).astype(BF16).astype(F32)

    def at(s, i):
        return rims[s][i : i + 1]

    nw = corner(0, at(0, 0), at(3, 0))
    ne = corner(1, at(0, end), at(1, 0))
    se = corner(2, at(1, end), at(2, end))
    sw = corner(3, at(2, 0), at(3, end))
    lines = (
        ((rims[0], nw, ne), (top[0], at(3, 0), at(1, 0)), (top[1], at(3, 1), at(1, 1))),
        (
            (right[:, last - 1], at(0, end - 1), at(2, end - 1)),
            (right[:, last], at(0, end), at(2, end)),
            (rims[1], ne, se),
        ),
        (
            (low[0], at(3, end - 1), at(1, end - 1)),
            (low[1], at(3, end), at(1, end)),
            (rims[2], sw, se),
        ),
        ((rims[3], nw, sw), (left[:, 0], at(0, 0), at(2, 0)), (left[:, 1], at(0, 1), at(2, 1))),
    )
    for s in range(4):
        for a in range(3):
            line, before, after = lines[s][a]
            for hf in range(2):
                lanes = slice(hf * LANES, hf * LANES + LANES)
                strip[s, hf, a, PAD : PAD + side, :] = line[:, lanes]
                strip[s, hf, a, PAD - 1 : PAD, :] = before[:, lanes]
                strip[s, hf, a, PAD + side : PAD + side + 1, :] = after[:, lanes]
    cots = jnp.concatenate(
        [
            ctop_ref[0, 0].astype(F32),
            cright_ref[0].astype(F32)[:, last],
            clow_ref[0, 0].astype(F32),
            cleft_ref[0].astype(F32)[:, 0],
        ],
        axis=0,
    ).astype(BF16)
    ga = lax.dot_general(cots, w_ref[...], (((1,), (1,)), ((), ())), preferred_element_type=F32)
    row = lax.broadcasted_iota(jnp.int32, (side, LANES), 0)
    middle = jnp.logical_and(row > 0, row < end)
    for s in range(4):
        upright = s % 2 == 0
        rim_line = 0 if s in (0, 3) else 2
        for hf in range(2):
            lanes = slice(hf * LANES, hf * LANES + LANES)

            def tap(a, b):
                k = 3 * a + b if upright else 3 * b + a
                return k, tap_ref[k : k + 1, lanes]

            h = jnp.zeros((side, LANES), F32) + bias_ref[0:1, lanes]
            for a in range(3):
                for b in range(3):
                    h = h + tap(a, b)[1] * strip[s, hf, a, PAD - 1 + b : PAD - 1 + b + side, :]
            act, slope = gelu_pair(h)
            g = (ga[s * side : s * side + side, lanes] * slope).astype(BF16)
            gr_ref[s, 0, :, lanes] = g
            g = g.astype(F32)
            counted = g
            if not upright:
                counted = jnp.where(middle, g, 0.0)
                act = jnp.where(middle, act, 0.0)
            acts[s * side : s * side + side, lanes] = act.astype(BF16)
            for a in range(3):
                for b in range(3):
                    k = tap(a, b)[0]
                    term = counted * strip[s, hf, a, PAD - 1 + b : PAD - 1 + b + side, :]
                    acc[hf, k] += jnp.sum(term.reshape(side // SUB, SUB, LANES), axis=0)
            acc[hf, 9] += jnp.sum(counted.reshape(side // SUB, SUB, LANES), axis=0)
            ext[PAD : PAD + side, :] = g
            first, mid, final = (tap(rim_line, b)[1] for b in range(3))
            back = (
                first * ext[PAD + 1 : PAD + 1 + side, :]
                + mid * g
                + final * ext[PAD - 1 : PAD - 1 + side, :]
            )
            back = back + jnp.where(row == 0, (0.5 * masks[LOW[s]]) * first * g, 0.0)
            back = back + jnp.where(row == end, (0.5 * masks[HIGH[s]]) * final * g, 0.0)
            turned[s, :, lanes] = turn(table, s, back.astype(BF16))
    for d, to in enumerate((to0, to1, to2, to3)):
        to[0] = turned[table[SIDE_OF_DIR + d]]
    point_ref[...] += lax.dot_general(acts[...], cots, (((0,), (0,)), ((), ())), preferred_element_type=F32)

    @pl.when(step == pl.num_programs(0) - 1)
    def _():
        line_ref[...] = acc[...]


def ring_call(table, state, cotangent, got, weight, taps, bias, point_inner, depth_inner):
    batch, side, cols, channels = state.shape
    wide = 8
    two = lambda at: pl.BlockSpec((1, 2, cols, channels), lambda b: (b, at, 0, 0))
    one = lambda at: pl.BlockSpec((1, 1, cols, channels), lambda b: (b, at, 0, 0))
    column = lambda at: pl.BlockSpec((1, side, wide, channels), lambda b: (b, 0, at, 0))
    strips = pl.BlockSpec((4, 1, side, channels), lambda b: (0, b, 0, 0))
    facing = pl.BlockSpec((1, side, channels), lambda b: (b, 0, 0))
    far = cols // wide - 1
    return pl.pallas_call(
        ring_body,
        grid=(batch,),
        in_specs=[
            pl.BlockSpec(memory_space=pltpu.SMEM),
            two(0),
            two(side // 2 - 1),
            column(0),
            column(far),
            one(0),
            one(side - 1),
            column(0),
            column(far),
            *[facing] * 4,
            pl.BlockSpec((channels, channels), lambda b: (0, 0)),
            pl.BlockSpec((9, channels), lambda b: (0, 0)),
            pl.BlockSpec((1, channels), lambda b: (0, 0)),
            pl.BlockSpec((channels, channels), lambda b: (0, 0)),
            pl.BlockSpec((2, 10, SUB, LANES), lambda b: (0, 0, 0, 0)),
        ],
        out_specs=[
            strips,
            *[facing] * 4,
            pl.BlockSpec((channels, channels), lambda b: (0, 0)),
            pl.BlockSpec((2, 10, SUB, LANES), lambda b: (0, 0, 0, 0)),
        ],
        out_shape=[
            jax.ShapeDtypeStruct((4, batch, side, channels), BF16),
            *[jax.ShapeDtypeStruct((batch, side, channels), BF16)] * 4,
            jax.ShapeDtypeStruct((channels, channels), F32),
            jax.ShapeDtypeStruct((2, 10, SUB, LANES), F32),
        ],
        scratch_shapes=[
            pltpu.VMEM((4, 2, 3, cols + 2 * PAD, LANES), F32),
            pltpu.VMEM((cols + 2 * PAD, LANES), F32),
            pltpu.VMEM((4 * side, channels), BF16),
            pltpu.VMEM((2, 10, SUB, LANES), F32),
            pltpu.VMEM((4, side, channels), BF16),
        ],
        compiler_params=pltpu.CompilerParams(vmem_limit_bytes=57 << 20),
        cost_estimate=pl.CostEstimate(
            flops=3_000_000_000, bytes_accessed=12 << 20, transcendentals=state.size // 16
        ),
        name="ring",
    )(table, state, state, state, state, cotangent, cotangent, cotangent, cotangent, *got, weight, taps, bias,
      point_inner, depth_inner)


def spread_body(rows, first, table, gh_ref, above_ref, below_ref, gr_ref, got0, got1, got2, got3, tap_ref, out_ref, token_ref, gf, near, far, ring, back):
    got = (got0, got1, got2, got3)
    side = gr_ref.shape[2]
    cols = gh_ref.shape[2]
    count = gh_ref.shape[1]
    chunks = side // count
    step = (pl.program_id(0) + first) % chunks
    token_ref[...] = jnp.zeros_like(token_ref)
    start = step * count

    @pl.when(jnp.logical_or(pl.program_id(0) == 0, step == 0))
    def _():
        for k, s in enumerate((1, 3)):
            back[k] = from_dir(table, got, s)
        for hf in range(2):
            lanes = slice(hf * LANES, hf * LANES + LANES)
            gf[hf, :, 0:PAD, :] = jnp.zeros((count + 2, PAD, LANES), F32)
            gf[hf, :, PAD + cols : 2 * PAD + cols, :] = jnp.zeros((count + 2, PAD, LANES), F32)
            for k, s in enumerate((1, 3)):
                ring[k, hf, 0:PAD, :] = jnp.zeros((PAD, LANES), F32)
                ring[k, hf, PAD + side :, :] = jnp.zeros((PAD, LANES), F32)
                ring[k, hf, PAD : PAD + side, :] = gr_ref[s, 0, :, lanes].astype(F32)
        near[...] = jnp.zeros_like(near)
        far[...] = jnp.zeros_like(far)

    def put(i, v):
        v = v.astype(F32)
        gf[0, i, PAD : PAD + cols, :] = v[:, :LANES]
        gf[1, i, PAD : PAD + cols, :] = v[:, LANES:]

    put(0, jnp.where(step > 0, above_ref[0, 0], jnp.zeros_like(above_ref[0, 0])))
    put(count + 1, jnp.where(step < chunks - 1, below_ref[0, 0], jnp.zeros_like(below_ref[0, 0])))
    for i in range(count):
        put(i + 1, gh_ref[0, i])
    cut = [back[k, pl.ds(pl.multiple_of(start, count), count), :].astype(F32) for k in range(2)]
    for hf in range(2):
        lanes = slice(hf * LANES, hf * LANES + LANES)
        for k, j in ((0, PAD + cols - 1), (1, PAD)):
            own = ring[k, hf, pl.ds(pl.multiple_of(PAD + start, SUB), count), :]
            gf[hf, 1 : count + 1, j : j + 1, :] = own.reshape(count, 1, LANES)
            gf[hf, 0, j : j + 1, :] = ring[k, hf, pl.ds(PAD + start - 1, 1), :]
            gf[hf, count + 1, j : j + 1, :] = ring[k, hf, pl.ds(PAD + start + count, 1), :]
        near[hf, :, 0:1, :] = cut[1][:, lanes].reshape(count, 1, LANES)
        far[hf, :, SUB - 1 : SUB, :] = cut[0][:, lanes].reshape(count, 1, LANES)

    def line(i, s):
        v = gr_ref[s, 0].astype(F32)
        for hf in range(2):
            gf[hf, i, PAD : PAD + cols, :] = v[:, hf * LANES : hf * LANES + LANES]

    @pl.when(step == 0)
    def _():
        line(1, 0)

    @pl.when(step == chunks - 1)
    def _():
        line(count, 2)

    for hf in range(2):
        lanes = slice(hf * LANES, hf * LANES + LANES)
        taps = [tap_at(tap_ref, hf, k) for k in range(9)]
        for jb in range(cols // 16):

            def body(it, carry):
                i = it * rows
                win = {}
                for q in range(rows):
                    pair = []
                    for half in range(2):
                        j = PAD + jb * 16 + half * SUB
                        total = None
                        for r in range(3):
                            for c in range(3):
                                at = (q + 2 - r, 2 - c, half)
                                if at not in win:
                                    win[at] = gf[hf, i + at[0], j - 1 + at[1] : j - 1 + at[1] + SUB, :]
                                term = taps[3 * r + c] * win[at]
                                total = term if total is None else total + term
                        if jb == 0 and half == 0:
                            total = total + near[hf, i + q]
                        if jb == cols // 16 - 1 and half == 1:
                            total = total + far[hf, i + q]
                        pair.append(total)
                    out_ref[0, i + q, jb * 16 : jb * 16 + 16, lanes] = jnp.concatenate(pair, axis=0).astype(BF16)
                return carry

            lax.fori_loop(0, count // rows, body, 0)

    def add(i, s):
        out_ref[0, i] = (out_ref[0, i].astype(F32) + from_dir(table, got, s).astype(F32)).astype(BF16)

    @pl.when(step == 0)
    def _():
        add(0, 0)

    @pl.when(step == chunks - 1)
    def _():
        add(count - 1, 2)


CHUNK = 16


def spread_call(first, steps, table, grad, ring, got, taps, into):
    batch, side, cols, channels = grad.shape
    chunks = side // CHUNK
    high = side - 1
    at = lambda i: ((i + first) // chunks, (i + first) % chunks)
    strips = pl.BlockSpec((4, 1, side, channels), lambda i: (0, at(i)[0], 0, 0))
    facing = pl.BlockSpec((1, side, channels), lambda i: (at(i)[0], 0, 0))
    rows = pl.BlockSpec((1, CHUNK, cols, channels), lambda i: (*at(i), 0, 0))
    in_specs = [
        pl.BlockSpec(memory_space=pltpu.SMEM),
        rows,
        pl.BlockSpec((1, 1, cols, channels), lambda i: (at(i)[0], jnp.maximum(at(i)[1] * CHUNK - 1, 0), 0, 0)),
        pl.BlockSpec((1, 1, cols, channels), lambda i: (at(i)[0], jnp.minimum(at(i)[1] * CHUNK + CHUNK, high), 0, 0)),
        strips,
        *[facing] * 4,
        pl.BlockSpec((9, channels), lambda i: (0, 0)),
    ]
    operands = [table, grad, grad, grad, ring, *got, taps]
    aliases = {}
    if into is not None:
        aliases = {len(operands): 0}
        in_specs.append(pl.BlockSpec(memory_space=pl.ANY))
        operands.append(into)

    def body(*refs):
        spread_body(4, first, *refs[:10], *refs[len(operands) :])

    return pl.pallas_call(
        body,
        grid=(steps,),
        in_specs=in_specs,
        out_specs=[rows, pl.BlockSpec((SUB, LANES), lambda i: (0, 0))],
        out_shape=[jax.ShapeDtypeStruct(grad.shape, BF16), jax.ShapeDtypeStruct((SUB, LANES), F32)],
        scratch_shapes=[
            pltpu.VMEM((2, CHUNK + 2, cols + 2 * PAD, LANES), F32),
            pltpu.VMEM((2, CHUNK, SUB, LANES), F32),
            pltpu.VMEM((2, CHUNK, SUB, LANES), F32),
            pltpu.VMEM((2, 2, side + 2 * PAD, LANES), F32),
            pltpu.VMEM((2, side, channels), BF16),
        ],
        input_output_aliases=aliases,
        compiler_params=pltpu.CompilerParams(vmem_limit_bytes=57 << 20),
        cost_estimate=pl.CostEstimate(
            flops=750_000_000 * steps, bytes_accessed=grad.size * 4 * steps // (batch * chunks), transcendentals=0
        ),
        name="spread",
    )(*operands)


def finish_body(scale, table, mine_ref, other_ref, dg_ref, bg_ref, pg_ref):
    rows = mine_ref.shape[0]
    channels = pg_ref.shape[0]
    own = mine_ref[...] * scale
    far = other_ref[...] * scale
    first = table[CORE] == 0
    low = jnp.where(first, own, far)
    high = jnp.where(first, far, own)
    pg_ref[0:rows, :] = low
    pg_ref[rows:channels, :] = high[: channels - rows]
    tail = high[channels - rows :]
    dg_ref[...] = tail[0:9]
    bg_ref[...] = tail[9:10]


def finish_call(scale, bit, mine, other):
    channels = mine.shape[1]
    vmem = pl.BlockSpec(memory_space=pltpu.VMEM)
    return pl.pallas_call(
        functools.partial(finish_body, scale),
        in_specs=[pl.BlockSpec(memory_space=pltpu.SMEM), vmem, vmem],
        out_specs=[vmem, vmem, vmem],
        out_shape=[
            jax.ShapeDtypeStruct((9, channels), F32),
            jax.ShapeDtypeStruct((1, channels), F32),
            jax.ShapeDtypeStruct((channels, channels), F32),
        ],
        name="finish",
    )(bit, mine, other)


def exchange(facing):
    got = [None] * 4
    for axis, low, high in (("face", 0, 2), ("tile", 3, 1)):
        count = lax.axis_size(axis)
        up = [(i, (i + 1) % count) for i in range(count)]
        down = [(target, source) for source, target in up]
        got[low] = lax.ppermute(facing[high], axis, up)
        got[high] = lax.ppermute(facing[low], axis, down)
    return got


def swap(value, mask):
    devices = lax.axis_size("face") * lax.axis_size("tile")
    return lax.ppermute(value, ("face", "tile"), [(i, i ^ mask) for i in range(devices)])


def after(value, *others):
    return lax.optimization_barrier((value, *others))[0]


def shards(
    state, cotangent, depth_weight, depth_bias, point_weight, tile_links, link_sides, link_flips, corner_masks
):
    batch, side, cols, channels = state.shape
    face_count = lax.axis_size("face")
    tile_count = lax.axis_size("tile")
    face_pos = lax.axis_index("face")
    tile_pos = lax.axis_index("tile")
    where = jnp.stack([face_pos, tile_pos])
    bias = depth_bias.reshape(1, channels)
    *edges, table = edges_call(where, tile_links, link_flips, corner_masks, state)
    got = exchange(edges)
    layer = (point_weight, depth_weight, bias)
    early = batch // 2
    grad, point_sum, depth_sum = inner_call(0, early, state, cotangent, *layer)
    ring, *facing, point_sum, depth_sum = ring_call(table, state, cotangent, got, *layer, point_sum, depth_sum)
    incoming = exchange(facing)
    grad, mine, sent = inner_call(
        early, batch - early, state, cotangent, *layer, (table, grad, point_sum, depth_sum)
    )

    first, field_grad = 0, None
    for stage, (mask_bits, steps) in enumerate(
        ((1, 2), (2, 2), (6, 2), (8, 2), (24, 2), (32, 2), (96, 2), (1, 2))
    ):
        got = swap(sent if stage == 0 else mine, mask_bits)
        if steps:
            held = after(depth_weight, mine if stage else sent)
            field_grad, token = spread_call(first, steps, table, grad, ring, incoming, held, field_grad)
            got = after(got, token)
            first += steps
        if stage < 7:
            mine = mine + got
    scale = float(batch * side * cols * face_count * tile_count) ** -0.5
    depth_grad, bias_grad, point_grad = finish_call(scale, table, mine, got)
    return field_grad, depth_grad, bias_grad.reshape(channels), point_grad


def solution(mesh):
    tiles = P(None, "face", "tile", None)
    table = P(("face", "tile"), None)
    return jax.shard_map(
        shards,
        mesh=mesh,
        in_specs=(tiles, tiles, P(), P(), P(), table, table, table, table),
        out_specs=(tiles, P(), P(), P()),
        check_vma=False,
    )
```

```python
import functools

import jax
import jax.numpy as jnp
from jax import lax
from jax.experimental import pallas as pl
from jax.experimental.pallas import tpu as pltpu
from jax.sharding import PartitionSpec as P

ROOT = 0.7978845608028654
CUBIC = 0.044715
F32 = jnp.float32
BF16 = jnp.bfloat16
LANES = 128
SUB = 8
PAD = 8


def gelu_pair(h):
    h2 = h * h
    s = 0.5 * jnp.tanh(h * ((CUBIC * ROOT) * h2 + ROOT)) + 0.5
    act = h * s
    slope = s + act * (1.0 - s) * ((6.0 * CUBIC * ROOT) * h2 + 2.0 * ROOT)
    return act, slope


ALPHA = (CUBIC * ROOT) ** (1.0 / 3.0)
KAPPA = ROOT / ALPHA


def gelu_scaled(h):
    h2 = h * h
    t = jnp.tanh(h * (h2 + KAPPA))
    up = 1.0 + t
    act = h * up
    return act, up + act * (1.0 - t) * (3.0 * h2 + KAPPA)


def tap_at(ref, hf, k):
    return jnp.broadcast_to(ref[k : k + 1, hf * LANES : hf * LANES + LANES], (SUB, LANES))


def inner_body(pairs, carried, x_ref, cot_ref, w_ref, tap_ref, bias_ref, gh_ref, outs, u, hide, acc, half_w, pg_ref, *bufs):
    step = pl.program_id(0)
    side = x_ref.shape[1]
    cols = x_ref.shape[2]
    sets = (bufs[0:4], bufs[4:8])

    @pl.when(step == 0)
    def _():
        for hf in range(2):
            for c in range(3):
                w0, w1, w2 = (tap_at(tap_ref, hf, 3 * r + c) * ALPHA for r in range(3))
                u[hf, c] = w0
                u[hf, 3 + c] = (w0 + w1 + w2) * 0.5
                u[hf, 6 + c] = (w0 - w1 + w2) * 0.5
                u[hf, 9 + c] = w2
            u[hf, 12] = tap_at(bias_ref, hf, 0) * ALPHA
        half_w[...] = w_ref[...] * jnp.asarray(0.5, BF16)
        for qt, _, _, _ in sets:
            edge = jnp.zeros((2, pairs, 4, PAD, LANES), F32)
            qt[:, :, :, 0:PAD, :] = edge
            qt[:, :, :, PAD + cols :, :] = edge
        col = lax.broadcasted_iota(jnp.int32, (cols, 2 * LANES), 0)
        keep = jnp.logical_and(col > 0, col < cols - 1)
        hide[0] = jnp.where(keep, 1.0, 0.0).astype(BF16)
        hide[1] = jnp.zeros((cols, 2 * LANES), BF16)
        acc[...] = jnp.zeros_like(acc)
        pg_ref[...] = jnp.zeros_like(pg_ref)

    rows = 2 * pairs

    def outer(buf):
        _, _, act, cot = buf
        pg_ref[...] += lax.dot_general(
            act[...], cot[...], (((0,), (0,)), ((), ())), preferred_element_type=F32
        )

    def chunk(t, buf):
        qt, ga, act, cot = buf
        base = t * rows
        for q in range(rows):
            i = base + q
            kind = jnp.where(jnp.logical_or(i == 0, i == side - 1), 1, 0)
            cot[q * cols : q * cols + cols, :] = cot_ref[0, i] * hide[kind]
        g = lax.dot_general(cot[...], half_w[...], (((1,), (1,)), ((), ())), preferred_element_type=F32)
        ga[0] = g[:, :LANES]
        ga[1] = g[:, LANES:]
        for hf in range(2):
            lanes = slice(hf * LANES, hf * LANES + LANES)
            line = [x_ref[0, jnp.maximum(base - 1, 0), :, lanes].astype(F32)]
            for q in range(rows):
                line.append(x_ref[0, base + q, :, lanes].astype(F32))
            line.append(x_ref[0, jnp.minimum(base + rows, side - 1), :, lanes].astype(F32))
            for p in range(pairs):
                q0, q1, q2, q3 = line[2 * p : 2 * p + 4]
                for k, v in enumerate((q0 - q2, q1 + q2, q2 - q1, q1 - q3)):
                    qt[hf, p, k, PAD : PAD + cols, :] = v
        for hf in range(2):
            lanes = slice(hf * LANES, hf * LANES + LANES)
            sums = [acc[hf, k] for k in range(13)]
            for p in range(pairs):
                for jb in range(cols // 16):
                    halves = []
                    for half in range(2):
                        j = jb * 16 + half * SUB
                        win = [
                            [qt[hf, p, k, PAD - 1 + j + c : PAD - 1 + j + c + SUB, :] for c in range(3)]
                            for k in range(4)
                        ]
                        m = []
                        for k in range(4):
                            v = u[hf, 3 * k] * win[k][0]
                            v = v + u[hf, 3 * k + 1] * win[k][1]
                            m.append(v + u[hf, 3 * k + 2] * win[k][2])
                        both = m[1] + u[hf, 12]
                        found = []
                        for q, h in enumerate((both + m[0] + m[2], both - m[2] - m[3])):
                            a, slope = gelu_scaled(h)
                            at = (2 * p + q) * cols + j
                            found.append((a, ga[hf, at : at + SUB, :] * slope))
                        g0, g1 = found[0][1], found[1][1]
                        plus, minus = g0 + g1, g0 - g1
                        for k, v in enumerate((g0, plus, minus, g1)):
                            for c in range(3):
                                sums[3 * k + c] = sums[3 * k + c] + v * win[k][c]
                        sums[12] = sums[12] + plus
                        halves.append(found)
                    for q in range(2):
                        at = (2 * p + q) * cols + jb * 16
                        act[at : at + 16, lanes] = jnp.concatenate(
                            [halves[0][q][0], halves[1][q][0]], axis=0
                        ).astype(BF16)
                        gh_ref[0, base + 2 * p + q, jb * 16 : jb * 16 + 16, lanes] = jnp.concatenate(
                            [halves[0][q][1], halves[1][q][1]], axis=0
                        ).astype(BF16)
            for k in range(13):
                acc[hf, k] = sums[k]

    def body(t, carry):
        chunk(2 * t, sets[0])
        outer(sets[1])
        chunk(2 * t + 1, sets[1])
        outer(sets[0])
        return carry

    sets[1][2][...] = jnp.zeros_like(sets[1][2])
    sets[1][3][...] = jnp.zeros_like(sets[1][3])
    lax.fori_loop(0, side // (2 * rows), body, 0)
    outer(sets[1])

    def tap_sums(hf):
        lines = [None] * 10
        for c in range(3):
            d1, d2, d3, d4 = (acc[hf, 3 * k + c] for k in range(4))
            even = 0.5 * (d2 + d3)
            lines[c] = d1 + even
            lines[3 + c] = 0.5 * (d2 - d3)
            lines[6 + c] = even - d4
        lines[9] = acc[hf, 12]
        return lines

    @pl.when(step == pl.num_programs(0) - 1)
    def _():
        point = pg_ref[...] * (0.5 / ALPHA)
        if carried is None:
            pg_out, dg_out = outs
            pg_out[...] = point
            for hf in range(2):
                for k, line in enumerate(tap_sums(hf)):
                    dg_out[hf, k] = line
            return
        table, _, pg_in, dg_in = carried
        mine, sent = outs
        rows = mine.shape[0]
        lines = []
        for hf in range(2):
            own = [jnp.sum(v + dg_in[hf, k], axis=0, keepdims=True) for k, v in enumerate(tap_sums(hf))]
            lines.append(jnp.concatenate(own + [jnp.zeros((6, LANES), F32)], axis=0))
        point = point + pg_in[...]
        low = point[:rows]
        high = jnp.concatenate([point[rows:], jnp.concatenate(lines, axis=1)], axis=0)
        first = table[CORE] == 0
        mine[...] = jnp.where(first, low, high)
        sent[...] = jnp.where(first, high, low)


PAIRS = 4


def inner_call(first, count, state, cotangent, weight, taps, bias, carried=None):
    batch, side, cols, channels = state.shape
    tile = pl.BlockSpec((1, side, cols, channels), lambda b: (b + first, 0, 0, 0))
    whole = lambda *shape: pl.BlockSpec(shape, lambda b: (0,) * len(shape))
    buf = [
        pltpu.VMEM((2, PAIRS, 4, cols + 2 * PAD, LANES), F32),
        pltpu.VMEM((2, 2 * PAIRS * cols, LANES), F32),
        pltpu.VMEM((2 * PAIRS * cols, channels), BF16),
        pltpu.VMEM((2 * PAIRS * cols, channels), BF16),
    ]
    square, lines, half = (channels, channels), (2, 10, SUB, LANES), ((channels + 16) // 2, channels)
    in_specs = [tile, tile, whole(*square), whole(9, channels), whole(1, channels)]
    operands = [state, cotangent, weight, taps, bias]
    shapes, aliases = (square, lines), {}
    if carried is not None:
        in_specs += [pl.BlockSpec(memory_space=pltpu.SMEM), pl.BlockSpec(memory_space=pl.ANY), whole(*square), whole(*lines)]
        operands += carried
        shapes, aliases = (half, half), {6: 0}
    given = len(operands)

    def body(*refs):
        extra = None if carried is None else refs[5:given]
        inner_body(PAIRS, extra, *refs[:5], refs[given], refs[given + 1 : given + 3], *refs[given + 3 :])

    return pl.pallas_call(
        body,
        grid=(count,),
        in_specs=in_specs,
        out_specs=[tile, *(whole(*shape) for shape in shapes)],
        out_shape=[
            jax.ShapeDtypeStruct(state.shape, BF16),
            *(jax.ShapeDtypeStruct(shape, F32) for shape in shapes),
        ],
        scratch_shapes=[
            pltpu.VMEM((2, 13, SUB, LANES), F32),
            pltpu.VMEM((2, cols, channels), BF16),
            pltpu.VMEM((2, 13, SUB, LANES), F32),
            pltpu.VMEM(square, BF16),
            pltpu.VMEM(square, F32),
            *buf,
            *buf,
        ],
        input_output_aliases=aliases,
        compiler_params=pltpu.CompilerParams(vmem_limit_bytes=57 << 20),
        cost_estimate=pl.CostEstimate(
            flops=10_000_000_000 * count, bytes_accessed=state.size * 6 * count // batch, transcendentals=state.size
        ),
        name="inner",
    )(*operands)


DIR_OF_SIDE, SIDE_OF_DIR, FLIPS, MASKS, CORE = 0, 4, 8, 12, 16


def from_dir(table, got, s):
    d = table[DIR_OF_SIDE + s]
    rows = got[3][0]
    for k in range(3):
        rows = jnp.where(d == k, got[k][0], rows)
    return rows


def turn(table, s, rows):
    count = rows.shape[0]
    i = lax.broadcasted_iota(jnp.int32, (count, count), 0)
    j = lax.broadcasted_iota(jnp.int32, (count, count), 1)
    source = jnp.where(table[FLIPS + s] == 1, count - 1 - i, i)
    pick = jnp.where(j == source, 1.0, 0.0).astype(BF16)
    return jnp.dot(pick, rows, preferred_element_type=F32).astype(BF16)


def edges_body(sizes, where, links, flips, masks, top_ref, low_ref, left_ref, right_ref, to0, to1, to2, to3, table, turned):
    faces, tiles = sizes

    @pl.when(pl.program_id(0) == 0)
    def _():
        face, tile = where[0], where[1]
        face_step = 1 - 2 * lax.rem(face, 2)
        tile_step = 1 - 2 * lax.rem(tile, 2)
        towards = (
            (face + face_step) * tiles + tile,
            lax.rem(face - face_step + faces, faces) * tiles + tile,
            face * tiles + tile + tile_step,
            face * tiles + lax.rem(tile - tile_step + tiles, tiles),
        )
        met = [[jnp.where(links[0, s] == to, 1, 0) for to in towards] for s in range(4)]
        for k in range(4):
            table[DIR_OF_SIDE + k] = met[k][1] + 2 * met[k][2] + 3 * met[k][3]
            table[SIDE_OF_DIR + k] = met[1][k] + 2 * met[2][k] + 3 * met[3][k]
            table[FLIPS + k] = flips[0, k]
            table[MASKS + k] = masks[0, k]
        table[CORE] = lax.rem(tile, 2)

    last = right_ref.shape[2] - 1
    turned[0] = turn(table, 0, top_ref[0, 0])
    turned[1] = turn(table, 1, right_ref[0].astype(F32)[:, last].astype(BF16))
    turned[2] = turn(table, 2, low_ref[0, 0])
    turned[3] = turn(table, 3, left_ref[0].astype(F32)[:, 0].astype(BF16))
    for d, to in enumerate((to0, to1, to2, to3)):
        to[0] = turned[table[SIDE_OF_DIR + d]]


def edges_call(where, links, flips, masks, state):
    batch, side, cols, channels = state.shape
    wide = 8
    one = lambda at: pl.BlockSpec((1, 1, cols, channels), lambda b: (b, at, 0, 0))
    column = lambda at: pl.BlockSpec((1, side, wide, channels), lambda b: (b, 0, at, 0))
    facing = pl.BlockSpec((1, side, channels), lambda b: (b, 0, 0))
    return pl.pallas_call(
        functools.partial(edges_body, (lax.axis_size("face"), lax.axis_size("tile"))),
        grid=(batch,),
        in_specs=[
            *[pl.BlockSpec(memory_space=pltpu.SMEM)] * 4,
            one(0),
            one(side - 1),
            column(0),
            column(cols // wide - 1),
        ],
        out_specs=[*[facing] * 4, pl.BlockSpec(memory_space=pltpu.SMEM)],
        out_shape=[
            *[jax.ShapeDtypeStruct((batch, side, channels), BF16)] * 4,
            jax.ShapeDtypeStruct((CORE + 1,), jnp.int32),
        ],
        scratch_shapes=[pltpu.VMEM((4, side, channels), BF16)],
        compiler_params=pltpu.CompilerParams(vmem_limit_bytes=57 << 20),
        name="edges",
    )(where, links, flips, masks, state, state, state, state)


LOW = (0, 1, 3, 0)
HIGH = (1, 2, 2, 3)


def ring_body(
    table, top_ref, low_ref, left_ref, right_ref, ctop_ref, clow_ref, cleft_ref, cright_ref,
    got0, got1, got2, got3, w_ref, tap_ref, bias_ref, pg_ref, dg_ref,
    gr_ref, to0, to1, to2, to3, point_ref, line_ref, strip, ext, acts, acc, turned,
):
    step = pl.program_id(0)
    side = got0.shape[1]
    got = (got0, got1, got2, got3)
    masks = [table[MASKS + k].astype(F32) for k in range(4)]

    @pl.when(step == 0)
    def _():
        acc[...] = dg_ref[...]
        point_ref[...] = pg_ref[...]
        ext[...] = jnp.zeros_like(ext)

    rims = [from_dir(table, got, s).astype(F32) for s in range(4)]
    top = top_ref[0].astype(F32)
    low = low_ref[0].astype(F32)
    left = left_ref[0].astype(F32)
    right = right_ref[0].astype(F32)
    last = left.shape[1] - 1
    end = side - 1

    def corner(k, first, second):
        return (masks[k] * 0.5 * (first + second)).astype(BF16).astype(F32)

    def at(s, i):
        return rims[s][i : i + 1]

    nw = corner(0, at(0, 0), at(3, 0))
    ne = corner(1, at(0, end), at(1, 0))
    se = corner(2, at(1, end), at(2, end))
    sw = corner(3, at(2, 0), at(3, end))
    lines = (
        ((rims[0], nw, ne), (top[0], at(3, 0), at(1, 0)), (top[1], at(3, 1), at(1, 1))),
        (
            (right[:, last - 1], at(0, end - 1), at(2, end - 1)),
            (right[:, last], at(0, end), at(2, end)),
            (rims[1], ne, se),
        ),
        (
            (low[0], at(3, end - 1), at(1, end - 1)),
            (low[1], at(3, end), at(1, end)),
            (rims[2], sw, se),
        ),
        ((rims[3], nw, sw), (left[:, 0], at(0, 0), at(2, 0)), (left[:, 1], at(0, 1), at(2, 1))),
    )
    for s in range(4):
        for a in range(3):
            line, before, after = lines[s][a]
            for hf in range(2):
                lanes = slice(hf * LANES, hf * LANES + LANES)
                strip[s, hf, a, PAD : PAD + side, :] = line[:, lanes]
                strip[s, hf, a, PAD - 1 : PAD, :] = before[:, lanes]
                strip[s, hf, a, PAD + side : PAD + side + 1, :] = after[:, lanes]
    cots = jnp.concatenate(
        [
            ctop_ref[0, 0].astype(F32),
            cright_ref[0].astype(F32)[:, last],
            clow_ref[0, 0].astype(F32),
            cleft_ref[0].astype(F32)[:, 0],
        ],
        axis=0,
    ).astype(BF16)
    ga = lax.dot_general(cots, w_ref[...], (((1,), (1,)), ((), ())), preferred_element_type=F32)
    row = lax.broadcasted_iota(jnp.int32, (side, LANES), 0)
    middle = jnp.logical_and(row > 0, row < end)
    for s in range(4):
        upright = s % 2 == 0
        rim_line = 0 if s in (0, 3) else 2
        for hf in range(2):
            lanes = slice(hf * LANES, hf * LANES + LANES)

            def tap(a, b):
                k = 3 * a + b if upright else 3 * b + a
                return k, tap_ref[k : k + 1, lanes]

            h = jnp.zeros((side, LANES), F32) + bias_ref[0:1, lanes]
            for a in range(3):
                for b in range(3):
                    h = h + tap(a, b)[1] * strip[s, hf, a, PAD - 1 + b : PAD - 1 + b + side, :]
            act, slope = gelu_pair(h)
            g = (ga[s * side : s * side + side, lanes] * slope).astype(BF16)
            gr_ref[s, 0, :, lanes] = g
            g = g.astype(F32)
            counted = g
            if not upright:
                counted = jnp.where(middle, g, 0.0)
                act = jnp.where(middle, act, 0.0)
            acts[s * side : s * side + side, lanes] = act.astype(BF16)
            for a in range(3):
                for b in range(3):
                    k = tap(a, b)[0]
                    term = counted * strip[s, hf, a, PAD - 1 + b : PAD - 1 + b + side, :]
                    acc[hf, k] += jnp.sum(term.reshape(side // SUB, SUB, LANES), axis=0)
            acc[hf, 9] += jnp.sum(counted.reshape(side // SUB, SUB, LANES), axis=0)
            ext[PAD : PAD + side, :] = g
            first, mid, final = (tap(rim_line, b)[1] for b in range(3))
            back = (
                first * ext[PAD + 1 : PAD + 1 + side, :]
                + mid * g
                + final * ext[PAD - 1 : PAD - 1 + side, :]
            )
            back = back + jnp.where(row == 0, (0.5 * masks[LOW[s]]) * first * g, 0.0)
            back = back + jnp.where(row == end, (0.5 * masks[HIGH[s]]) * final * g, 0.0)
            turned[s, :, lanes] = turn(table, s, back.astype(BF16))
    for d, to in enumerate((to0, to1, to2, to3)):
        to[0] = turned[table[SIDE_OF_DIR + d]]
    point_ref[...] += lax.dot_general(acts[...], cots, (((0,), (0,)), ((), ())), preferred_element_type=F32)

    @pl.when(step == pl.num_programs(0) - 1)
    def _():
        line_ref[...] = acc[...]


def ring_call(table, state, cotangent, got, weight, taps, bias, point_inner, depth_inner):
    batch, side, cols, channels = state.shape
    wide = 8
    two = lambda at: pl.BlockSpec((1, 2, cols, channels), lambda b: (b, at, 0, 0))
    one = lambda at: pl.BlockSpec((1, 1, cols, channels), lambda b: (b, at, 0, 0))
    column = lambda at: pl.BlockSpec((1, side, wide, channels), lambda b: (b, 0, at, 0))
    strips = pl.BlockSpec((4, 1, side, channels), lambda b: (0, b, 0, 0))
    facing = pl.BlockSpec((1, side, channels), lambda b: (b, 0, 0))
    far = cols // wide - 1
    return pl.pallas_call(
        ring_body,
        grid=(batch,),
        in_specs=[
            pl.BlockSpec(memory_space=pltpu.SMEM),
            two(0),
            two(side // 2 - 1),
            column(0),
            column(far),
            one(0),
            one(side - 1),
            column(0),
            column(far),
            *[facing] * 4,
            pl.BlockSpec((channels, channels), lambda b: (0, 0)),
            pl.BlockSpec((9, channels), lambda b: (0, 0)),
            pl.BlockSpec((1, channels), lambda b: (0, 0)),
            pl.BlockSpec((channels, channels), lambda b: (0, 0)),
            pl.BlockSpec((2, 10, SUB, LANES), lambda b: (0, 0, 0, 0)),
        ],
        out_specs=[
            strips,
            *[facing] * 4,
            pl.BlockSpec((channels, channels), lambda b: (0, 0)),
            pl.BlockSpec((2, 10, SUB, LANES), lambda b: (0, 0, 0, 0)),
        ],
        out_shape=[
            jax.ShapeDtypeStruct((4, batch, side, channels), BF16),
            *[jax.ShapeDtypeStruct((batch, side, channels), BF16)] * 4,
            jax.ShapeDtypeStruct((channels, channels), F32),
            jax.ShapeDtypeStruct((2, 10, SUB, LANES), F32),
        ],
        scratch_shapes=[
            pltpu.VMEM((4, 2, 3, cols + 2 * PAD, LANES), F32),
            pltpu.VMEM((cols + 2 * PAD, LANES), F32),
            pltpu.VMEM((4 * side, channels), BF16),
            pltpu.VMEM((2, 10, SUB, LANES), F32),
            pltpu.VMEM((4, side, channels), BF16),
        ],
        compiler_params=pltpu.CompilerParams(vmem_limit_bytes=57 << 20),
        cost_estimate=pl.CostEstimate(
            flops=3_000_000_000, bytes_accessed=12 << 20, transcendentals=state.size // 16
        ),
        name="ring",
    )(table, state, state, state, state, cotangent, cotangent, cotangent, cotangent, *got, weight, taps, bias,
      point_inner, depth_inner)


def spread_body(rows, first, table, gh_ref, above_ref, below_ref, gr_ref, got0, got1, got2, got3, tap_ref, out_ref, token_ref, gf, near, far, ring, back):
    got = (got0, got1, got2, got3)
    side = gr_ref.shape[2]
    cols = gh_ref.shape[2]
    count = gh_ref.shape[1]
    chunks = side // count
    step = (pl.program_id(0) + first) % chunks
    token_ref[...] = jnp.zeros_like(token_ref)
    start = step * count

    @pl.when(jnp.logical_or(pl.program_id(0) == 0, step == 0))
    def _():
        for k, s in enumerate((1, 3)):
            back[k] = from_dir(table, got, s)
        for hf in range(2):
            lanes = slice(hf * LANES, hf * LANES + LANES)
            gf[hf, :, 0:PAD, :] = jnp.zeros((count + 2, PAD, LANES), F32)
            gf[hf, :, PAD + cols : 2 * PAD + cols, :] = jnp.zeros((count + 2, PAD, LANES), F32)
            for k, s in enumerate((1, 3)):
                ring[k, hf, 0:PAD, :] = jnp.zeros((PAD, LANES), F32)
                ring[k, hf, PAD + side :, :] = jnp.zeros((PAD, LANES), F32)
                ring[k, hf, PAD : PAD + side, :] = gr_ref[s, 0, :, lanes].astype(F32)
        near[...] = jnp.zeros_like(near)
        far[...] = jnp.zeros_like(far)

    def put(i, v):
        v = v.astype(F32)
        gf[0, i, PAD : PAD + cols, :] = v[:, :LANES]
        gf[1, i, PAD : PAD + cols, :] = v[:, LANES:]

    put(0, jnp.where(step > 0, above_ref[0, 0], jnp.zeros_like(above_ref[0, 0])))
    put(count + 1, jnp.where(step < chunks - 1, below_ref[0, 0], jnp.zeros_like(below_ref[0, 0])))
    for i in range(count):
        put(i + 1, gh_ref[0, i])
    cut = [back[k, pl.ds(pl.multiple_of(start, count), count), :].astype(F32) for k in range(2)]
    for hf in range(2):
        lanes = slice(hf * LANES, hf * LANES + LANES)
        for k, j in ((0, PAD + cols - 1), (1, PAD)):
            own = ring[k, hf, pl.ds(pl.multiple_of(PAD + start, SUB), count), :]
            gf[hf, 1 : count + 1, j : j + 1, :] = own.reshape(count, 1, LANES)
            gf[hf, 0, j : j + 1, :] = ring[k, hf, pl.ds(PAD + start - 1, 1), :]
            gf[hf, count + 1, j : j + 1, :] = ring[k, hf, pl.ds(PAD + start + count, 1), :]
        near[hf, :, 0:1, :] = cut[1][:, lanes].reshape(count, 1, LANES)
        far[hf, :, SUB - 1 : SUB, :] = cut[0][:, lanes].reshape(count, 1, LANES)

    def line(i, s):
        v = gr_ref[s, 0].astype(F32)
        for hf in range(2):
            gf[hf, i, PAD : PAD + cols, :] = v[:, hf * LANES : hf * LANES + LANES]

    @pl.when(step == 0)
    def _():
        line(1, 0)

    @pl.when(step == chunks - 1)
    def _():
        line(count, 2)

    for hf in range(2):
        lanes = slice(hf * LANES, hf * LANES + LANES)
        taps = [tap_at(tap_ref, hf, k) for k in range(9)]
        for jb in range(cols // 16):

            def body(it, carry):
                i = it * rows
                win = {}
                for q in range(rows):
                    pair = []
                    for half in range(2):
                        j = PAD + jb * 16 + half * SUB
                        total = None
                        for r in range(3):
                            for c in range(3):
                                at = (q + 2 - r, 2 - c, half)
                                if at not in win:
                                    win[at] = gf[hf, i + at[0], j - 1 + at[1] : j - 1 + at[1] + SUB, :]
                                term = taps[3 * r + c] * win[at]
                                total = term if total is None else total + term
                        if jb == 0 and half == 0:
                            total = total + near[hf, i + q]
                        if jb == cols // 16 - 1 and half == 1:
                            total = total + far[hf, i + q]
                        pair.append(total)
                    out_ref[0, i + q, jb * 16 : jb * 16 + 16, lanes] = jnp.concatenate(pair, axis=0).astype(BF16)
                return carry

            for it in range(count // rows):
                body(it, 0)

    def add(i, s):
        out_ref[0, i] = (out_ref[0, i].astype(F32) + from_dir(table, got, s).astype(F32)).astype(BF16)

    @pl.when(step == 0)
    def _():
        add(0, 0)

    @pl.when(step == chunks - 1)
    def _():
        add(count - 1, 2)


CHUNK = 16


def spread_call(first, steps, table, grad, ring, got, taps, into):
    batch, side, cols, channels = grad.shape
    chunks = side // CHUNK
    high = side - 1
    at = lambda i: ((i + first) // chunks, (i + first) % chunks)
    strips = pl.BlockSpec((4, 1, side, channels), lambda i: (0, at(i)[0], 0, 0))
    facing = pl.BlockSpec((1, side, channels), lambda i: (at(i)[0], 0, 0))
    rows = pl.BlockSpec((1, CHUNK, cols, channels), lambda i: (*at(i), 0, 0))
    in_specs = [
        pl.BlockSpec(memory_space=pltpu.SMEM),
        rows,
        pl.BlockSpec((1, 1, cols, channels), lambda i: (at(i)[0], jnp.maximum(at(i)[1] * CHUNK - 1, 0), 0, 0)),
        pl.BlockSpec((1, 1, cols, channels), lambda i: (at(i)[0], jnp.minimum(at(i)[1] * CHUNK + CHUNK, high), 0, 0)),
        strips,
        *[facing] * 4,
        pl.BlockSpec((9, channels), lambda i: (0, 0)),
    ]
    operands = [table, grad, grad, grad, ring, *got, taps]
    aliases = {}
    if into is not None:
        aliases = {len(operands): 0}
        in_specs.append(pl.BlockSpec(memory_space=pl.ANY))
        operands.append(into)

    def body(*refs):
        spread_body(4, first, *refs[:10], *refs[len(operands) :])

    return pl.pallas_call(
        body,
        grid=(steps,),
        in_specs=in_specs,
        out_specs=[rows, pl.BlockSpec((SUB, LANES), lambda i: (0, 0))],
        out_shape=[jax.ShapeDtypeStruct(grad.shape, BF16), jax.ShapeDtypeStruct((SUB, LANES), F32)],
        scratch_shapes=[
            pltpu.VMEM((2, CHUNK + 2, cols + 2 * PAD, LANES), F32),
            pltpu.VMEM((2, CHUNK, SUB, LANES), F32),
            pltpu.VMEM((2, CHUNK, SUB, LANES), F32),
            pltpu.VMEM((2, 2, side + 2 * PAD, LANES), F32),
            pltpu.VMEM((2, side, channels), BF16),
        ],
        input_output_aliases=aliases,
        compiler_params=pltpu.CompilerParams(vmem_limit_bytes=57 << 20),
        cost_estimate=pl.CostEstimate(
            flops=750_000_000 * steps, bytes_accessed=grad.size * 4 * steps // (batch * chunks), transcendentals=0
        ),
        name="spread",
    )(*operands)


def finish_body(scale, table, mine_ref, other_ref, dg_ref, bg_ref, pg_ref):
    rows = mine_ref.shape[0]
    channels = pg_ref.shape[0]
    own = mine_ref[...] * scale
    far = other_ref[...] * scale
    first = table[CORE] == 0
    low = jnp.where(first, own, far)
    high = jnp.where(first, far, own)
    pg_ref[0:rows, :] = low
    pg_ref[rows:channels, :] = high[: channels - rows]
    tail = high[channels - rows :]
    dg_ref[...] = tail[0:9]
    bg_ref[...] = tail[9:10]


def finish_call(scale, bit, mine, other):
    channels = mine.shape[1]
    vmem = pl.BlockSpec(memory_space=pltpu.VMEM)
    return pl.pallas_call(
        functools.partial(finish_body, scale),
        in_specs=[pl.BlockSpec(memory_space=pltpu.SMEM), vmem, vmem],
        out_specs=[vmem, vmem, vmem],
        out_shape=[
            jax.ShapeDtypeStruct((9, channels), F32),
            jax.ShapeDtypeStruct((1, channels), F32),
            jax.ShapeDtypeStruct((channels, channels), F32),
        ],
        name="finish",
    )(bit, mine, other)


def exchange(facing):
    faces, tiles = lax.axis_size("face"), lax.axis_size("tile")
    got = []
    for d, rows in enumerate(facing):
        pairs = []
        for i in range(faces * tiles):
            at = [i // tiles, i % tiles]
            k = d // 2
            step = 1 - 2 * (at[k] % 2)
            at[k] = (at[k] + (step if d % 2 == 0 else -step)) % (faces, tiles)[k]
            pairs.append((i, at[0] * tiles + at[1]))
        got.append(lax.ppermute(rows, ("face", "tile"), pairs))
    return got


def swap(value, mask):
    devices = lax.axis_size("face") * lax.axis_size("tile")
    return lax.ppermute(value, ("face", "tile"), [(i, i ^ mask) for i in range(devices)])


def after(value, *others):
    return lax.optimization_barrier((value, *others))[0]


def shards(
    state, cotangent, depth_weight, depth_bias, point_weight, tile_links, link_sides, link_flips, corner_masks
):
    batch, side, cols, channels = state.shape
    face_count = lax.axis_size("face")
    tile_count = lax.axis_size("tile")
    face_pos = lax.axis_index("face")
    tile_pos = lax.axis_index("tile")
    where = jnp.stack([face_pos, tile_pos])
    bias = depth_bias.reshape(1, channels)
    *edges, table = edges_call(where, tile_links, link_flips, corner_masks, state)
    got = exchange(edges)
    layer = (point_weight, depth_weight, bias)
    early = batch // 2
    grad, point_sum, depth_sum = inner_call(0, early, state, cotangent, *layer)
    ring, *facing, point_sum, depth_sum = ring_call(table, state, cotangent, got, *layer, point_sum, depth_sum)
    incoming = exchange(facing)
    grad, mine, sent = inner_call(
        early, batch - early, state, cotangent, *layer, (table, grad, point_sum, depth_sum)
    )

    first, field_grad = 0, None
    for stage, (mask_bits, steps) in enumerate(
        ((1, 2), (2, 2), (6, 2), (8, 2), (24, 2), (32, 2), (96, 2), (1, 2))
    ):
        got = swap(sent if stage == 0 else mine, mask_bits)
        if steps:
            held = after(depth_weight, mine if stage else sent)
            field_grad, token = spread_call(first, steps, table, grad, ring, incoming, held, field_grad)
            got = after(got, token)
            first += steps
        if stage < 7:
            mine = mine + got
    scale = float(batch * side * cols * face_count * tile_count) ** -0.5
    depth_grad, bias_grad, point_grad = finish_call(scale, table, mine, got)
    return field_grad, depth_grad, bias_grad.reshape(channels), point_grad


def solution(mesh):
    tiles = P(None, "face", "tile", None)
    table = P(("face", "tile"), None)
    return jax.shard_map(
        shards,
        mesh=mesh,
        in_specs=(tiles, tiles, P(), P(), P(), table, table, table, table),
        out_specs=(tiles, P(), P(), P()),
        check_vma=False,
    )
```

```python
import functools

import jax
import jax.numpy as jnp
from jax import lax
from jax.experimental import pallas as pl
from jax.experimental.pallas import tpu as pltpu
from jax.sharding import PartitionSpec as P

ROOT = 0.7978845608028654
CUBIC = 0.044715
F32 = jnp.float32
BF16 = jnp.bfloat16
LANES = 128
SUB = 8
PAD = 8


def gelu_pair(h):
    h2 = h * h
    s = 0.5 * jnp.tanh(h * ((CUBIC * ROOT) * h2 + ROOT)) + 0.5
    act = h * s
    slope = s + act * (1.0 - s) * ((6.0 * CUBIC * ROOT) * h2 + 2.0 * ROOT)
    return act, slope


ALPHA = (CUBIC * ROOT) ** (1.0 / 3.0)
KAPPA = ROOT / ALPHA


def gelu_scaled(h):
    h2 = h * h
    t = jnp.tanh(h * (h2 + KAPPA))
    up = 1.0 + t
    act = h * up
    return act, up + act * (1.0 - t) * (3.0 * h2 + KAPPA)


def tap_at(ref, hf, k):
    return jnp.broadcast_to(ref[k : k + 1, hf * LANES : hf * LANES + LANES], (SUB, LANES))


def inner_body(pairs, x_ref, cot_ref, w_ref, tap_ref, bias_ref, gh_ref, pg_out, dg_out, u, hide, acc, half_w, pg_ref, *bufs):
    step = pl.program_id(0)
    side = x_ref.shape[1]
    cols = x_ref.shape[2]
    sets = (bufs[0:4], bufs[4:8])

    @pl.when(step == 0)
    def _():
        for hf in range(2):
            for c in range(3):
                w0, w1, w2 = (tap_at(tap_ref, hf, 3 * r + c) * ALPHA for r in range(3))
                u[hf, c] = w0
                u[hf, 3 + c] = (w0 + w1 + w2) * 0.5
                u[hf, 6 + c] = (w0 - w1 + w2) * 0.5
                u[hf, 9 + c] = w2
            u[hf, 12] = tap_at(bias_ref, hf, 0) * ALPHA
        half_w[...] = w_ref[...] * jnp.asarray(0.5, BF16)
        for qt, _, _, _ in sets:
            edge = jnp.zeros((2, pairs, 4, PAD, LANES), F32)
            qt[:, :, :, 0:PAD, :] = edge
            qt[:, :, :, PAD + cols :, :] = edge
        col = lax.broadcasted_iota(jnp.int32, (cols, 2 * LANES), 0)
        keep = jnp.logical_and(col > 0, col < cols - 1)
        hide[0] = jnp.where(keep, 1.0, 0.0).astype(BF16)
        hide[1] = jnp.zeros((cols, 2 * LANES), BF16)
        acc[...] = jnp.zeros_like(acc)
        pg_ref[...] = jnp.zeros_like(pg_ref)

    rows = 2 * pairs

    def outer(buf):
        _, _, act, cot = buf
        pg_ref[...] += lax.dot_general(
            act[...], cot[...], (((0,), (0,)), ((), ())), preferred_element_type=F32
        )

    def chunk(t, buf):
        qt, ga, act, cot = buf
        base = t * rows
        for q in range(rows):
            i = base + q
            kind = jnp.where(jnp.logical_or(i == 0, i == side - 1), 1, 0)
            cot[q * cols : q * cols + cols, :] = cot_ref[0, i] * hide[kind]
        g = lax.dot_general(cot[...], half_w[...], (((1,), (1,)), ((), ())), preferred_element_type=F32)
        ga[0] = g[:, :LANES]
        ga[1] = g[:, LANES:]
        for hf in range(2):
            lanes = slice(hf * LANES, hf * LANES + LANES)
            line = [x_ref[0, jnp.maximum(base - 1, 0), :, lanes].astype(F32)]
            for q in range(rows):
                line.append(x_ref[0, base + q, :, lanes].astype(F32))
            line.append(x_ref[0, jnp.minimum(base + rows, side - 1), :, lanes].astype(F32))
            for p in range(pairs):
                q0, q1, q2, q3 = line[2 * p : 2 * p + 4]
                for k, v in enumerate((q0 - q2, q1 + q2, q2 - q1, q1 - q3)):
                    qt[hf, p, k, PAD : PAD + cols, :] = v
        for hf in range(2):
            lanes = slice(hf * LANES, hf * LANES + LANES)
            sums = [acc[hf, k] for k in range(13)]
            for p in range(pairs):
                for jb in range(cols // 16):
                    halves = []
                    for half in range(2):
                        j = jb * 16 + half * SUB
                        win = [
                            [qt[hf, p, k, PAD - 1 + j + c : PAD - 1 + j + c + SUB, :] for c in range(3)]
                            for k in range(4)
                        ]
                        m = []
                        for k in range(4):
                            v = u[hf, 3 * k] * win[k][0]
                            v = v + u[hf, 3 * k + 1] * win[k][1]
                            m.append(v + u[hf, 3 * k + 2] * win[k][2])
                        both = m[1] + u[hf, 12]
                        found = []
                        for q, h in enumerate((both + m[0] + m[2], both - m[2] - m[3])):
                            a, slope = gelu_scaled(h)
                            at = (2 * p + q) * cols + j
                            found.append((a, ga[hf, at : at + SUB, :] * slope))
                        g0, g1 = found[0][1], found[1][1]
                        plus, minus = g0 + g1, g0 - g1
                        for k, v in enumerate((g0, plus, minus, g1)):
                            for c in range(3):
                                sums[3 * k + c] = sums[3 * k + c] + v * win[k][c]
                        sums[12] = sums[12] + plus
                        halves.append(found)
                    for q in range(2):
                        at = (2 * p + q) * cols + jb * 16
                        act[at : at + 16, lanes] = jnp.concatenate(
                            [halves[0][q][0], halves[1][q][0]], axis=0
                        ).astype(BF16)
                        gh_ref[0, base + 2 * p + q, jb * 16 : jb * 16 + 16, lanes] = jnp.concatenate(
                            [halves[0][q][1], halves[1][q][1]], axis=0
                        ).astype(BF16)
            for k in range(13):
                acc[hf, k] = sums[k]

    def body(t, carry):
        chunk(2 * t, sets[0])
        outer(sets[1])
        chunk(2 * t + 1, sets[1])
        outer(sets[0])
        return carry

    sets[1][2][...] = jnp.zeros_like(sets[1][2])
    sets[1][3][...] = jnp.zeros_like(sets[1][3])
    lax.fori_loop(0, side // (2 * rows), body, 0)
    outer(sets[1])

    def tap_sums(hf):
        lines = [None] * 10
        for c in range(3):
            d1, d2, d3, d4 = (acc[hf, 3 * k + c] for k in range(4))
            even = 0.5 * (d2 + d3)
            lines[c] = d1 + even
            lines[3 + c] = 0.5 * (d2 - d3)
            lines[6 + c] = even - d4
        lines[9] = acc[hf, 12]
        return lines

    @pl.when(step == pl.num_programs(0) - 1)
    def _():
        point = pg_ref[...] * (0.5 / ALPHA)
        pg_out[...] = point
        for hf in range(2):
            for k, line in enumerate(tap_sums(hf)):
                dg_out[hf, k] = line


PAIRS = 4


def inner_call(state, cotangent, weight, taps, bias):
    batch, side, cols, channels = state.shape
    tile = pl.BlockSpec((1, side, cols, channels), lambda b: (b, 0, 0, 0))
    whole = lambda *shape: pl.BlockSpec(shape, lambda b: (0,) * len(shape))
    buf = [
        pltpu.VMEM((2, PAIRS, 4, cols + 2 * PAD, LANES), F32),
        pltpu.VMEM((2, 2 * PAIRS * cols, LANES), F32),
        pltpu.VMEM((2 * PAIRS * cols, channels), BF16),
        pltpu.VMEM((2 * PAIRS * cols, channels), BF16),
    ]
    square, lines = (channels, channels), (2, 10, SUB, LANES)
    shapes = (square, lines)
    return pl.pallas_call(
        functools.partial(inner_body, PAIRS),
        grid=(batch,),
        in_specs=[tile, tile, whole(*square), whole(9, channels), whole(1, channels)],
        out_specs=[tile, *(whole(*shape) for shape in shapes)],
        out_shape=[
            jax.ShapeDtypeStruct(state.shape, BF16),
            *(jax.ShapeDtypeStruct(shape, F32) for shape in shapes),
        ],
        scratch_shapes=[
            pltpu.VMEM((2, 13, SUB, LANES), F32),
            pltpu.VMEM((2, cols, channels), BF16),
            pltpu.VMEM((2, 13, SUB, LANES), F32),
            pltpu.VMEM(square, BF16),
            pltpu.VMEM(square, F32),
            *buf,
            *buf,
        ],
        compiler_params=pltpu.CompilerParams(vmem_limit_bytes=57 << 20),
        cost_estimate=pl.CostEstimate(
            flops=40_000_000_000, bytes_accessed=state.size * 6, transcendentals=state.size
        ),
        name="inner",
    )(state, cotangent, weight, taps, bias)


DIR_OF_SIDE, SIDE_OF_DIR, FLIPS, MASKS, CORE = 0, 4, 8, 12, 16


def from_dir(table, got, s, b=0):
    d = table[DIR_OF_SIDE + s]
    rows = got[3][b]
    for k in range(3):
        rows = jnp.where(d == k, got[k][b], rows)
    return rows


def turn(table, s, rows):
    count = rows.shape[0]
    i = lax.broadcasted_iota(jnp.int32, (count, count), 0)
    j = lax.broadcasted_iota(jnp.int32, (count, count), 1)
    source = jnp.where(table[FLIPS + s] == 1, count - 1 - i, i)
    pick = jnp.where(j == source, 1.0, 0.0).astype(BF16)
    return jnp.dot(pick, rows, preferred_element_type=F32).astype(BF16)


def columns(tile, buf, which):
    rows = tile.shape[0]
    flat = tile.astype(F32).reshape(rows * SUB, 2 * LANES)
    for hf in range(2):
        buf[hf] = flat[:, hf * LANES : hf * LANES + LANES]
    return [
        jnp.concatenate([buf[hf, pl.ds(c, rows, stride=SUB), :] for hf in range(2)], axis=1) for c in which
    ]


def edges_body(sizes, where, links, flips, masks, top_ref, low_ref, left_ref, right_ref, to0, to1, to2, to3, table, turned, wide):
    faces, tiles = sizes

    @pl.when(pl.program_id(0) == 0)
    def _():
        face, tile = where[0], where[1]
        face_step = 1 - 2 * lax.rem(face, 2)
        tile_step = 1 - 2 * lax.rem(tile, 2)
        towards = (
            (face + face_step) * tiles + tile,
            lax.rem(face - face_step + faces, faces) * tiles + tile,
            face * tiles + tile + tile_step,
            face * tiles + lax.rem(tile - tile_step + tiles, tiles),
        )
        met = [[jnp.where(links[0, s] == to, 1, 0) for to in towards] for s in range(4)]
        for k in range(4):
            table[DIR_OF_SIDE + k] = met[k][1] + 2 * met[k][2] + 3 * met[k][3]
            table[SIDE_OF_DIR + k] = met[1][k] + 2 * met[2][k] + 3 * met[3][k]
            table[FLIPS + k] = flips[0, k]
            table[MASKS + k] = masks[0, k]
        table[CORE] = lax.rem(tile, 2)

    last = right_ref.shape[2] - 1
    for b in range(top_ref.shape[0]):
        turned[b, 0] = turn(table, 0, top_ref[b, 0])
        turned[b, 1] = turn(table, 1, columns(right_ref[b], wide.at[0], (last,))[0].astype(BF16))
        turned[b, 2] = turn(table, 2, low_ref[b, 0])
        turned[b, 3] = turn(table, 3, columns(left_ref[b], wide.at[1], (0,))[0].astype(BF16))
    for b in range(top_ref.shape[0]):
        for d, to in enumerate((to0, to1, to2, to3)):
            to[b] = turned[b, table[SIDE_OF_DIR + d]]


EDGE_SAMPLES, RING_SAMPLES = 2, 2


def edges_call(where, links, flips, masks, state):
    batch, side, cols, channels = state.shape
    wide, held = 8, EDGE_SAMPLES
    one = lambda at: pl.BlockSpec((held, 1, cols, channels), lambda b: (b, at, 0, 0))
    column = lambda at: pl.BlockSpec((held, side, wide, channels), lambda b: (b, 0, at, 0))
    facing = pl.BlockSpec((held, side, channels), lambda b: (b, 0, 0))
    return pl.pallas_call(
        functools.partial(edges_body, (lax.axis_size("face"), lax.axis_size("tile"))),
        grid=(batch // held,),
        in_specs=[
            *[pl.BlockSpec(memory_space=pltpu.SMEM)] * 4,
            one(0),
            one(side - 1),
            column(0),
            column(cols // wide - 1),
        ],
        out_specs=[*[facing] * 4, pl.BlockSpec(memory_space=pltpu.SMEM)],
        out_shape=[
            *[jax.ShapeDtypeStruct((batch, side, channels), BF16)] * 4,
            jax.ShapeDtypeStruct((CORE + 1,), jnp.int32),
        ],
        scratch_shapes=[
            pltpu.VMEM((held, 4, side, channels), BF16),
            pltpu.VMEM((2, 2, side * SUB, LANES), F32),
        ],
        compiler_params=pltpu.CompilerParams(vmem_limit_bytes=57 << 20),
        name="edges",
    )(where, links, flips, masks, state, state, state, state)


LOW = (0, 1, 3, 0)
HIGH = (1, 2, 2, 3)


def ring_body(
    table, top_ref, low_ref, left_ref, right_ref, ctop_ref, clow_ref, cleft_ref, cright_ref,
    got0, got1, got2, got3, w_ref, tap_ref, bias_ref, pg_ref, dg_ref,
    gr_ref, to0, to1, to2, to3, mine, sent, strip, ext, acts, acc, turned, wide, point_ref,
):
    step = pl.program_id(0)
    side = got0.shape[1]
    got = (got0, got1, got2, got3)
    masks = [table[MASKS + k].astype(F32) for k in range(4)]

    @pl.when(step == 0)
    def _():
        acc[...] = dg_ref[...]
        point_ref[...] = pg_ref[...]
        ext[...] = jnp.zeros_like(ext)

    def sample(n):
        rims = [from_dir(table, got, s, n).astype(F32) for s in range(4)]
        top = top_ref[n].astype(F32)
        low = low_ref[n].astype(F32)
        last = SUB - 1
        left = columns(left_ref[n], wide.at[0], (0, 1))
        right = columns(right_ref[n], wide.at[1], (last - 1, last))
        end = side - 1

        def corner(k, first, second):
            return (masks[k] * 0.5 * (first + second)).astype(BF16).astype(F32)

        def at(s, i):
            return rims[s][i : i + 1]

        nw = corner(0, at(0, 0), at(3, 0))
        ne = corner(1, at(0, end), at(1, 0))
        se = corner(2, at(1, end), at(2, end))
        sw = corner(3, at(2, 0), at(3, end))
        lines = (
            ((rims[0], nw, ne), (top[0], at(3, 0), at(1, 0)), (top[1], at(3, 1), at(1, 1))),
            (
                (right[0], at(0, end - 1), at(2, end - 1)),
                (right[1], at(0, end), at(2, end)),
                (rims[1], ne, se),
            ),
            (
                (low[0], at(3, end - 1), at(1, end - 1)),
                (low[1], at(3, end), at(1, end)),
                (rims[2], sw, se),
            ),
            ((rims[3], nw, sw), (left[0], at(0, 0), at(2, 0)), (left[1], at(0, 1), at(2, 1))),
        )
        for s in range(4):
            for a in range(3):
                line, before, after = lines[s][a]
                for hf in range(2):
                    lanes = slice(hf * LANES, hf * LANES + LANES)
                    strip[n, s, hf, a, PAD : PAD + side, :] = line[:, lanes]
                    strip[n, s, hf, a, PAD - 1 : PAD, :] = before[:, lanes]
                    strip[n, s, hf, a, PAD + side : PAD + side + 1, :] = after[:, lanes]
        cots = jnp.concatenate(
            [
                ctop_ref[n, 0].astype(F32),
                columns(cright_ref[n], wide.at[2], (last,))[0],
                clow_ref[n, 0].astype(F32),
                columns(cleft_ref[n], wide.at[3], (0,))[0],
            ],
            axis=0,
        ).astype(BF16)
        ga = lax.dot_general(cots, w_ref[...], (((1,), (1,)), ((), ())), preferred_element_type=F32)
        row = lax.broadcasted_iota(jnp.int32, (side, LANES), 0)
        middle = jnp.logical_and(row > 0, row < end)
        for s in range(4):
            upright = s % 2 == 0
            rim_line = 0 if s in (0, 3) else 2
            for hf in range(2):
                lanes = slice(hf * LANES, hf * LANES + LANES)

                def tap(a, b):
                    k = 3 * a + b if upright else 3 * b + a
                    return k, tap_ref[k : k + 1, lanes]

                h = jnp.zeros((side, LANES), F32) + bias_ref[0:1, lanes]
                for a in range(3):
                    for b in range(3):
                        h = h + tap(a, b)[1] * strip[n, s, hf, a, PAD - 1 + b : PAD - 1 + b + side, :]
                act, slope = gelu_pair(h)
                g = (ga[s * side : s * side + side, lanes] * slope).astype(BF16)
                gr_ref[s, n, :, lanes] = g
                g = g.astype(F32)
                counted = g
                if not upright:
                    counted = jnp.where(middle, g, 0.0)
                    act = jnp.where(middle, act, 0.0)
                acts[n, s * side : s * side + side, lanes] = act.astype(BF16)
                for a in range(3):
                    for b in range(3):
                        k = tap(a, b)[0]
                        term = counted * strip[n, s, hf, a, PAD - 1 + b : PAD - 1 + b + side, :]
                        acc[hf, k] += jnp.sum(term.reshape(side // SUB, SUB, LANES), axis=0)
                acc[hf, 9] += jnp.sum(counted.reshape(side // SUB, SUB, LANES), axis=0)
                ext[n, PAD : PAD + side, :] = g
                first, mid, final = (tap(rim_line, b)[1] for b in range(3))
                back = (
                    first * ext[n, PAD + 1 : PAD + 1 + side, :]
                    + mid * g
                    + final * ext[n, PAD - 1 : PAD - 1 + side, :]
                )
                back = back + jnp.where(row == 0, (0.5 * masks[LOW[s]]) * first * g, 0.0)
                back = back + jnp.where(row == end, (0.5 * masks[HIGH[s]]) * final * g, 0.0)
                turned[n, s, :, lanes] = turn(table, s, back.astype(BF16))
        for d, to in enumerate((to0, to1, to2, to3)):
            to[n] = turned[n, table[SIDE_OF_DIR + d]]
        point_ref[...] += lax.dot_general(acts[n], cots, (((0,), (0,)), ((), ())), preferred_element_type=F32)

    for n in range(got0.shape[0]):
        sample(n)

    @pl.when(step == pl.num_programs(0) - 1)
    def _():
        rows = mine.shape[0]
        lines = []
        for hf in range(2):
            own = [jnp.sum(acc[hf, k], axis=0, keepdims=True) for k in range(10)]
            lines.append(jnp.concatenate(own + [jnp.zeros((6, LANES), F32)], axis=0))
        low = point_ref[0:rows]
        high = jnp.concatenate([point_ref[rows:], jnp.concatenate(lines, axis=1)], axis=0)
        first = table[CORE] == 0
        mine[...] = jnp.where(first, low, high)
        sent[...] = jnp.where(first, high, low)


def ring_call(table, state, cotangent, got, weight, taps, bias, point_inner, depth_inner):
    batch, side, cols, channels = state.shape
    wide, held, half = 8, RING_SAMPLES, (channels + 16) // 2
    two = lambda at: pl.BlockSpec((held, 2, cols, channels), lambda b: (b, at, 0, 0))
    one = lambda at: pl.BlockSpec((held, 1, cols, channels), lambda b: (b, at, 0, 0))
    column = lambda at: pl.BlockSpec((held, side, wide, channels), lambda b: (b, 0, at, 0))
    strips = pl.BlockSpec((4, held, side, channels), lambda b: (0, b, 0, 0))
    facing = pl.BlockSpec((held, side, channels), lambda b: (b, 0, 0))
    far = cols // wide - 1
    return pl.pallas_call(
        ring_body,
        grid=(batch // held,),
        in_specs=[
            pl.BlockSpec(memory_space=pltpu.SMEM),
            two(0),
            two(side // 2 - 1),
            column(0),
            column(far),
            one(0),
            one(side - 1),
            column(0),
            column(far),
            *[facing] * 4,
            pl.BlockSpec((channels, channels), lambda b: (0, 0)),
            pl.BlockSpec((9, channels), lambda b: (0, 0)),
            pl.BlockSpec((1, channels), lambda b: (0, 0)),
            pl.BlockSpec((channels, channels), lambda b: (0, 0)),
            pl.BlockSpec((2, 10, SUB, LANES), lambda b: (0, 0, 0, 0)),
        ],
        out_specs=[
            strips,
            *[facing] * 4,
            *[pl.BlockSpec((half, channels), lambda b: (0, 0))] * 2,
        ],
        out_shape=[
            jax.ShapeDtypeStruct((4, batch, side, channels), BF16),
            *[jax.ShapeDtypeStruct((batch, side, channels), BF16)] * 4,
            *[jax.ShapeDtypeStruct((half, channels), F32)] * 2,
        ],
        scratch_shapes=[
            pltpu.VMEM((held, 4, 2, 3, cols + 2 * PAD, LANES), F32),
            pltpu.VMEM((held, cols + 2 * PAD, LANES), F32),
            pltpu.VMEM((held, 4 * side, channels), BF16),
            pltpu.VMEM((2, 10, SUB, LANES), F32),
            pltpu.VMEM((held, 4, side, channels), BF16),
            pltpu.VMEM((4, 2, side * SUB, LANES), F32),
            pltpu.VMEM((channels, channels), F32),
        ],
        compiler_params=pltpu.CompilerParams(vmem_limit_bytes=57 << 20),
        cost_estimate=pl.CostEstimate(
            flops=3_000_000_000, bytes_accessed=12 << 20, transcendentals=state.size // 16
        ),
        name="ring",
    )(table, state, state, state, state, cotangent, cotangent, cotangent, cotangent, *got, weight, taps, bias,
      point_inner, depth_inner)


def spread_body(rows, first, table, gh_ref, above_ref, below_ref, gr_ref, got0, got1, got2, got3, tap_ref, out_ref, token_ref, gf, near, far, ring, back):
    got = (got0, got1, got2, got3)
    side = gr_ref.shape[2]
    cols = gh_ref.shape[2]
    count = gh_ref.shape[1]
    chunks = side // count
    step = (pl.program_id(0) + first) % chunks
    token_ref[...] = jnp.zeros_like(token_ref)
    start = step * count

    @pl.when(jnp.logical_or(pl.program_id(0) == 0, step == 0))
    def _():
        for k, s in enumerate((1, 3)):
            back[k] = from_dir(table, got, s)
        for hf in range(2):
            lanes = slice(hf * LANES, hf * LANES + LANES)
            gf[hf, :, 0:PAD, :] = jnp.zeros((count + 2, PAD, LANES), F32)
            gf[hf, :, PAD + cols : 2 * PAD + cols, :] = jnp.zeros((count + 2, PAD, LANES), F32)
            for k, s in enumerate((1, 3)):
                ring[k, hf, 0:PAD, :] = jnp.zeros((PAD, LANES), F32)
                ring[k, hf, PAD + side :, :] = jnp.zeros((PAD, LANES), F32)
                ring[k, hf, PAD : PAD + side, :] = gr_ref[s, 0, :, lanes].astype(F32)
        near[...] = jnp.zeros_like(near)
        far[...] = jnp.zeros_like(far)

    def put(i, v):
        v = v.astype(F32)
        gf[0, i, PAD : PAD + cols, :] = v[:, :LANES]
        gf[1, i, PAD : PAD + cols, :] = v[:, LANES:]

    put(0, jnp.where(step > 0, above_ref[0, 0], jnp.zeros_like(above_ref[0, 0])))
    put(count + 1, jnp.where(step < chunks - 1, below_ref[0, 0], jnp.zeros_like(below_ref[0, 0])))
    for i in range(count):
        put(i + 1, gh_ref[0, i])
    cut = [back[k, pl.ds(pl.multiple_of(start, count), count), :].astype(F32) for k in range(2)]
    for hf in range(2):
        lanes = slice(hf * LANES, hf * LANES + LANES)
        for k, j in ((0, PAD + cols - 1), (1, PAD)):
            own = ring[k, hf, pl.ds(pl.multiple_of(PAD + start, SUB), count), :]
            gf[hf, 1 : count + 1, j : j + 1, :] = own.reshape(count, 1, LANES)
            gf[hf, 0, j : j + 1, :] = ring[k, hf, pl.ds(PAD + start - 1, 1), :]
            gf[hf, count + 1, j : j + 1, :] = ring[k, hf, pl.ds(PAD + start + count, 1), :]
        near[hf, :, 0:1, :] = cut[1][:, lanes].reshape(count, 1, LANES)
        far[hf, :, SUB - 1 : SUB, :] = cut[0][:, lanes].reshape(count, 1, LANES)

    def line(i, s):
        v = gr_ref[s, 0].astype(F32)
        for hf in range(2):
            gf[hf, i, PAD : PAD + cols, :] = v[:, hf * LANES : hf * LANES + LANES]

    @pl.when(step == 0)
    def _():
        line(1, 0)

    @pl.when(step == chunks - 1)
    def _():
        line(count, 2)

    for hf in range(2):
        lanes = slice(hf * LANES, hf * LANES + LANES)
        taps = [tap_at(tap_ref, hf, k) for k in range(9)]
        for jb in range(cols // 16):

            def body(it, carry):
                i = it * rows
                win = {}
                for q in range(rows):
                    pair = []
                    for half in range(2):
                        j = PAD + jb * 16 + half * SUB
                        total = None
                        for r in range(3):
                            for c in range(3):
                                at = (q + 2 - r, 2 - c, half)
                                if at not in win:
                                    win[at] = gf[hf, i + at[0], j - 1 + at[1] : j - 1 + at[1] + SUB, :]
                                term = taps[3 * r + c] * win[at]
                                total = term if total is None else total + term
                        if jb == 0 and half == 0:
                            total = total + near[hf, i + q]
                        if jb == cols // 16 - 1 and half == 1:
                            total = total + far[hf, i + q]
                        pair.append(total)
                    out_ref[0, i + q, jb * 16 : jb * 16 + 16, lanes] = jnp.concatenate(pair, axis=0).astype(BF16)
                return carry

            for it in range(count // rows):
                body(it, 0)

    def add(i, s):
        out_ref[0, i] = (out_ref[0, i].astype(F32) + from_dir(table, got, s).astype(F32)).astype(BF16)

    @pl.when(step == 0)
    def _():
        add(0, 0)

    @pl.when(step == chunks - 1)
    def _():
        add(count - 1, 2)


CHUNK = 16


def spread_call(first, steps, table, grad, ring, got, taps, into):
    batch, side, cols, channels = grad.shape
    chunks = side // CHUNK
    high = side - 1
    at = lambda i: ((i + first) // chunks, (i + first) % chunks)
    strips = pl.BlockSpec((4, 1, side, channels), lambda i: (0, at(i)[0], 0, 0))
    facing = pl.BlockSpec((1, side, channels), lambda i: (at(i)[0], 0, 0))
    rows = pl.BlockSpec((1, CHUNK, cols, channels), lambda i: (*at(i), 0, 0))
    in_specs = [
        pl.BlockSpec(memory_space=pltpu.SMEM),
        rows,
        pl.BlockSpec((1, 1, cols, channels), lambda i: (at(i)[0], jnp.maximum(at(i)[1] * CHUNK - 1, 0), 0, 0)),
        pl.BlockSpec((1, 1, cols, channels), lambda i: (at(i)[0], jnp.minimum(at(i)[1] * CHUNK + CHUNK, high), 0, 0)),
        strips,
        *[facing] * 4,
        pl.BlockSpec((9, channels), lambda i: (0, 0)),
    ]
    operands = [table, grad, grad, grad, ring, *got, taps]
    aliases = {}
    if into is not None:
        aliases = {len(operands): 0}
        in_specs.append(pl.BlockSpec(memory_space=pl.ANY))
        operands.append(into)

    def body(*refs):
        spread_body(4, first, *refs[:10], *refs[len(operands) :])

    return pl.pallas_call(
        body,
        grid=(steps,),
        in_specs=in_specs,
        out_specs=[rows, pl.BlockSpec((SUB, LANES), lambda i: (0, 0))],
        out_shape=[jax.ShapeDtypeStruct(grad.shape, BF16), jax.ShapeDtypeStruct((SUB, LANES), F32)],
        scratch_shapes=[
            pltpu.VMEM((2, CHUNK + 2, cols + 2 * PAD, LANES), F32),
            pltpu.VMEM((2, CHUNK, SUB, LANES), F32),
            pltpu.VMEM((2, CHUNK, SUB, LANES), F32),
            pltpu.VMEM((2, 2, side + 2 * PAD, LANES), F32),
            pltpu.VMEM((2, side, channels), BF16),
        ],
        input_output_aliases=aliases,
        compiler_params=pltpu.CompilerParams(vmem_limit_bytes=57 << 20),
        cost_estimate=pl.CostEstimate(
            flops=750_000_000 * steps, bytes_accessed=grad.size * 4 * steps // (batch * chunks), transcendentals=0
        ),
        name="spread",
    )(*operands)


def finish_body(scale, table, mine_ref, other_ref, dg_ref, bg_ref, pg_ref):
    rows = mine_ref.shape[0]
    channels = pg_ref.shape[0]
    own = mine_ref[...] * scale
    far = other_ref[...] * scale
    first = table[CORE] == 0
    low = jnp.where(first, own, far)
    high = jnp.where(first, far, own)
    pg_ref[0:rows, :] = low
    pg_ref[rows:channels, :] = high[: channels - rows]
    tail = high[channels - rows :]
    dg_ref[...] = tail[0:9]
    bg_ref[...] = tail[9:10]


def finish_call(scale, bit, mine, other):
    channels = mine.shape[1]
    vmem = pl.BlockSpec(memory_space=pltpu.VMEM)
    return pl.pallas_call(
        functools.partial(finish_body, scale),
        in_specs=[pl.BlockSpec(memory_space=pltpu.SMEM), vmem, vmem],
        out_specs=[vmem, vmem, vmem],
        out_shape=[
            jax.ShapeDtypeStruct((9, channels), F32),
            jax.ShapeDtypeStruct((1, channels), F32),
            jax.ShapeDtypeStruct((channels, channels), F32),
        ],
        name="finish",
    )(bit, mine, other)


def exchange(facing):
    faces, tiles = lax.axis_size("face"), lax.axis_size("tile")
    got = []
    for d, rows in enumerate(facing):
        pairs = []
        for i in range(faces * tiles):
            at = [i // tiles, i % tiles]
            k = d // 2
            step = 1 - 2 * (at[k] % 2)
            at[k] = (at[k] + (step if d % 2 == 0 else -step)) % (faces, tiles)[k]
            pairs.append((i, at[0] * tiles + at[1]))
        got.append(lax.ppermute(rows, ("face", "tile"), pairs))
    return got


def swap(value, mask):
    devices = lax.axis_size("face") * lax.axis_size("tile")
    return lax.ppermute(value, ("face", "tile"), [(i, i ^ mask) for i in range(devices)])


def after(value, *others):
    return lax.optimization_barrier((value, *others))[0]


def shards(
    state, cotangent, depth_weight, depth_bias, point_weight, tile_links, link_sides, link_flips, corner_masks
):
    batch, side, cols, channels = state.shape
    face_count = lax.axis_size("face")
    tile_count = lax.axis_size("tile")
    face_pos = lax.axis_index("face")
    tile_pos = lax.axis_index("tile")
    where = jnp.stack([face_pos, tile_pos])
    bias = depth_bias.reshape(1, channels)
    *edges, table = edges_call(where, tile_links, link_flips, corner_masks, state)
    got = exchange(edges)
    layer = (point_weight, depth_weight, bias)
    grad, point_sum, depth_sum = inner_call(state, cotangent, *layer)
    ring, *facing, mine, sent = ring_call(table, state, cotangent, got, *layer, point_sum, depth_sum)
    incoming = exchange(facing)

    first, field_grad = 0, None
    for stage, (mask_bits, steps) in enumerate(
        ((1, 0), (2, 2), (6, 2), (8, 2), (24, 3), (32, 2), (96, 3), (1, 2))
    ):
        got = swap(sent if stage == 0 else mine, mask_bits)
        if steps:
            held = after(depth_weight, mine)
            field_grad, token = spread_call(first, steps, table, grad, ring, incoming, held, field_grad)
            got = after(got, token)
            first += steps
        if stage < 7:
            mine = mine + got
    scale = float(batch * side * cols * face_count * tile_count) ** -0.5
    depth_grad, bias_grad, point_grad = finish_call(scale, table, mine, got)
    return field_grad, depth_grad, bias_grad.reshape(channels), point_grad


def solution(mesh):
    tiles = P(None, "face", "tile", None)
    table = P(("face", "tile"), None)
    return jax.shard_map(
        shards,
        mesh=mesh,
        in_specs=(tiles, tiles, P(), P(), P(), table, table, table, table),
        out_specs=(tiles, P(), P(), P()),
        check_vma=False,
    )
```

```python
import functools

import jax
import jax.numpy as jnp
from jax import lax
from jax.experimental import pallas as pl
from jax.experimental.pallas import tpu as pltpu
from jax.sharding import PartitionSpec as P

ROOT = 0.7978845608028654
CUBIC = 0.044715
F32 = jnp.float32
BF16 = jnp.bfloat16
LANES = 128
SUB = 8
PAD = 8


def gelu_pair(h):
    h2 = h * h
    s = 0.5 * jnp.tanh(h * ((CUBIC * ROOT) * h2 + ROOT)) + 0.5
    act = h * s
    slope = s + act * (1.0 - s) * ((6.0 * CUBIC * ROOT) * h2 + 2.0 * ROOT)
    return act, slope


ALPHA = (CUBIC * ROOT) ** (1.0 / 3.0)
KAPPA = ROOT / ALPHA


def gelu_scaled(h):
    h2 = h * h
    t = jnp.tanh(h * (h2 + KAPPA))
    up = 1.0 + t
    act = h * up
    return act, up + act * (1.0 - t) * (3.0 * h2 + KAPPA)


def tap_at(ref, hf, k):
    return jnp.broadcast_to(ref[k : k + 1, hf * LANES : hf * LANES + LANES], (SUB, LANES))


def inner_body(pairs, x_ref, cot_ref, w_ref, tap_ref, bias_ref, gh_ref, pg_out, dg_out, u, hide, acc, half_w, pg_ref, *bufs):
    step = pl.program_id(0)
    side = x_ref.shape[1]
    cols = x_ref.shape[2]
    sets = (bufs[0:4], bufs[4:8])

    @pl.when(step == 0)
    def _():
        for hf in range(2):
            for c in range(3):
                w0, w1, w2 = (tap_at(tap_ref, hf, 3 * r + c) * ALPHA for r in range(3))
                u[hf, c] = w0
                u[hf, 3 + c] = (w0 + w1 + w2) * 0.5
                u[hf, 6 + c] = (w0 - w1 + w2) * 0.5
                u[hf, 9 + c] = w2
            u[hf, 12] = tap_at(bias_ref, hf, 0) * ALPHA
        half_w[...] = w_ref[...] * jnp.asarray(0.5, BF16)
        for qt, _, _, _ in sets:
            edge = jnp.zeros((2, pairs, 4, PAD, LANES), F32)
            qt[:, :, :, 0:PAD, :] = edge
            qt[:, :, :, PAD + cols :, :] = edge
        col = lax.broadcasted_iota(jnp.int32, (cols, 2 * LANES), 0)
        keep = jnp.logical_and(col > 0, col < cols - 1)
        hide[0] = jnp.where(keep, 1.0, 0.0).astype(BF16)
        hide[1] = jnp.zeros((cols, 2 * LANES), BF16)
        acc[...] = jnp.zeros_like(acc)
        pg_ref[...] = jnp.zeros_like(pg_ref)

    rows = 2 * pairs

    def outer(buf):
        _, _, act, cot = buf
        pg_ref[...] += lax.dot_general(
            act[...], cot[...], (((0,), (0,)), ((), ())), preferred_element_type=F32
        )

    def chunk(t, buf):
        qt, ga, act, cot = buf
        base = t * rows
        for q in range(rows):
            i = base + q
            kind = jnp.where(jnp.logical_or(i == 0, i == side - 1), 1, 0)
            cot[q * cols : q * cols + cols, :] = cot_ref[0, i] * hide[kind]
        g = lax.dot_general(cot[...], half_w[...], (((1,), (1,)), ((), ())), preferred_element_type=F32)
        ga[0] = g[:, :LANES]
        ga[1] = g[:, LANES:]
        for hf in range(2):
            lanes = slice(hf * LANES, hf * LANES + LANES)
            line = [x_ref[0, jnp.maximum(base - 1, 0), :, lanes].astype(F32)]
            for q in range(rows):
                line.append(x_ref[0, base + q, :, lanes].astype(F32))
            line.append(x_ref[0, jnp.minimum(base + rows, side - 1), :, lanes].astype(F32))
            for p in range(pairs):
                q0, q1, q2, q3 = line[2 * p : 2 * p + 4]
                for k, v in enumerate((q0 - q2, q1 + q2, q2 - q1, q1 - q3)):
                    qt[hf, p, k, PAD : PAD + cols, :] = v
        for hf in range(2):
            lanes = slice(hf * LANES, hf * LANES + LANES)
            sums = [acc[hf, k] for k in range(13)]
            for p in range(pairs):
                for jb in range(cols // 16):
                    halves = []
                    for half in range(2):
                        j = jb * 16 + half * SUB
                        win = [
                            [qt[hf, p, k, PAD - 1 + j + c : PAD - 1 + j + c + SUB, :] for c in range(3)]
                            for k in range(4)
                        ]
                        m = []
                        for k in range(4):
                            v = u[hf, 3 * k] * win[k][0]
                            v = v + u[hf, 3 * k + 1] * win[k][1]
                            m.append(v + u[hf, 3 * k + 2] * win[k][2])
                        both = m[1] + u[hf, 12]
                        found = []
                        for q, h in enumerate((both + m[0] + m[2], both - m[2] - m[3])):
                            a, slope = gelu_scaled(h)
                            at = (2 * p + q) * cols + j
                            found.append((a, ga[hf, at : at + SUB, :] * slope))
                        g0, g1 = found[0][1], found[1][1]
                        plus, minus = g0 + g1, g0 - g1
                        for k, v in enumerate((g0, plus, minus, g1)):
                            for c in range(3):
                                sums[3 * k + c] = sums[3 * k + c] + v * win[k][c]
                        sums[12] = sums[12] + plus
                        halves.append(found)
                    for q in range(2):
                        at = (2 * p + q) * cols + jb * 16
                        act[at : at + 16, lanes] = jnp.concatenate(
                            [halves[0][q][0], halves[1][q][0]], axis=0
                        ).astype(BF16)
                        gh_ref[0, base + 2 * p + q, jb * 16 : jb * 16 + 16, lanes] = jnp.concatenate(
                            [halves[0][q][1], halves[1][q][1]], axis=0
                        ).astype(BF16)
            for k in range(13):
                acc[hf, k] = sums[k]

    def body(t, carry):
        chunk(2 * t, sets[0])
        outer(sets[1])
        chunk(2 * t + 1, sets[1])
        outer(sets[0])
        return carry

    sets[1][2][...] = jnp.zeros_like(sets[1][2])
    sets[1][3][...] = jnp.zeros_like(sets[1][3])
    lax.fori_loop(0, side // (2 * rows), body, 0)
    outer(sets[1])

    def tap_sums(hf):
        lines = [None] * 10
        for c in range(3):
            d1, d2, d3, d4 = (acc[hf, 3 * k + c] for k in range(4))
            even = 0.5 * (d2 + d3)
            lines[c] = d1 + even
            lines[3 + c] = 0.5 * (d2 - d3)
            lines[6 + c] = even - d4
        lines[9] = acc[hf, 12]
        return lines

    @pl.when(step == pl.num_programs(0) - 1)
    def _():
        point = pg_ref[...] * (0.5 / ALPHA)
        pg_out[...] = point
        for hf in range(2):
            for k, line in enumerate(tap_sums(hf)):
                dg_out[hf, k] = line


PAIRS = 4


def inner_call(state, cotangent, weight, taps, bias):
    batch, side, cols, channels = state.shape
    tile = pl.BlockSpec((1, side, cols, channels), lambda b: (b, 0, 0, 0))
    whole = lambda *shape: pl.BlockSpec(shape, lambda b: (0,) * len(shape))
    buf = [
        pltpu.VMEM((2, PAIRS, 4, cols + 2 * PAD, LANES), F32),
        pltpu.VMEM((2, 2 * PAIRS * cols, LANES), F32),
        pltpu.VMEM((2 * PAIRS * cols, channels), BF16),
        pltpu.VMEM((2 * PAIRS * cols, channels), BF16),
    ]
    square, lines = (channels, channels), (2, 10, SUB, LANES)
    shapes = (square, lines)
    return pl.pallas_call(
        functools.partial(inner_body, PAIRS),
        grid=(batch,),
        in_specs=[tile, tile, whole(*square), whole(9, channels), whole(1, channels)],
        out_specs=[tile, *(whole(*shape) for shape in shapes)],
        out_shape=[
            jax.ShapeDtypeStruct(state.shape, BF16),
            *(jax.ShapeDtypeStruct(shape, F32) for shape in shapes),
        ],
        scratch_shapes=[
            pltpu.VMEM((2, 13, SUB, LANES), F32),
            pltpu.VMEM((2, cols, channels), BF16),
            pltpu.VMEM((2, 13, SUB, LANES), F32),
            pltpu.VMEM(square, BF16),
            pltpu.VMEM(square, F32),
            *buf,
            *buf,
        ],
        compiler_params=pltpu.CompilerParams(vmem_limit_bytes=57 << 20),
        cost_estimate=pl.CostEstimate(
            flops=40_000_000_000, bytes_accessed=state.size * 6, transcendentals=state.size
        ),
        name="inner",
    )(state, cotangent, weight, taps, bias)


DIR_OF_SIDE, SIDE_OF_DIR, FLIPS, MASKS, CORE = 0, 4, 8, 12, 16


def from_dir(table, got, s, b=0):
    d = table[DIR_OF_SIDE + s]
    rows = got[3][b]
    for k in range(3):
        rows = jnp.where(d == k, got[k][b], rows)
    return rows


def turn(table, s, rows):
    count = rows.shape[0]
    i = lax.broadcasted_iota(jnp.int32, (count, count), 0)
    j = lax.broadcasted_iota(jnp.int32, (count, count), 1)
    source = jnp.where(table[FLIPS + s] == 1, count - 1 - i, i)
    pick = jnp.where(j == source, 1.0, 0.0).astype(BF16)
    return jnp.dot(pick, rows, preferred_element_type=F32).astype(BF16)


def columns(tile, buf, which):
    rows = tile.shape[0]
    flat = tile.astype(F32).reshape(rows * SUB, 2 * LANES)
    for hf in range(2):
        buf[hf] = flat[:, hf * LANES : hf * LANES + LANES]
    return [
        jnp.concatenate([buf[hf, pl.ds(c, rows, stride=SUB), :] for hf in range(2)], axis=1) for c in which
    ]


def edges_body(sizes, where, links, flips, masks, top_ref, low_ref, left_ref, right_ref, to0, to1, to2, to3, table, turned, wide):
    faces, tiles = sizes

    @pl.when(pl.program_id(0) == 0)
    def _():
        face, tile = where[0], where[1]
        face_step = 1 - 2 * lax.rem(face, 2)
        tile_step = 1 - 2 * lax.rem(tile, 2)
        towards = (
            (face + face_step) * tiles + tile,
            lax.rem(face - face_step + faces, faces) * tiles + tile,
            face * tiles + tile + tile_step,
            face * tiles + lax.rem(tile - tile_step + tiles, tiles),
        )
        met = [[jnp.where(links[0, s] == to, 1, 0) for to in towards] for s in range(4)]
        for k in range(4):
            table[DIR_OF_SIDE + k] = met[k][1] + 2 * met[k][2] + 3 * met[k][3]
            table[SIDE_OF_DIR + k] = met[1][k] + 2 * met[2][k] + 3 * met[3][k]
            table[FLIPS + k] = flips[0, k]
            table[MASKS + k] = masks[0, k]
        table[CORE] = lax.rem(tile, 2)

    last = right_ref.shape[2] - 1
    for b in range(top_ref.shape[0]):
        turned[b, 0] = turn(table, 0, top_ref[b, 0])
        turned[b, 1] = turn(table, 1, columns(right_ref[b], wide.at[0], (last,))[0].astype(BF16))
        turned[b, 2] = turn(table, 2, low_ref[b, 0])
        turned[b, 3] = turn(table, 3, columns(left_ref[b], wide.at[1], (0,))[0].astype(BF16))
    for b in range(top_ref.shape[0]):
        for d, to in enumerate((to0, to1, to2, to3)):
            to[b] = turned[b, table[SIDE_OF_DIR + d]]


EDGE_SAMPLES, RING_SAMPLES = 2, 2


def edges_call(where, links, flips, masks, state):
    batch, side, cols, channels = state.shape
    wide, held = 8, EDGE_SAMPLES
    one = lambda at: pl.BlockSpec((held, 1, cols, channels), lambda b: (b, at, 0, 0))
    column = lambda at: pl.BlockSpec((held, side, wide, channels), lambda b: (b, 0, at, 0))
    facing = pl.BlockSpec((held, side, channels), lambda b: (b, 0, 0))
    return pl.pallas_call(
        functools.partial(edges_body, (lax.axis_size("face"), lax.axis_size("tile"))),
        grid=(batch // held,),
        in_specs=[
            *[pl.BlockSpec(memory_space=pltpu.SMEM)] * 4,
            one(0),
            one(side - 1),
            column(0),
            column(cols // wide - 1),
        ],
        out_specs=[*[facing] * 4, pl.BlockSpec(memory_space=pltpu.SMEM)],
        out_shape=[
            *[jax.ShapeDtypeStruct((batch, side, channels), BF16)] * 4,
            jax.ShapeDtypeStruct((CORE + 1,), jnp.int32),
        ],
        scratch_shapes=[
            pltpu.VMEM((held, 4, side, channels), BF16),
            pltpu.VMEM((2, 2, side * SUB, LANES), F32),
        ],
        compiler_params=pltpu.CompilerParams(vmem_limit_bytes=57 << 20),
        name="edges",
    )(where, links, flips, masks, state, state, state, state)


LOW = (0, 1, 3, 0)
HIGH = (1, 2, 2, 3)


def ring_body(
    table, top_ref, low_ref, left_ref, right_ref, ctop_ref, clow_ref, cleft_ref, cright_ref,
    got0, got1, got2, got3, w_ref, tap_ref, bias_ref, pg_ref, dg_ref,
    gr_ref, to0, to1, to2, to3, mine, sent, strip, ext, acts, acc, turned, wide, point_ref,
):
    step = pl.program_id(0)
    side = got0.shape[1]
    got = (got0, got1, got2, got3)
    masks = [table[MASKS + k].astype(F32) for k in range(4)]

    @pl.when(step == 0)
    def _():
        acc[...] = dg_ref[...]
        point_ref[...] = pg_ref[...]
        ext[...] = jnp.zeros_like(ext)

    def sample(n):
        rims = [from_dir(table, got, s, n).astype(F32) for s in range(4)]
        top = top_ref[n].astype(F32)
        low = low_ref[n].astype(F32)
        last = SUB - 1
        left = columns(left_ref[n], wide.at[0], (0, 1))
        right = columns(right_ref[n], wide.at[1], (last - 1, last))
        end = side - 1

        def corner(k, first, second):
            return (masks[k] * 0.5 * (first + second)).astype(BF16).astype(F32)

        def at(s, i):
            return rims[s][i : i + 1]

        nw = corner(0, at(0, 0), at(3, 0))
        ne = corner(1, at(0, end), at(1, 0))
        se = corner(2, at(1, end), at(2, end))
        sw = corner(3, at(2, 0), at(3, end))
        lines = (
            ((rims[0], nw, ne), (top[0], at(3, 0), at(1, 0)), (top[1], at(3, 1), at(1, 1))),
            (
                (right[0], at(0, end - 1), at(2, end - 1)),
                (right[1], at(0, end), at(2, end)),
                (rims[1], ne, se),
            ),
            (
                (low[0], at(3, end - 1), at(1, end - 1)),
                (low[1], at(3, end), at(1, end)),
                (rims[2], sw, se),
            ),
            ((rims[3], nw, sw), (left[0], at(0, 0), at(2, 0)), (left[1], at(0, 1), at(2, 1))),
        )
        for s in range(4):
            for a in range(3):
                line, before, after = lines[s][a]
                for hf in range(2):
                    lanes = slice(hf * LANES, hf * LANES + LANES)
                    strip[n, s, hf, a, PAD : PAD + side, :] = line[:, lanes]
                    strip[n, s, hf, a, PAD - 1 : PAD, :] = before[:, lanes]
                    strip[n, s, hf, a, PAD + side : PAD + side + 1, :] = after[:, lanes]
        cots = jnp.concatenate(
            [
                ctop_ref[n, 0].astype(F32),
                columns(cright_ref[n], wide.at[2], (last,))[0],
                clow_ref[n, 0].astype(F32),
                columns(cleft_ref[n], wide.at[3], (0,))[0],
            ],
            axis=0,
        ).astype(BF16)
        ga = lax.dot_general(cots, w_ref[...], (((1,), (1,)), ((), ())), preferred_element_type=F32)
        row = lax.broadcasted_iota(jnp.int32, (side, LANES), 0)
        middle = jnp.logical_and(row > 0, row < end)
        for s in range(4):
            upright = s % 2 == 0
            rim_line = 0 if s in (0, 3) else 2
            for hf in range(2):
                lanes = slice(hf * LANES, hf * LANES + LANES)

                def tap(a, b):
                    k = 3 * a + b if upright else 3 * b + a
                    return k, tap_ref[k : k + 1, lanes]

                h = jnp.zeros((side, LANES), F32) + bias_ref[0:1, lanes]
                for a in range(3):
                    for b in range(3):
                        h = h + tap(a, b)[1] * strip[n, s, hf, a, PAD - 1 + b : PAD - 1 + b + side, :]
                act, slope = gelu_pair(h)
                g = (ga[s * side : s * side + side, lanes] * slope).astype(BF16)
                gr_ref[s, n, :, lanes] = g
                g = g.astype(F32)
                counted = g
                if not upright:
                    counted = jnp.where(middle, g, 0.0)
                    act = jnp.where(middle, act, 0.0)
                acts[n, s * side : s * side + side, lanes] = act.astype(BF16)
                for a in range(3):
                    for b in range(3):
                        k = tap(a, b)[0]
                        term = counted * strip[n, s, hf, a, PAD - 1 + b : PAD - 1 + b + side, :]
                        acc[hf, k] += jnp.sum(term.reshape(side // SUB, SUB, LANES), axis=0)
                acc[hf, 9] += jnp.sum(counted.reshape(side // SUB, SUB, LANES), axis=0)
                ext[n, PAD : PAD + side, :] = g
                first, mid, final = (tap(rim_line, b)[1] for b in range(3))
                back = (
                    first * ext[n, PAD + 1 : PAD + 1 + side, :]
                    + mid * g
                    + final * ext[n, PAD - 1 : PAD - 1 + side, :]
                )
                back = back + jnp.where(row == 0, (0.5 * masks[LOW[s]]) * first * g, 0.0)
                back = back + jnp.where(row == end, (0.5 * masks[HIGH[s]]) * final * g, 0.0)
                turned[n, s, :, lanes] = turn(table, s, back.astype(BF16))
        for d, to in enumerate((to0, to1, to2, to3)):
            to[n] = turned[n, table[SIDE_OF_DIR + d]]
        point_ref[...] += lax.dot_general(acts[n], cots, (((0,), (0,)), ((), ())), preferred_element_type=F32)

    for n in range(got0.shape[0]):
        sample(n)

    @pl.when(step == pl.num_programs(0) - 1)
    def _():
        rows = mine.shape[0]
        lines = []
        for hf in range(2):
            own = [jnp.sum(acc[hf, k], axis=0, keepdims=True) for k in range(10)]
            lines.append(jnp.concatenate(own + [jnp.zeros((6, LANES), F32)], axis=0))
        low = point_ref[0:rows]
        high = jnp.concatenate([point_ref[rows:], jnp.concatenate(lines, axis=1)], axis=0)
        first = table[CORE] == 0
        mine[...] = jnp.where(first, low, high)
        sent[...] = jnp.where(first, high, low)


def ring_call(table, state, cotangent, got, weight, taps, bias, point_inner, depth_inner):
    batch, side, cols, channels = state.shape
    wide, held, half = 8, RING_SAMPLES, (channels + 16) // 2
    two = lambda at: pl.BlockSpec((held, 2, cols, channels), lambda b: (b, at, 0, 0))
    one = lambda at: pl.BlockSpec((held, 1, cols, channels), lambda b: (b, at, 0, 0))
    column = lambda at: pl.BlockSpec((held, side, wide, channels), lambda b: (b, 0, at, 0))
    strips = pl.BlockSpec((4, held, side, channels), lambda b: (0, b, 0, 0))
    facing = pl.BlockSpec((held, side, channels), lambda b: (b, 0, 0))
    far = cols // wide - 1
    return pl.pallas_call(
        ring_body,
        grid=(batch // held,),
        in_specs=[
            pl.BlockSpec(memory_space=pltpu.SMEM),
            two(0),
            two(side // 2 - 1),
            column(0),
            column(far),
            one(0),
            one(side - 1),
            column(0),
            column(far),
            *[facing] * 4,
            pl.BlockSpec((channels, channels), lambda b: (0, 0)),
            pl.BlockSpec((9, channels), lambda b: (0, 0)),
            pl.BlockSpec((1, channels), lambda b: (0, 0)),
            pl.BlockSpec((channels, channels), lambda b: (0, 0)),
            pl.BlockSpec((2, 10, SUB, LANES), lambda b: (0, 0, 0, 0)),
        ],
        out_specs=[
            strips,
            *[facing] * 4,
            *[pl.BlockSpec((half, channels), lambda b: (0, 0))] * 2,
        ],
        out_shape=[
            jax.ShapeDtypeStruct((4, batch, side, channels), BF16),
            *[jax.ShapeDtypeStruct((batch, side, channels), BF16)] * 4,
            *[jax.ShapeDtypeStruct((half, channels), F32)] * 2,
        ],
        scratch_shapes=[
            pltpu.VMEM((held, 4, 2, 3, cols + 2 * PAD, LANES), F32),
            pltpu.VMEM((held, cols + 2 * PAD, LANES), F32),
            pltpu.VMEM((held, 4 * side, channels), BF16),
            pltpu.VMEM((2, 10, SUB, LANES), F32),
            pltpu.VMEM((held, 4, side, channels), BF16),
            pltpu.VMEM((4, 2, side * SUB, LANES), F32),
            pltpu.VMEM((channels, channels), F32),
        ],
        compiler_params=pltpu.CompilerParams(vmem_limit_bytes=57 << 20),
        cost_estimate=pl.CostEstimate(
            flops=3_000_000_000, bytes_accessed=12 << 20, transcendentals=state.size // 16
        ),
        name="ring",
    )(table, state, state, state, state, cotangent, cotangent, cotangent, cotangent, *got, weight, taps, bias,
      point_inner, depth_inner)


def spread_body(rows, first, table, gh_ref, above_ref, below_ref, gr_ref, got0, got1, got2, got3, tap_ref, out_ref, token_ref, gf, near, far, ring, back):
    got = (got0, got1, got2, got3)
    side = gr_ref.shape[2]
    cols = gh_ref.shape[2]
    count = gh_ref.shape[1]
    chunks = side // count
    step = (pl.program_id(0) + first) % chunks
    token_ref[...] = jnp.zeros_like(token_ref)
    start = step * count

    @pl.when(jnp.logical_or(pl.program_id(0) == 0, step == 0))
    def _():
        for k, s in enumerate((1, 3)):
            back[k] = from_dir(table, got, s)
        for hf in range(2):
            lanes = slice(hf * LANES, hf * LANES + LANES)
            gf[hf, :, 0:PAD, :] = jnp.zeros((count + 2, PAD, LANES), F32)
            gf[hf, :, PAD + cols : 2 * PAD + cols, :] = jnp.zeros((count + 2, PAD, LANES), F32)
            for k, s in enumerate((1, 3)):
                ring[k, hf, 0:PAD, :] = jnp.zeros((PAD, LANES), F32)
                ring[k, hf, PAD + side :, :] = jnp.zeros((PAD, LANES), F32)
                ring[k, hf, PAD : PAD + side, :] = gr_ref[s, 0, :, lanes].astype(F32)
        near[...] = jnp.zeros_like(near)
        far[...] = jnp.zeros_like(far)

    def put(i, v):
        v = v.astype(F32)
        gf[0, i, PAD : PAD + cols, :] = v[:, :LANES]
        gf[1, i, PAD : PAD + cols, :] = v[:, LANES:]

    put(0, jnp.where(step > 0, above_ref[0, 0], jnp.zeros_like(above_ref[0, 0])))
    put(count + 1, jnp.where(step < chunks - 1, below_ref[0, 0], jnp.zeros_like(below_ref[0, 0])))
    for i in range(count):
        put(i + 1, gh_ref[0, i])
    cut = [back[k, pl.ds(pl.multiple_of(start, count), count), :].astype(F32) for k in range(2)]
    for hf in range(2):
        lanes = slice(hf * LANES, hf * LANES + LANES)
        for k, j in ((0, PAD + cols - 1), (1, PAD)):
            own = ring[k, hf, pl.ds(pl.multiple_of(PAD + start, SUB), count), :]
            gf[hf, 1 : count + 1, j : j + 1, :] = own.reshape(count, 1, LANES)
            gf[hf, 0, j : j + 1, :] = ring[k, hf, pl.ds(PAD + start - 1, 1), :]
            gf[hf, count + 1, j : j + 1, :] = ring[k, hf, pl.ds(PAD + start + count, 1), :]
        near[hf, :, 0:1, :] = cut[1][:, lanes].reshape(count, 1, LANES)
        far[hf, :, SUB - 1 : SUB, :] = cut[0][:, lanes].reshape(count, 1, LANES)

    def line(i, s):
        v = gr_ref[s, 0].astype(F32)
        for hf in range(2):
            gf[hf, i, PAD : PAD + cols, :] = v[:, hf * LANES : hf * LANES + LANES]

    @pl.when(step == 0)
    def _():
        line(1, 0)

    @pl.when(step == chunks - 1)
    def _():
        line(count, 2)

    for hf in range(2):
        lanes = slice(hf * LANES, hf * LANES + LANES)
        taps = [tap_at(tap_ref, hf, k) for k in range(9)]
        for jb in range(cols // 16):

            def body(it, carry):
                i = it * rows
                win = {}
                for q in range(rows):
                    pair = []
                    for half in range(2):
                        j = PAD + jb * 16 + half * SUB
                        total = None
                        for r in range(3):
                            for c in range(3):
                                at = (q + 2 - r, 2 - c, half)
                                if at not in win:
                                    win[at] = gf[hf, i + at[0], j - 1 + at[1] : j - 1 + at[1] + SUB, :]
                                term = taps[3 * r + c] * win[at]
                                total = term if total is None else total + term
                        if jb == 0 and half == 0:
                            total = total + near[hf, i + q]
                        if jb == cols // 16 - 1 and half == 1:
                            total = total + far[hf, i + q]
                        pair.append(total)
                    out_ref[0, i + q, jb * 16 : jb * 16 + 16, lanes] = jnp.concatenate(pair, axis=0).astype(BF16)
                return carry

            for it in range(count // rows):
                body(it, 0)

    def add(i, s):
        out_ref[0, i] = (out_ref[0, i].astype(F32) + from_dir(table, got, s).astype(F32)).astype(BF16)

    @pl.when(step == 0)
    def _():
        add(0, 0)

    @pl.when(step == chunks - 1)
    def _():
        add(count - 1, 2)


CHUNK = 16


def spread_call(first, steps, table, grad, ring, got, taps, into):
    batch, side, cols, channels = grad.shape
    chunks = side // CHUNK
    high = side - 1
    at = lambda i: ((i + first) // chunks, (i + first) % chunks)
    strips = pl.BlockSpec((4, 1, side, channels), lambda i: (0, at(i)[0], 0, 0))
    facing = pl.BlockSpec((1, side, channels), lambda i: (at(i)[0], 0, 0))
    rows = pl.BlockSpec((1, CHUNK, cols, channels), lambda i: (*at(i), 0, 0))
    in_specs = [
        pl.BlockSpec(memory_space=pltpu.SMEM),
        rows,
        pl.BlockSpec((1, 1, cols, channels), lambda i: (at(i)[0], jnp.maximum(at(i)[1] * CHUNK - 1, 0), 0, 0)),
        pl.BlockSpec((1, 1, cols, channels), lambda i: (at(i)[0], jnp.minimum(at(i)[1] * CHUNK + CHUNK, high), 0, 0)),
        strips,
        *[facing] * 4,
        pl.BlockSpec((9, channels), lambda i: (0, 0)),
    ]
    operands = [table, grad, grad, grad, ring, *got, taps]
    aliases = {}
    if into is not None:
        aliases = {len(operands): 0}
        in_specs.append(pl.BlockSpec(memory_space=pl.ANY))
        operands.append(into)

    def body(*refs):
        spread_body(4, first, *refs[:10], *refs[len(operands) :])

    return pl.pallas_call(
        body,
        grid=(steps,),
        in_specs=in_specs,
        out_specs=[rows, pl.BlockSpec((SUB, LANES), lambda i: (0, 0))],
        out_shape=[jax.ShapeDtypeStruct(grad.shape, BF16), jax.ShapeDtypeStruct((SUB, LANES), F32)],
        scratch_shapes=[
            pltpu.VMEM((2, CHUNK + 2, cols + 2 * PAD, LANES), F32),
            pltpu.VMEM((2, CHUNK, SUB, LANES), F32),
            pltpu.VMEM((2, CHUNK, SUB, LANES), F32),
            pltpu.VMEM((2, 2, side + 2 * PAD, LANES), F32),
            pltpu.VMEM((2, side, channels), BF16),
        ],
        input_output_aliases=aliases,
        compiler_params=pltpu.CompilerParams(vmem_limit_bytes=57 << 20),
        cost_estimate=pl.CostEstimate(
            flops=750_000_000 * steps, bytes_accessed=grad.size * 4 * steps // (batch * chunks), transcendentals=0
        ),
        name="spread",
    )(*operands)


def exchange(facing):
    faces, tiles = lax.axis_size("face"), lax.axis_size("tile")
    got = []
    for d, rows in enumerate(facing):
        pairs = []
        for i in range(faces * tiles):
            at = [i // tiles, i % tiles]
            k = d // 2
            step = 1 - 2 * (at[k] % 2)
            at[k] = (at[k] + (step if d % 2 == 0 else -step)) % (faces, tiles)[k]
            pairs.append((i, at[0] * tiles + at[1]))
        got.append(lax.ppermute(rows, ("face", "tile"), pairs))
    return got


def swap(value, mask):
    devices = lax.axis_size("face") * lax.axis_size("tile")
    return lax.ppermute(value, ("face", "tile"), [(i, i ^ mask) for i in range(devices)])


def after(value, *others):
    return lax.optimization_barrier((value, *others))[0]


def shards(
    state, cotangent, depth_weight, depth_bias, point_weight, tile_links, link_sides, link_flips, corner_masks
):
    batch, side, cols, channels = state.shape
    face_count = lax.axis_size("face")
    tile_count = lax.axis_size("tile")
    face_pos = lax.axis_index("face")
    tile_pos = lax.axis_index("tile")
    where = jnp.stack([face_pos, tile_pos])
    bias = depth_bias.reshape(1, channels)
    *edges, table = edges_call(where, tile_links, link_flips, corner_masks, state)
    got = exchange(edges)
    layer = (point_weight, depth_weight, bias)
    grad, point_sum, depth_sum = inner_call(state, cotangent, *layer)
    ring, *facing, mine, sent = ring_call(table, state, cotangent, got, *layer, point_sum, depth_sum)
    incoming = exchange(facing)

    first, field_grad = 0, None
    for stage, (mask_bits, steps) in enumerate(((1, 0), (2, 2), (6, 3), (8, 2), (24, 3), (32, 3), (96, 3))):
        last = mask_bits == 96
        got = [swap(sent if stage == 0 else mine, bits) for bits in ((96, 1, 97) if last else (mask_bits,))]
        if steps:
            held = after(depth_weight, mine)
            field_grad, token = spread_call(first, steps, table, grad, ring, incoming, held, field_grad)
            got = lax.optimization_barrier((*got, token))[:-1]
            first += steps
        mine = mine + got[0]
    other = got[1] + got[2]
    scale = float(batch * side * cols * face_count * tile_count) ** -0.5
    core = tile_pos % 2
    rows = channels - mine.shape[0]
    low = jnp.where(core == 0, mine, other) * scale
    high = jnp.where(core == 0, other, mine) * scale
    point_grad = jnp.concatenate([low, high[:rows]], axis=0)
    return field_grad, high[rows : rows + 9], high[rows + 9], point_grad


def solution(mesh):
    tiles = P(None, "face", "tile", None)
    table = P(("face", "tile"), None)
    return jax.shard_map(
        shards,
        mesh=mesh,
        in_specs=(tiles, tiles, P(), P(), P(), table, table, table, table),
        out_specs=(tiles, P(), P(), P()),
        check_vma=False,
    )
```

```python
import functools

import jax
import jax.numpy as jnp
from jax import lax
from jax.experimental import pallas as pl
from jax.experimental.pallas import tpu as pltpu
from jax.sharding import PartitionSpec as P

ROOT = 0.7978845608028654
CUBIC = 0.044715
F32 = jnp.float32
BF16 = jnp.bfloat16
LANES = 128
SUB = 8
PAD = 8


def gelu_pair(h):
    h2 = h * h
    s = 0.5 * jnp.tanh(h * ((CUBIC * ROOT) * h2 + ROOT)) + 0.5
    act = h * s
    slope = s + act * (1.0 - s) * ((6.0 * CUBIC * ROOT) * h2 + 2.0 * ROOT)
    return act, slope


ALPHA = (CUBIC * ROOT) ** (1.0 / 3.0)
KAPPA = ROOT / ALPHA


def gelu_scaled(h):
    h2 = h * h
    t = jnp.tanh(h * (h2 + KAPPA))
    up = 1.0 + t
    act = h * up
    return act, up + act * (1.0 - t) * (3.0 * h2 + KAPPA)


def tap_at(ref, hf, k):
    return jnp.broadcast_to(ref[k : k + 1, hf * LANES : hf * LANES + LANES], (SUB, LANES))


def inner_body(pairs, x_ref, cot_ref, w_ref, tap_ref, bias_ref, gh_ref, pg_out, dg_out, u, hide, acc, half_w, pg_ref, *bufs):
    step = pl.program_id(0)
    side = x_ref.shape[1]
    cols = x_ref.shape[2]
    sets = (bufs[0:4], bufs[4:8])

    @pl.when(step == 0)
    def _():
        for hf in range(2):
            for c in range(3):
                w0, w1, w2 = (tap_at(tap_ref, hf, 3 * r + c) * ALPHA for r in range(3))
                u[hf, c] = w0
                u[hf, 3 + c] = (w0 + w1 + w2) * 0.5
                u[hf, 6 + c] = (w0 - w1 + w2) * 0.5
                u[hf, 9 + c] = w2
            u[hf, 12] = tap_at(bias_ref, hf, 0) * ALPHA
        half_w[...] = w_ref[...] * jnp.asarray(0.5, BF16)
        for qt, _, _, _ in sets:
            edge = jnp.zeros((2, pairs, 4, PAD, LANES), F32)
            qt[:, :, :, 0:PAD, :] = edge
            qt[:, :, :, PAD + cols :, :] = edge
        col = lax.broadcasted_iota(jnp.int32, (cols, 2 * LANES), 0)
        keep = jnp.logical_and(col > 0, col < cols - 1)
        hide[0] = jnp.where(keep, 1.0, 0.0).astype(BF16)
        hide[1] = jnp.zeros((cols, 2 * LANES), BF16)
        acc[...] = jnp.zeros_like(acc)
        pg_ref[...] = jnp.zeros_like(pg_ref)

    rows = 2 * pairs

    def outer(buf):
        _, _, act, cot = buf
        pg_ref[...] += lax.dot_general(
            act[...], cot[...], (((0,), (0,)), ((), ())), preferred_element_type=F32
        )

    def chunk(t, buf):
        qt, ga, act, cot = buf
        base = t * rows
        for q in range(rows):
            i = base + q
            kind = jnp.where(jnp.logical_or(i == 0, i == side - 1), 1, 0)
            cot[q * cols : q * cols + cols, :] = cot_ref[0, i] * hide[kind]
        g = lax.dot_general(cot[...], half_w[...], (((1,), (1,)), ((), ())), preferred_element_type=F32)
        ga[0] = g[:, :LANES]
        ga[1] = g[:, LANES:]
        for hf in range(2):
            lanes = slice(hf * LANES, hf * LANES + LANES)
            line = [x_ref[0, jnp.maximum(base - 1, 0), :, lanes].astype(F32)]
            for q in range(rows):
                line.append(x_ref[0, base + q, :, lanes].astype(F32))
            line.append(x_ref[0, jnp.minimum(base + rows, side - 1), :, lanes].astype(F32))
            for p in range(pairs):
                q0, q1, q2, q3 = line[2 * p : 2 * p + 4]
                for k, v in enumerate((q0 - q2, q1 + q2, q2 - q1, q1 - q3)):
                    qt[hf, p, k, PAD : PAD + cols, :] = v
        for hf in range(2):
            lanes = slice(hf * LANES, hf * LANES + LANES)
            sums = [acc[hf, k] for k in range(13)]
            for p in range(pairs):
                for jb in range(cols // 16):
                    halves = []
                    for half in range(2):
                        j = jb * 16 + half * SUB
                        win = [
                            [qt[hf, p, k, PAD - 1 + j + c : PAD - 1 + j + c + SUB, :] for c in range(3)]
                            for k in range(4)
                        ]
                        m = []
                        for k in range(4):
                            v = u[hf, 3 * k] * win[k][0]
                            v = v + u[hf, 3 * k + 1] * win[k][1]
                            m.append(v + u[hf, 3 * k + 2] * win[k][2])
                        both = m[1] + u[hf, 12]
                        found = []
                        for q, h in enumerate((both + m[0] + m[2], both - m[2] - m[3])):
                            a, slope = gelu_scaled(h)
                            at = (2 * p + q) * cols + j
                            found.append((a, ga[hf, at : at + SUB, :] * slope))
                        g0, g1 = found[0][1], found[1][1]
                        plus, minus = g0 + g1, g0 - g1
                        for k, v in enumerate((g0, plus, minus, g1)):
                            for c in range(3):
                                sums[3 * k + c] = sums[3 * k + c] + v * win[k][c]
                        sums[12] = sums[12] + plus
                        halves.append(found)
                    for q in range(2):
                        at = (2 * p + q) * cols + jb * 16
                        act[at : at + 16, lanes] = jnp.concatenate(
                            [halves[0][q][0], halves[1][q][0]], axis=0
                        ).astype(BF16)
                        gh_ref[0, base + 2 * p + q, jb * 16 : jb * 16 + 16, lanes] = jnp.concatenate(
                            [halves[0][q][1], halves[1][q][1]], axis=0
                        ).astype(BF16)
            for k in range(13):
                acc[hf, k] = sums[k]

    def body(t, carry):
        chunk(2 * t, sets[0])
        outer(sets[1])
        chunk(2 * t + 1, sets[1])
        outer(sets[0])
        return carry

    sets[1][2][...] = jnp.zeros_like(sets[1][2])
    sets[1][3][...] = jnp.zeros_like(sets[1][3])
    lax.fori_loop(0, side // (2 * rows), body, 0)
    outer(sets[1])

    def tap_sums(hf):
        lines = [None] * 10
        for c in range(3):
            d1, d2, d3, d4 = (acc[hf, 3 * k + c] for k in range(4))
            even = 0.5 * (d2 + d3)
            lines[c] = d1 + even
            lines[3 + c] = 0.5 * (d2 - d3)
            lines[6 + c] = even - d4
        lines[9] = acc[hf, 12]
        return lines

    @pl.when(step == pl.num_programs(0) - 1)
    def _():
        point = pg_ref[...] * (0.5 / ALPHA)
        pg_out[...] = point
        for hf in range(2):
            for k, line in enumerate(tap_sums(hf)):
                dg_out[hf, k] = line


PAIRS = 4


def inner_call(state, cotangent, weight, taps, bias):
    batch, side, cols, channels = state.shape
    tile = pl.BlockSpec((1, side, cols, channels), lambda b: (b, 0, 0, 0))
    whole = lambda *shape: pl.BlockSpec(shape, lambda b: (0,) * len(shape))
    buf = [
        pltpu.VMEM((2, PAIRS, 4, cols + 2 * PAD, LANES), F32),
        pltpu.VMEM((2, 2 * PAIRS * cols, LANES), F32),
        pltpu.VMEM((2 * PAIRS * cols, channels), BF16),
        pltpu.VMEM((2 * PAIRS * cols, channels), BF16),
    ]
    square, lines = (channels, channels), (2, 10, SUB, LANES)
    shapes = (square, lines)
    return pl.pallas_call(
        functools.partial(inner_body, PAIRS),
        grid=(batch,),
        in_specs=[tile, tile, whole(*square), whole(9, channels), whole(1, channels)],
        out_specs=[tile, *(whole(*shape) for shape in shapes)],
        out_shape=[
            jax.ShapeDtypeStruct(state.shape, BF16),
            *(jax.ShapeDtypeStruct(shape, F32) for shape in shapes),
        ],
        scratch_shapes=[
            pltpu.VMEM((2, 13, SUB, LANES), F32),
            pltpu.VMEM((2, cols, channels), BF16),
            pltpu.VMEM((2, 13, SUB, LANES), F32),
            pltpu.VMEM(square, BF16),
            pltpu.VMEM(square, F32),
            *buf,
            *buf,
        ],
        compiler_params=pltpu.CompilerParams(vmem_limit_bytes=57 << 20),
        cost_estimate=pl.CostEstimate(
            flops=40_000_000_000, bytes_accessed=state.size * 6, transcendentals=state.size
        ),
        name="inner",
    )(state, cotangent, weight, taps, bias)


DIR_OF_SIDE, SIDE_OF_DIR, FLIPS, MASKS, CORE = 0, 4, 8, 12, 16


def from_dir(table, got, s, b=0):
    d = table[DIR_OF_SIDE + s]
    rows = got[3][b]
    for k in range(3):
        rows = jnp.where(d == k, got[k][b], rows)
    return rows


def turn(table, s, rows):
    count = rows.shape[0]
    i = lax.broadcasted_iota(jnp.int32, (count, count), 0)
    j = lax.broadcasted_iota(jnp.int32, (count, count), 1)
    source = jnp.where(table[FLIPS + s] == 1, count - 1 - i, i)
    pick = jnp.where(j == source, 1.0, 0.0).astype(BF16)
    return jnp.dot(pick, rows, preferred_element_type=F32).astype(BF16)


def columns(tile, buf, which):
    rows = tile.shape[0]
    flat = tile.astype(F32).reshape(rows * SUB, 2 * LANES)
    for hf in range(2):
        buf[hf] = flat[:, hf * LANES : hf * LANES + LANES]
    return [
        jnp.concatenate([buf[hf, pl.ds(c, rows, stride=SUB), :] for hf in range(2)], axis=1) for c in which
    ]


def edges_body(sizes, where, links, flips, masks, top_ref, low_ref, left_ref, right_ref, to0, to1, to2, to3, table, turned, wide):
    faces, tiles = sizes

    @pl.when(pl.program_id(0) == 0)
    def _():
        face, tile = where[0], where[1]
        face_step = 1 - 2 * lax.rem(face, 2)
        tile_step = 1 - 2 * lax.rem(tile, 2)
        towards = (
            (face + face_step) * tiles + tile,
            lax.rem(face - face_step + faces, faces) * tiles + tile,
            face * tiles + tile + tile_step,
            face * tiles + lax.rem(tile - tile_step + tiles, tiles),
        )
        met = [[jnp.where(links[0, s] == to, 1, 0) for to in towards] for s in range(4)]
        for k in range(4):
            table[DIR_OF_SIDE + k] = met[k][1] + 2 * met[k][2] + 3 * met[k][3]
            table[SIDE_OF_DIR + k] = met[1][k] + 2 * met[2][k] + 3 * met[3][k]
            table[FLIPS + k] = flips[0, k]
            table[MASKS + k] = masks[0, k]
        table[CORE] = lax.rem(tile, 2)

    last = right_ref.shape[2] - 1
    for b in range(top_ref.shape[0]):
        turned[b, 0] = turn(table, 0, top_ref[b, 0])
        turned[b, 1] = turn(table, 1, columns(right_ref[b], wide.at[0], (last,))[0].astype(BF16))
        turned[b, 2] = turn(table, 2, low_ref[b, 0])
        turned[b, 3] = turn(table, 3, columns(left_ref[b], wide.at[1], (0,))[0].astype(BF16))
    for b in range(top_ref.shape[0]):
        for d, to in enumerate((to0, to1, to2, to3)):
            to[b] = turned[b, table[SIDE_OF_DIR + d]]


EDGE_SAMPLES, RING_SAMPLES = 2, 2


def edges_call(where, links, flips, masks, state):
    batch, side, cols, channels = state.shape
    wide, held = 8, EDGE_SAMPLES
    one = lambda at: pl.BlockSpec((held, 1, cols, channels), lambda b: (b, at, 0, 0))
    column = lambda at: pl.BlockSpec((held, side, wide, channels), lambda b: (b, 0, at, 0))
    facing = pl.BlockSpec((held, side, channels), lambda b: (b, 0, 0))
    return pl.pallas_call(
        functools.partial(edges_body, (lax.axis_size("face"), lax.axis_size("tile"))),
        grid=(batch // held,),
        in_specs=[
            *[pl.BlockSpec(memory_space=pltpu.SMEM)] * 4,
            one(0),
            one(side - 1),
            column(0),
            column(cols // wide - 1),
        ],
        out_specs=[*[facing] * 4, pl.BlockSpec(memory_space=pltpu.SMEM)],
        out_shape=[
            *[jax.ShapeDtypeStruct((batch, side, channels), BF16)] * 4,
            jax.ShapeDtypeStruct((CORE + 1,), jnp.int32),
        ],
        scratch_shapes=[
            pltpu.VMEM((held, 4, side, channels), BF16),
            pltpu.VMEM((2, 2, side * SUB, LANES), F32),
        ],
        compiler_params=pltpu.CompilerParams(vmem_limit_bytes=57 << 20),
        name="edges",
    )(where, links, flips, masks, state, state, state, state)


LOW = (0, 1, 3, 0)
HIGH = (1, 2, 2, 3)


def ring_body(
    table, top_ref, low_ref, left_ref, right_ref, ctop_ref, clow_ref, cleft_ref, cright_ref,
    got0, got1, got2, got3, w_ref, tap_ref, bias_ref, pg_ref, dg_ref,
    gr_ref, to0, to1, to2, to3, mine, sent, strip, ext, acts, acc, turned, wide, point_ref,
):
    step = pl.program_id(0)
    side = got0.shape[1]
    got = (got0, got1, got2, got3)
    masks = [table[MASKS + k].astype(F32) for k in range(4)]

    @pl.when(step == 0)
    def _():
        acc[...] = dg_ref[...]
        point_ref[...] = pg_ref[...]
        ext[...] = jnp.zeros_like(ext)

    def sample(n):
        rims = [from_dir(table, got, s, n).astype(F32) for s in range(4)]
        top = top_ref[n].astype(F32)
        low = low_ref[n].astype(F32)
        last = SUB - 1
        left = columns(left_ref[n], wide.at[0], (0, 1))
        right = columns(right_ref[n], wide.at[1], (last - 1, last))
        end = side - 1

        def corner(k, first, second):
            return (masks[k] * 0.5 * (first + second)).astype(BF16).astype(F32)

        def at(s, i):
            return rims[s][i : i + 1]

        nw = corner(0, at(0, 0), at(3, 0))
        ne = corner(1, at(0, end), at(1, 0))
        se = corner(2, at(1, end), at(2, end))
        sw = corner(3, at(2, 0), at(3, end))
        lines = (
            ((rims[0], nw, ne), (top[0], at(3, 0), at(1, 0)), (top[1], at(3, 1), at(1, 1))),
            (
                (right[0], at(0, end - 1), at(2, end - 1)),
                (right[1], at(0, end), at(2, end)),
                (rims[1], ne, se),
            ),
            (
                (low[0], at(3, end - 1), at(1, end - 1)),
                (low[1], at(3, end), at(1, end)),
                (rims[2], sw, se),
            ),
            ((rims[3], nw, sw), (left[0], at(0, 0), at(2, 0)), (left[1], at(0, 1), at(2, 1))),
        )
        for s in range(4):
            for a in range(3):
                line, before, after = lines[s][a]
                for hf in range(2):
                    lanes = slice(hf * LANES, hf * LANES + LANES)
                    strip[n, s, hf, a, PAD : PAD + side, :] = line[:, lanes]
                    strip[n, s, hf, a, PAD - 1 : PAD, :] = before[:, lanes]
                    strip[n, s, hf, a, PAD + side : PAD + side + 1, :] = after[:, lanes]
        cots = jnp.concatenate(
            [
                ctop_ref[n, 0].astype(F32),
                columns(cright_ref[n], wide.at[2], (last,))[0],
                clow_ref[n, 0].astype(F32),
                columns(cleft_ref[n], wide.at[3], (0,))[0],
            ],
            axis=0,
        ).astype(BF16)
        ga = lax.dot_general(cots, w_ref[...], (((1,), (1,)), ((), ())), preferred_element_type=F32)
        row = lax.broadcasted_iota(jnp.int32, (side, LANES), 0)
        middle = jnp.logical_and(row > 0, row < end)
        for s in range(4):
            upright = s % 2 == 0
            rim_line = 0 if s in (0, 3) else 2
            for hf in range(2):
                lanes = slice(hf * LANES, hf * LANES + LANES)

                def tap(a, b):
                    k = 3 * a + b if upright else 3 * b + a
                    return k, tap_ref[k : k + 1, lanes]

                h = jnp.zeros((side, LANES), F32) + bias_ref[0:1, lanes]
                for a in range(3):
                    for b in range(3):
                        h = h + tap(a, b)[1] * strip[n, s, hf, a, PAD - 1 + b : PAD - 1 + b + side, :]
                act, slope = gelu_pair(h)
                g = (ga[s * side : s * side + side, lanes] * slope).astype(BF16)
                gr_ref[s, n, :, lanes] = g
                g = g.astype(F32)
                counted = g
                if not upright:
                    counted = jnp.where(middle, g, 0.0)
                    act = jnp.where(middle, act, 0.0)
                acts[n, s * side : s * side + side, lanes] = act.astype(BF16)
                for a in range(3):
                    for b in range(3):
                        k = tap(a, b)[0]
                        term = counted * strip[n, s, hf, a, PAD - 1 + b : PAD - 1 + b + side, :]
                        acc[hf, k] += jnp.sum(term.reshape(side // SUB, SUB, LANES), axis=0)
                acc[hf, 9] += jnp.sum(counted.reshape(side // SUB, SUB, LANES), axis=0)
                ext[n, PAD : PAD + side, :] = g
                first, mid, final = (tap(rim_line, b)[1] for b in range(3))
                back = (
                    first * ext[n, PAD + 1 : PAD + 1 + side, :]
                    + mid * g
                    + final * ext[n, PAD - 1 : PAD - 1 + side, :]
                )
                back = back + jnp.where(row == 0, (0.5 * masks[LOW[s]]) * first * g, 0.0)
                back = back + jnp.where(row == end, (0.5 * masks[HIGH[s]]) * final * g, 0.0)
                turned[n, s, :, lanes] = turn(table, s, back.astype(BF16))
        for d, to in enumerate((to0, to1, to2, to3)):
            to[n] = turned[n, table[SIDE_OF_DIR + d]]
        point_ref[...] += lax.dot_general(acts[n], cots, (((0,), (0,)), ((), ())), preferred_element_type=F32)

    for n in range(got0.shape[0]):
        sample(n)

    @pl.when(step == pl.num_programs(0) - 1)
    def _():
        rows = mine.shape[0]
        lines = []
        for hf in range(2):
            own = [jnp.sum(acc[hf, k], axis=0, keepdims=True) for k in range(10)]
            lines.append(jnp.concatenate(own + [jnp.zeros((6, LANES), F32)], axis=0))
        low = point_ref[0:rows]
        high = jnp.concatenate([point_ref[rows:], jnp.concatenate(lines, axis=1)], axis=0)
        first = table[CORE] == 0
        mine[...] = jnp.where(first, low, high)
        sent[...] = jnp.where(first, high, low)


def ring_call(table, state, cotangent, got, weight, taps, bias, point_inner, depth_inner):
    batch, side, cols, channels = state.shape
    wide, held, half = 8, RING_SAMPLES, (channels + 16) // 2
    two = lambda at: pl.BlockSpec((held, 2, cols, channels), lambda b: (b, at, 0, 0))
    one = lambda at: pl.BlockSpec((held, 1, cols, channels), lambda b: (b, at, 0, 0))
    column = lambda at: pl.BlockSpec((held, side, wide, channels), lambda b: (b, 0, at, 0))
    strips = pl.BlockSpec((4, held, side, channels), lambda b: (0, b, 0, 0))
    facing = pl.BlockSpec((held, side, channels), lambda b: (b, 0, 0))
    far = cols // wide - 1
    return pl.pallas_call(
        ring_body,
        grid=(batch // held,),
        in_specs=[
            pl.BlockSpec(memory_space=pltpu.SMEM),
            two(0),
            two(side // 2 - 1),
            column(0),
            column(far),
            one(0),
            one(side - 1),
            column(0),
            column(far),
            *[facing] * 4,
            pl.BlockSpec((channels, channels), lambda b: (0, 0)),
            pl.BlockSpec((9, channels), lambda b: (0, 0)),
            pl.BlockSpec((1, channels), lambda b: (0, 0)),
            pl.BlockSpec((channels, channels), lambda b: (0, 0)),
            pl.BlockSpec((2, 10, SUB, LANES), lambda b: (0, 0, 0, 0)),
        ],
        out_specs=[
            strips,
            *[facing] * 4,
            *[pl.BlockSpec((half, channels), lambda b: (0, 0))] * 2,
        ],
        out_shape=[
            jax.ShapeDtypeStruct((4, batch, side, channels), BF16),
            *[jax.ShapeDtypeStruct((batch, side, channels), BF16)] * 4,
            *[jax.ShapeDtypeStruct((half, channels), F32)] * 2,
        ],
        scratch_shapes=[
            pltpu.VMEM((held, 4, 2, 3, cols + 2 * PAD, LANES), F32),
            pltpu.VMEM((held, cols + 2 * PAD, LANES), F32),
            pltpu.VMEM((held, 4 * side, channels), BF16),
            pltpu.VMEM((2, 10, SUB, LANES), F32),
            pltpu.VMEM((held, 4, side, channels), BF16),
            pltpu.VMEM((4, 2, side * SUB, LANES), F32),
            pltpu.VMEM((channels, channels), F32),
        ],
        compiler_params=pltpu.CompilerParams(vmem_limit_bytes=57 << 20),
        cost_estimate=pl.CostEstimate(
            flops=3_000_000_000, bytes_accessed=12 << 20, transcendentals=state.size // 16
        ),
        name="ring",
    )(table, state, state, state, state, cotangent, cotangent, cotangent, cotangent, *got, weight, taps, bias,
      point_inner, depth_inner)


def spread_body(rows, first, table, gh_ref, above_ref, below_ref, gr_ref, got0, got1, got2, got3, tap_ref, out_ref, token_ref, gf, near, far, ring, back):
    got = (got0, got1, got2, got3)
    side = gr_ref.shape[2]
    cols = gh_ref.shape[2]
    count = gh_ref.shape[1]
    chunks = side // count
    step = (pl.program_id(0) + first) % chunks
    token_ref[...] = jnp.zeros_like(token_ref)
    start = step * count

    @pl.when(jnp.logical_or(pl.program_id(0) == 0, step == 0))
    def _():
        for k, s in enumerate((1, 3)):
            back[k] = from_dir(table, got, s)
        for hf in range(2):
            lanes = slice(hf * LANES, hf * LANES + LANES)
            gf[hf, :, 0:PAD, :] = jnp.zeros((count + 2, PAD, LANES), F32)
            gf[hf, :, PAD + cols : 2 * PAD + cols, :] = jnp.zeros((count + 2, PAD, LANES), F32)
            for k, s in enumerate((1, 3)):
                ring[k, hf, 0:PAD, :] = jnp.zeros((PAD, LANES), F32)
                ring[k, hf, PAD + side :, :] = jnp.zeros((PAD, LANES), F32)
                ring[k, hf, PAD : PAD + side, :] = gr_ref[s, 0, :, lanes].astype(F32)
        near[...] = jnp.zeros_like(near)
        far[...] = jnp.zeros_like(far)

    def put(i, v):
        v = v.astype(F32)
        gf[0, i, PAD : PAD + cols, :] = v[:, :LANES]
        gf[1, i, PAD : PAD + cols, :] = v[:, LANES:]

    put(0, jnp.where(step > 0, above_ref[0, 0], jnp.zeros_like(above_ref[0, 0])))
    put(count + 1, jnp.where(step < chunks - 1, below_ref[0, 0], jnp.zeros_like(below_ref[0, 0])))
    for i in range(count):
        put(i + 1, gh_ref[0, i])
    cut = [back[k, pl.ds(pl.multiple_of(start, count), count), :].astype(F32) for k in range(2)]
    for hf in range(2):
        lanes = slice(hf * LANES, hf * LANES + LANES)
        for k, j in ((0, PAD + cols - 1), (1, PAD)):
            own = ring[k, hf, pl.ds(pl.multiple_of(PAD + start, SUB), count), :]
            gf[hf, 1 : count + 1, j : j + 1, :] = own.reshape(count, 1, LANES)
            gf[hf, 0, j : j + 1, :] = ring[k, hf, pl.ds(PAD + start - 1, 1), :]
            gf[hf, count + 1, j : j + 1, :] = ring[k, hf, pl.ds(PAD + start + count, 1), :]
        near[hf, :, 0:1, :] = cut[1][:, lanes].reshape(count, 1, LANES)
        far[hf, :, SUB - 1 : SUB, :] = cut[0][:, lanes].reshape(count, 1, LANES)

    def line(i, s):
        v = gr_ref[s, 0].astype(F32)
        for hf in range(2):
            gf[hf, i, PAD : PAD + cols, :] = v[:, hf * LANES : hf * LANES + LANES]

    @pl.when(step == 0)
    def _():
        line(1, 0)

    @pl.when(step == chunks - 1)
    def _():
        line(count, 2)

    for hf in range(2):
        lanes = slice(hf * LANES, hf * LANES + LANES)
        taps = [tap_at(tap_ref, hf, k) for k in range(9)]
        for jb in range(cols // 16):

            def body(it, carry):
                i = it * rows
                win = {}
                for q in range(rows):
                    pair = []
                    for half in range(2):
                        j = PAD + jb * 16 + half * SUB
                        total = None
                        for r in range(3):
                            for c in range(3):
                                at = (q + 2 - r, 2 - c, half)
                                if at not in win:
                                    win[at] = gf[hf, i + at[0], j - 1 + at[1] : j - 1 + at[1] + SUB, :]
                                term = taps[3 * r + c] * win[at]
                                total = term if total is None else total + term
                        if jb == 0 and half == 0:
                            total = total + near[hf, i + q]
                        if jb == cols // 16 - 1 and half == 1:
                            total = total + far[hf, i + q]
                        pair.append(total)
                    out_ref[0, i + q, jb * 16 : jb * 16 + 16, lanes] = jnp.concatenate(pair, axis=0).astype(BF16)
                return carry

            for it in range(count // rows):
                body(it, 0)

    def add(i, s):
        out_ref[0, i] = (out_ref[0, i].astype(F32) + from_dir(table, got, s).astype(F32)).astype(BF16)

    @pl.when(step == 0)
    def _():
        add(0, 0)

    @pl.when(step == chunks - 1)
    def _():
        add(count - 1, 2)


CHUNK = 16


def spread_call(first, steps, table, grad, ring, got, taps, into):
    batch, side, cols, channels = grad.shape
    chunks = side // CHUNK
    high = side - 1
    at = lambda i: ((i + first) // chunks, (i + first) % chunks)
    strips = pl.BlockSpec((4, 1, side, channels), lambda i: (0, at(i)[0], 0, 0))
    facing = pl.BlockSpec((1, side, channels), lambda i: (at(i)[0], 0, 0))
    rows = pl.BlockSpec((1, CHUNK, cols, channels), lambda i: (*at(i), 0, 0))
    in_specs = [
        pl.BlockSpec(memory_space=pltpu.SMEM),
        rows,
        pl.BlockSpec((1, 1, cols, channels), lambda i: (at(i)[0], jnp.maximum(at(i)[1] * CHUNK - 1, 0), 0, 0)),
        pl.BlockSpec((1, 1, cols, channels), lambda i: (at(i)[0], jnp.minimum(at(i)[1] * CHUNK + CHUNK, high), 0, 0)),
        strips,
        *[facing] * 4,
        pl.BlockSpec((9, channels), lambda i: (0, 0)),
    ]
    operands = [table, grad, grad, grad, ring, *got, taps]
    aliases = {}
    if into is not None:
        aliases = {len(operands): 0}
        in_specs.append(pl.BlockSpec(memory_space=pl.ANY))
        operands.append(into)

    def body(*refs):
        spread_body(4, first, *refs[:10], *refs[len(operands) :])

    return pl.pallas_call(
        body,
        grid=(steps,),
        in_specs=in_specs,
        out_specs=[rows, pl.BlockSpec((SUB, LANES), lambda i: (0, 0))],
        out_shape=[jax.ShapeDtypeStruct(grad.shape, BF16), jax.ShapeDtypeStruct((SUB, LANES), F32)],
        scratch_shapes=[
            pltpu.VMEM((2, CHUNK + 2, cols + 2 * PAD, LANES), F32),
            pltpu.VMEM((2, CHUNK, SUB, LANES), F32),
            pltpu.VMEM((2, CHUNK, SUB, LANES), F32),
            pltpu.VMEM((2, 2, side + 2 * PAD, LANES), F32),
            pltpu.VMEM((2, side, channels), BF16),
        ],
        input_output_aliases=aliases,
        compiler_params=pltpu.CompilerParams(vmem_limit_bytes=57 << 20),
        cost_estimate=pl.CostEstimate(
            flops=750_000_000 * steps, bytes_accessed=grad.size * 4 * steps // (batch * chunks), transcendentals=0
        ),
        name="spread",
    )(*operands)


def exchange(facing):
    faces, tiles = lax.axis_size("face"), lax.axis_size("tile")
    got = []
    for d, rows in enumerate(facing):
        pairs = []
        for i in range(faces * tiles):
            at = [i // tiles, i % tiles]
            k = d // 2
            step = 1 - 2 * (at[k] % 2)
            at[k] = (at[k] + (step if d % 2 == 0 else -step)) % (faces, tiles)[k]
            pairs.append((i, at[0] * tiles + at[1]))
        got.append(lax.ppermute(rows, ("face", "tile"), pairs))
    return got


def swap(value, mask):
    devices = lax.axis_size("face") * lax.axis_size("tile")
    return lax.ppermute(value, ("face", "tile"), [(i, i ^ mask) for i in range(devices)])


def after(value, *others):
    return lax.optimization_barrier((value, *others))[0]


def shards(
    state, cotangent, depth_weight, depth_bias, point_weight, tile_links, link_sides, link_flips, corner_masks
):
    batch, side, cols, channels = state.shape
    face_count = lax.axis_size("face")
    tile_count = lax.axis_size("tile")
    face_pos = lax.axis_index("face")
    tile_pos = lax.axis_index("tile")
    where = jnp.stack([face_pos, tile_pos])
    bias = depth_bias.reshape(1, channels)
    *edges, table = edges_call(where, tile_links, link_flips, corner_masks, state)
    got = exchange(edges)
    layer = (point_weight, depth_weight, bias)
    grad, point_sum, depth_sum = inner_call(state, cotangent, *layer)
    ring, *facing, mine, sent = ring_call(table, state, cotangent, got, *layer, point_sum, depth_sum)
    incoming = exchange(facing)

    first, field_grad = 0, None
    for stage, (mask_bits, steps) in enumerate(((1, 0), (2, 2), (6, 3), (8, 2), (24, 3), (32, 2), (96, 4))):
        last = mask_bits == 96
        got = [swap(sent if stage == 0 else mine, bits) for bits in ((96, 1, 97) if last else (mask_bits,))]
        if steps:
            held = after(depth_weight, mine)
            field_grad, token = spread_call(first, steps, table, grad, ring, incoming, held, field_grad)
            got = lax.optimization_barrier((*got, token))[:-1]
            first += steps
        mine = mine + got[0]
    other = got[1] + got[2]
    scale = float(batch * side * cols * face_count * tile_count) ** -0.5
    core = tile_pos % 2
    rows = channels - mine.shape[0]
    low = jnp.where(core == 0, mine, other) * scale
    high = jnp.where(core == 0, other, mine) * scale
    point_grad = jnp.concatenate([low, high[:rows]], axis=0)
    return field_grad, high[rows : rows + 9], high[rows + 9], point_grad


def solution(mesh):
    tiles = P(None, "face", "tile", None)
    table = P(("face", "tile"), None)
    return jax.shard_map(
        shards,
        mesh=mesh,
        in_specs=(tiles, tiles, P(), P(), P(), table, table, table, table),
        out_specs=(tiles, P(), P(), P()),
        check_vma=False,
    )
```
